32 devices in a mesh: dp: 16 (over z, y, core), expert: 2 (over x).
Axes of the slice: x: 2, y: 2, z: 4, core: 2. Of those that a mesh axis runs over, the one named last changes fastest.
Arguments:
- tokens: bfloat16 [4096, 2048], P(('dp', 'expert')), may hold values from -6 to 6
- cotangent: bfloat16 [4096, 2048], P(('dp', 'expert')), may hold values from -6 to 6
- expert_ids: int32 [4096, 8], P(('dp', 'expert')), may hold values from 0 to 127, as said below
- route_weights: float32 [4096, 8], P(('dp', 'expert')), may hold values from 0.1 to 1
- join_groups: int32 [16], replicated, may hold values from 0 to 1
- w_gate: bfloat16 [2048, 1024], P('dp', 'expert'), may hold values from -0.125 to 0.125
- w_up: bfloat16 [2048, 1024], P('dp', 'expert'), may hold values from -0.125 to 0.125
- w_down: bfloat16 [2048, 1024], P('dp', 'expert'), may hold values from -0.1875 to 0.1875
Outputs:
- mixed: bfloat16 [4096, 2048], P(('dp', 'expert'))
- grad_gate: bfloat16 [2048, 1024], P('dp', 'expert')
- grad_up: bfloat16 [2048, 1024], P('dp', 'expert')
- grad_down: bfloat16 [2048, 1024], P('dp', 'expert')
The draws below stay inside these ranges and needn't reach their ends.
Inputs may be any that keep to these rules, and one draw needn't show every extreme that they name: `expert_ids`: each row names 8 different experts; the rows of one device name expert 0 at most 16 times, and the rows of some device exactly 16 times.
All inputs are finite; a program needn't handle non-finite values.
Results may differ from the reference program's by a relative error of at most 0.014.
Values may be sent and summed in bfloat16 or wider, within the bound.
A program may use at most 64 MiB of HBM per device.

```python
import jax
import jax.numpy as jnp
from jax import lax

D = 2048
FF = 1024
NEXP_ALL = 128
TOP = 8
TOK_DEV = 128
CAP = 16
ROWS = 32
TOKENS = 4096
N_DP = 16
N_EXPERT = 2


def draw_expert_ids(key, part):
    key_count, key_pick, key_order, key_rest, key_turn = jax.random.split(key, 5)
    blocks = TOKENS // TOK_DEV
    counts = jax.random.randint(key_count, (blocks,), CAP // 4, CAP + 1)
    special = jax.random.randint(key_pick, (), 0, blocks)
    counts = jnp.where(jnp.arange(blocks) == special, CAP, counts)
    orders = jax.vmap(lambda sub_key: jax.random.permutation(sub_key, TOK_DEV))(jax.random.split(key_order, blocks))
    routed = (orders < counts[:, None]).reshape(TOKENS)
    scores = jax.random.randint(key_rest, (TOKENS, NEXP_ALL - 1), 0, 2 ** 30)
    others = 1 + jnp.argsort(scores, axis=-1)[:, :TOP]
    first = jnp.where(routed, 0, others[:, TOP - 1])
    chosen = jnp.concatenate([first[:, None], others[:, :TOP - 1]], axis=1)
    turns = jax.random.randint(key_turn, (TOKENS, 1), 0, TOP)
    index = (jnp.arange(TOP)[None, :] + turns) % TOP
    return jnp.take_along_axis(chosen, index, axis=1).astype(jnp.int32)


def set_ends(drawn, own_key, least, top_value):
    place = [jax.random.randint(jax.random.fold_in(own_key, axis), (), 0, length) for axis, length in enumerate(drawn.shape)]
    longest = drawn.shape.index(max(drawn.shape))
    next_to = place[:longest] + [(place[longest] + 1) % drawn.shape[longest]] + place[longest + 1:]
    return drawn.at[tuple(place)].set(least).at[tuple(next_to)].set(top_value)


def with_spikes(entries, rng, source, target, parts, factor):
    def block_of(dim):
        return (jnp.arange(entries.shape[dim]) // (entries.shape[dim] // parts)).reshape((-1,) + (1,) * (entries.ndim - 1 - dim))

    near = jax.random.permutation(rng, parts)[block_of(target)]
    second = (block_of(target) + parts // 2) % parts
    return jnp.where((block_of(source) == near) | (block_of(source) == second), factor * entries, entries)


def block_levels(own_key, shape, cuts, least, high):
    loudness, own = 1.0, jax.random.fold_in(own_key, 6)
    for dim, blocks in cuts:
        draws = jnp.exp(jax.random.uniform(jax.random.fold_in(own, dim), (blocks,), jnp.float32, least / len(cuts), high / len(cuts)))
        loudness = loudness * jnp.repeat(draws, shape[dim] // blocks).reshape([-1 if axis == dim else 1 for axis in range(len(shape))])
    return loudness


def scatter_about(key, extent, spread, bound, cuts=(), held_as=jnp.bfloat16):
    drawn = spread * jax.random.normal(key, extent, jnp.float32)
    if cuts:
        drawn = drawn * block_levels(key, extent, cuts, -0.22, 0.18)
    return jnp.clip(drawn, -bound, bound).astype(held_as)


def bell_draw_with(own_key, shape, spread, most, pieces, heavy, kind=jnp.bfloat16):
    values = spread * jax.random.normal(own_key, shape, jnp.float32)
    if pieces:
        values = values * block_levels(own_key, shape, pieces, -0.22, 0.18)
    return jnp.clip(with_spikes(values, jax.random.fold_in(own_key, 3), *heavy), -most, most).astype(kind)


def setup_inputs(seed: int = 0) -> dict:
    key_of = jax.random.split(jax.random.key(seed), 9)
    return {
        "tokens": bell_draw_with(key_of[0], (TOKENS, D), 1.0, 6.0, ((0, 32),), (0, 1, 32, 2.75)),
        "cotangent": bell_draw_with(key_of[1], (TOKENS, D), 1.0, 6.0, ((0, 32),), (0, 1, 32, 2.75)),
        "expert_ids": draw_expert_ids(jax.random.fold_in(key_of[8], 71), 0),
        "route_weights": jnp.clip(0.1 + 0.9 * jax.random.uniform(key_of[3], (TOKENS, TOP), jnp.float32) ** block_levels(key_of[3], (TOKENS, TOP), ((0, 32),), -0.2, 0.2), 0.1, 1.0),
        "join_groups": set_ends(jax.random.randint(key_of[4], (N_DP,), 0, 2), jax.random.fold_in(key_of[4], 1), 0, 1).astype(jnp.int32),
        "w_gate": scatter_about(key_of[5], (D, FF), D ** -0.5, 0.125, ((0, 16), (1, 2))),
        "w_up": scatter_about(key_of[6], (D, FF), D ** -0.5, 0.125, ((0, 16), (1, 2))),
        "w_down": scatter_about(key_of[7], (D, FF), FF ** -0.5, 0.1875, ((0, 16), (1, 2))),
    }


def reference(tokens, cotangent, expert_ids, route_weights, join_groups, w_gate, w_up, w_down):
    expert_count = N_EXPERT
    slice_width = FF // expert_count
    highest = lax.Precision.HIGHEST
    slot_ids = jnp.arange(CAP, dtype=jnp.int32)
    tok_groups = tokens.reshape(N_DP, expert_count, TOK_DEV, D)
    cot_groups = cotangent.reshape(N_DP, expert_count, TOK_DEV, D)
    id_groups = expert_ids.reshape(N_DP, expert_count, TOK_DEV, TOP)
    wt_groups = route_weights.reshape(N_DP, expert_count, TOK_DEV, TOP)

    def group_step(running, member):
        tok_block, cot_block, id_block, wt_block, joined = member
        chosen_mask = id_block == 0
        routed = jnp.any(chosen_mask, -1)
        weight = jnp.sum(jnp.where(chosen_mask, wt_block, 0.0), -1)
        places = jnp.cumsum(routed.astype(jnp.int32), -1) - 1
        chooser = ((places[:, None, :] == slot_ids[None, :, None]) & routed[:, None, :]).astype(jnp.float32)
        picked = jnp.einsum('ect,etd->ecd', chooser, tok_block.astype(jnp.float32), precision=highest)
        picked = picked.astype(jnp.bfloat16).reshape(ROWS, D)
        gate_acts = jnp.dot(picked, w_gate, preferred_element_type=jnp.float32)
        up_acts = jnp.dot(picked, w_up, preferred_element_type=jnp.float32)
        hidden = (jax.nn.silu(gate_acts) * up_acts).astype(jnp.bfloat16)
        partials = jnp.einsum('rjf,djf->jrd', hidden.reshape(ROWS, expert_count, slice_width).astype(jnp.float32),
                              w_down.reshape(D, expert_count, slice_width).astype(jnp.float32), precision=highest)
        out_rows = jnp.sum(partials.astype(jnp.bfloat16).astype(jnp.float32), 0).reshape(expert_count, CAP, D)
        mixed = jnp.einsum('ect,ecd->etd', chooser, out_rows, precision=highest) * weight[..., None]
        mixed = mixed.astype(jnp.bfloat16)
        scaled = cot_block.astype(jnp.float32) * weight[..., None]
        dpicked = jnp.einsum('ect,etd->ecd', chooser, scaled, precision=highest).astype(jnp.bfloat16).reshape(ROWS, D)
        hidden_grad = jnp.dot(dpicked, w_down, preferred_element_type=jnp.float32)
        sigma_gate = jax.nn.sigmoid(gate_acts)
        dgate = (hidden_grad * up_acts * sigma_gate * (1.0 + gate_acts * (1.0 - sigma_gate))).astype(jnp.bfloat16)
        dup = (hidden_grad * gate_acts * sigma_gate).astype(jnp.bfloat16)
        dims = (((0,), (0,)), ((), ()))
        term_gate = lax.dot_general(picked, dgate, dims, preferred_element_type=jnp.float32)
        term_up = lax.dot_general(picked, dup, dims, preferred_element_type=jnp.float32)
        term_down = lax.dot_general(dpicked, hidden, dims, preferred_element_type=jnp.float32)
        active = 1.0 - joined.astype(jnp.float32)
        running = running + active * jnp.stack([term_gate, term_up, term_down])
        return running, mixed

    start = jnp.zeros((3, D, FF), jnp.float32)
    sums, mixed_all = lax.scan(group_step, start, (tok_groups, cot_groups, id_groups, wt_groups, join_groups))
    return (mixed_all.reshape(TOKENS, D), sums[0].astype(jnp.bfloat16),
            sums[1].astype(jnp.bfloat16), sums[2].astype(jnp.bfloat16))
```

```python
import functools

import jax
import jax.numpy as jnp
from jax import lax
from jax.experimental import pallas as pl
from jax.experimental.pallas import tpu as pltpu
from jax.sharding import PartitionSpec as P

F32, BF16 = jnp.float32, jnp.bfloat16
MESH = pl.DeviceIdType.MESH
CHUNKS = 2


def dot(a, b, dims):
    return lax.dot_general(a, b, (dims, ((), ())), preferred_element_type=F32)


def kernel(
    pairs, members, cap,
    join, tok, cot, ids, wts, wg, wu, wd,
    mixed, grad_gate, grad_up, grad_down,
    tokv, cotv, wfull, blk, recv1, part, send2, recv_y, mid, recv_z, acc, all3, send4, recv4, gacc, sendg, recvg,
    local, sw, rw, s1, r1, s2y, r2y, s2z, r2z, s3y, r3y, s3z, r3z, s4, r4, sg, rg,
):
    p, j = lax.axis_index("dp"), lax.axis_index("expert")
    pair, core = lax.div(p, 2), lax.rem(p, 2)
    total = pairs * members
    flat = pair * members + j
    partner = (2 * pair + 1 - core, j)
    line, side = lax.div(pair, 2), lax.rem(pair, 2)
    lines = pairs // 2
    across = (2 * (2 * line + 1 - side) + core, j)
    last = lines - 1
    tok_count = tok.shape[0]
    depth, width = wg.shape
    chip_depth = 2 * depth
    rows = members * cap

    def flat_peer(d):
        other = lax.rem(flat + d, total)
        return other, lax.div(other, members), lax.rem(other, members)

    def copy(src, dst, send, recv, device):
        return pltpu.make_async_remote_copy(
            src_ref=src, dst_ref=dst, send_sem=send, recv_sem=recv, device_id=device, device_id_type=MESH
        )

    def on_line(other):
        return (2 * (2 * other + side) + core, j)

    weights = (wg, wu, wd)
    loads = [(cot, cotv), (tok, tokv)] + [(w, wfull.at[n, core]) for n, w in enumerate(weights)]
    loads = [pltpu.make_async_copy(src, dst, local.at[n]) for n, (src, dst) in enumerate(loads)]
    for load in loads:
        load.start()

    barrier = pltpu.get_barrier_semaphore()

    def greet(d, carry):
        _, pair2, j2 = flat_peer(d)
        pl.semaphore_signal(barrier, inc=1, device_id=(2 * pair2 + core, j2), device_id_type=MESH)
        return carry

    lax.fori_loop(1, total, greet, 0)
    pl.semaphore_signal(barrier, inc=1, device_id=partner, device_id_type=MESH)

    chosen = ids[...] == 0
    routed = jnp.max(jnp.where(chosen, 1.0, 0.0), axis=0, keepdims=True)
    weight = jnp.sum(jnp.where(chosen, wts[...], 0.0), axis=0, keepdims=True)
    upper = lax.broadcasted_iota(jnp.int32, (tok_count, tok_count), 0) <= lax.broadcasted_iota(
        jnp.int32, (tok_count, tok_count), 1
    )
    wide = jnp.broadcast_to(routed, (cap, tok_count))
    places = dot(wide.astype(BF16), jnp.where(upper, 1.0, 0.0).astype(BF16), ((1,), (0,))) - 1.0
    slot = lax.broadcasted_iota(jnp.int32, (cap, tok_count), 0).astype(F32)
    pick = jnp.where((places == slot) & (wide > 0.5), 1.0, 0.0)
    slot_weight = jnp.sum(pick * weight, axis=1, keepdims=True)
    spread = pick.T.astype(BF16)
    pick = pick.astype(BF16)
    active = 1.0 - join[p].astype(F32)
    loads[0].wait()
    dpicked_rows = (dot(pick, cotv[...], ((1,), (0,))) * (slot_weight * active)).astype(BF16)
    loads[1].wait()
    picked_rows = dot(pick, tokv[...], ((1,), (0,))).astype(BF16)
    for q in range(pairs):
        cols = slice(q * chip_depth, (q + 1) * chip_depth)
        blk[q, 0] = picked_rows[:, cols]
        blk[q, 1] = dpicked_rows[:, cols]

    pl.semaphore_wait(barrier, total)

    def start1(d, carry):
        _, pair2, j2 = flat_peer(d)
        copy(blk.at[pair2], recv1.at[flat], s1.at[d], r1.at[d], (2 * pair2 + core, j2)).start()
        return carry

    lax.fori_loop(1, total, start1, 0)
    for n, w in enumerate(weights):
        copy(w, wfull.at[n, core], sw.at[n], rw.at[n], partner).start()
    recv1[flat] = blk[pair]
    for n, w in enumerate(weights):
        loads[2 + n].wait()
        copy(w, wfull.at[n, 1 - core], sw.at[n], rw.at[n], partner).wait_recv()

    def wait1(d, carry):
        copy(blk.at[0], recv1.at[lax.rem(flat - d + total, total)], s1.at[d], r1.at[d], partner).wait_recv()
        return carry

    lax.fori_loop(1, total, wait1, 0)

    picked = recv1[:, 0].reshape(total * cap, chip_depth)
    dpicked = recv1[:, 1].reshape(total * cap, chip_depth)
    full = [wfull[n].reshape(chip_depth, width) for n in range(3)]
    for n, left in enumerate((picked, picked, dpicked)):
        term = dot(left, full[n], ((1,), (0,))).reshape(pairs, CHUNKS, rows // CHUNKS, width)
        for h in range(CHUNKS):
            part[h, :, n] = term[:, h]
            send2[h, :, n] = term[:, h].astype(BF16)

    def start2(h, d, carry):
        other, at = lax.rem(line + 1 + d, lines), h * lines + d
        copy(send2.at[h, 2 * other + 1 - side], recv_y.at[h, other], s2y.at[at], r2y.at[at], across).start()
        return carry

    def pass2(h, d, carry):
        other, at = lax.rem(line + 1 + d, lines), h * lines + d
        copy(send2.at[h, 0], recv_y.at[h, other], s2y.at[at], r2y.at[at], across).wait_recv()
        mid[h, other] = (part[h, 2 * other + side] + recv_y[h, other].astype(F32)).astype(BF16)
        copy(mid.at[h, other], recv_z.at[h, line], s2z.at[at], r2z.at[at], on_line(other)).start()
        return carry

    def add2(h, d, carry):
        source, at = lax.rem(line + last - d, lines), h * lines + d
        copy(mid.at[h, 0], recv_z.at[h, source], s2z.at[at], r2z.at[at], across).wait_recv()
        acc[h] += recv_z[h, source].astype(F32)
        return carry

    def start3(h, d, carry):
        other, at = lax.rem(line + 1 + d, lines), h * lines + d
        copy(all3.at[h, pair], all3.at[h, pair], s3z.at[at], r3z.at[at], on_line(other)).start()
        return carry

    def pass3(h, d, carry):
        at = h * lines + d
        held = all3.at[h, 2 * lax.rem(line + last - d, lines) + side]
        copy(all3.at[h, pair], held, s3z.at[at], r3z.at[at], across).wait_recv()
        copy(held, held, s3y.at[at], r3y.at[at], across).start()
        return carry

    def wait3(h, d, carry):
        at = h * lines + d
        place = all3.at[h, 2 * lax.rem(line + last - d, lines) + 1 - side]
        copy(all3.at[h, pair], place, s3y.at[at], r3y.at[at], across).wait_recv()
        return carry

    for h in range(CHUNKS):
        lax.fori_loop(0, lines, functools.partial(start2, h), 0)
    for h in range(CHUNKS):
        lax.fori_loop(0, last, functools.partial(pass2, h), 0)
        at = h * lines + last
        copy(send2.at[h, 0], recv_y.at[h, line], s2y.at[at], r2y.at[at], across).wait_recv()
        acc[h] = part[h, pair] + recv_y[h, line].astype(F32)
    for h in range(CHUNKS):
        lax.fori_loop(0, last, functools.partial(add2, h), 0)
        gate, up, dhidden = acc[h, 0], acc[h, 1], acc[h, 2]
        sig = 1.0 / (1.0 + jnp.exp(-gate))
        all3[h, pair, 0] = (gate * sig * up).astype(BF16)
        all3[h, pair, 1] = (dhidden * up * sig * (1.0 + gate * (1.0 - sig))).astype(BF16)
        all3[h, pair, 2] = (dhidden * gate * sig).astype(BF16)
        lax.fori_loop(0, last, functools.partial(start3, h), 0)
        at = h * lines + last
        copy(all3.at[h, pair], all3.at[h, pair], s3y.at[at], r3y.at[at], across).start()
    for h in range(CHUNKS):
        lax.fori_loop(0, last, functools.partial(pass3, h), 0)
    for h in range(CHUNKS):
        at = h * lines + last
        place = all3.at[h, 2 * line + 1 - side]
        copy(all3.at[h, pair], place, s3y.at[at], r3y.at[at], across).wait_recv()
        lax.fori_loop(0, last, functools.partial(wait3, h), 0)

    hidden, dgate, dup = (
        jnp.stack([all3[h, :, n] for h in range(CHUNKS)], axis=1).reshape(pairs * rows, width) for n in range(3)
    )
    send4[...] = dot(hidden, full[2], ((1,), (1,))).astype(BF16).reshape(total, cap, chip_depth)

    def start4(d, carry):
        other, pair2, j2 = flat_peer(d)
        copy(send4.at[other], recv4.at[j, pair], s4.at[d], r4.at[d], (2 * pair2 + core, j2)).start()
        return carry

    lax.fori_loop(1, total, start4, 0)
    recv4[j, pair] = send4[flat]

    for n, (left, right) in enumerate(((picked, dgate), (picked, dup), (dpicked, hidden))):
        term = dot(left, right, ((0,), (0,))).reshape(2, depth, width)
        gacc[n] = term
        sendg[n] = term.astype(BF16)
        copy(sendg.at[n, 1 - core], recvg.at[n], sg.at[n], rg.at[n], partner).start()

    def wait4(d, carry):
        source = lax.rem(flat - d + total, total)
        place = recv4.at[lax.rem(source, members), lax.div(source, members)]
        copy(send4.at[0], place, s4.at[d], r4.at[d], partner).wait_recv()
        return carry

    lax.fori_loop(1, total, wait4, 0)
    for q in range(pairs):
        out_rows = recv4[0, q].astype(F32)
        for m in range(1, members):
            out_rows += recv4[m, q].astype(F32)
        placed = dot(spread, (out_rows * slot_weight).astype(BF16), ((1,), (0,)))
        mixed[:, q * chip_depth : (q + 1) * chip_depth] = placed.astype(BF16)

    for n, out in enumerate((grad_gate, grad_up, grad_down)):
        copy(sendg.at[n, 0], recvg.at[n], sg.at[n], rg.at[n], partner).wait_recv()
        out[...] = (gacc[n, core] + recvg[n].astype(F32)).astype(BF16)

    for n, w in enumerate(weights):
        copy(w, wfull.at[n, core], sw.at[n], rw.at[n], partner).wait_send()
        copy(sendg.at[n, 0], recvg.at[n], sg.at[n], rg.at[n], partner).wait_send()

    def drain_flat(d, carry):
        copy(blk.at[0], recv1.at[0], s1.at[d], r1.at[d], partner).wait_send()
        copy(send4.at[0], recv4.at[0, 0], s4.at[d], r4.at[d], partner).wait_send()
        return carry

    def drain_y(d, carry):
        copy(send2.at[0, 0], recv_y.at[0, 0], s2y.at[d], r2y.at[d], across).wait_send()
        copy(all3.at[0, 0], all3.at[0, 0], s3y.at[d], r3y.at[d], across).wait_send()
        return carry

    def drain_z(h, d, carry):
        at = h * lines + d
        copy(mid.at[0, 0], recv_z.at[0, 0], s2z.at[at], r2z.at[at], across).wait_send()
        copy(all3.at[0, 0], all3.at[0, 0], s3z.at[at], r3z.at[at], across).wait_send()
        return carry

    lax.fori_loop(1, total, drain_flat, 0)
    lax.fori_loop(0, CHUNKS * lines, drain_y, 0)
    for h in range(CHUNKS):
        lax.fori_loop(0, last, functools.partial(drain_z, h), 0)


def write_out(*refs):
    sems = refs[-1]
    copies = [pltpu.make_async_copy(refs[n], refs[4 + n], sems.at[n]) for n in range(4)]
    for c in copies:
        c.start()
    for c in copies:
        c.wait()


def per_device(pairs, members, tokens, cotangent, expert_ids, route_weights, join_groups, w_gate, w_up, w_down):
    tok_count, model = tokens.shape
    depth, width = w_gate.shape
    cap = tok_count // 8
    total = pairs * members
    rows = members * cap
    vmem = pl.BlockSpec(memory_space=pltpu.VMEM)
    hbm = pl.BlockSpec(memory_space=pl.ANY)
    lines = pairs // 2
    dma = pltpu.SemaphoreType.DMA
    grad = pltpu.VMEM((depth, width), BF16)
    held = pl.pallas_call(
        functools.partial(kernel, pairs, members, cap),
        out_shape=(pltpu.VMEM((tok_count, model), BF16), grad, grad, grad),
        in_specs=[pl.BlockSpec(memory_space=pltpu.SMEM), hbm, hbm, vmem, vmem, hbm, hbm, hbm],
        out_specs=(vmem,) * 4,
        scratch_shapes=[
            pltpu.VMEM((tok_count, model), BF16),
            pltpu.VMEM((tok_count, model), BF16),
            pltpu.VMEM((3, 2, depth, width), BF16),
            pltpu.VMEM((pairs, 2, cap, 2 * depth), BF16),
            pltpu.VMEM((total, 2, cap, 2 * depth), BF16),
            pltpu.VMEM((CHUNKS, pairs, 3, rows // CHUNKS, width), F32),
            pltpu.VMEM((CHUNKS, pairs, 3, rows // CHUNKS, width), BF16),
            pltpu.VMEM((CHUNKS, lines, 3, rows // CHUNKS, width), BF16),
            pltpu.VMEM((CHUNKS, lines, 3, rows // CHUNKS, width), BF16),
            pltpu.VMEM((CHUNKS, lines, 3, rows // CHUNKS, width), BF16),
            pltpu.VMEM((CHUNKS, 3, rows // CHUNKS, width), F32),
            pltpu.VMEM((CHUNKS, pairs, 3, rows // CHUNKS, width), BF16),
            pltpu.VMEM((total, cap, 2 * depth), BF16),
            pltpu.VMEM((members, pairs, cap, 2 * depth), BF16),
            pltpu.VMEM((3, 2, depth, width), F32),
            pltpu.VMEM((3, 2, depth, width), BF16),
            pltpu.VMEM((3, depth, width), BF16),
            dma((5,)),
            dma((3,)), dma((3,)),
            dma((total,)), dma((total,)),
            dma((CHUNKS * lines,)), dma((CHUNKS * lines,)),
            dma((CHUNKS * lines,)), dma((CHUNKS * lines,)),
            dma((CHUNKS * lines,)), dma((CHUNKS * lines,)),
            dma((CHUNKS * lines,)), dma((CHUNKS * lines,)),
            dma((total,)), dma((total,)),
            dma((3,)), dma((3,)),
        ],
        compiler_params=pltpu.CompilerParams(
            collective_id=0, has_side_effects=True, vmem_limit_bytes=60 * 1024 * 1024
        ),
        name="expert_step",
    )(join_groups, tokens, cotangent, expert_ids.T, route_weights.T, w_gate, w_up, w_down)
    return pl.pallas_call(
        write_out,
        out_shape=tuple(jax.ShapeDtypeStruct(h.shape, h.dtype) for h in held),
        in_specs=[vmem] * 4,
        out_specs=(hbm,) * 4,
        scratch_shapes=[dma((4,))],
        name="write_out",
    )(*(pltpu.with_memory_space_constraint(h, pltpu.VMEM) for h in held))


def solution(mesh):
    in_specs = (
        P(("dp", "expert"), None),
        P(("dp", "expert"), None),
        P(("dp", "expert"), None),
        P(("dp", "expert"), None),
        P(),
        P("dp", "expert"),
        P("dp", "expert"),
        P("dp", "expert"),
    )
    out_specs = (P(("dp", "expert"), None), P("dp", "expert"), P("dp", "expert"), P("dp", "expert"))
    body = functools.partial(per_device, mesh.shape["dp"] // 2, mesh.shape["expert"])
    return jax.shard_map(body, mesh=mesh, in_specs=in_specs, out_specs=out_specs, check_vma=False)
```

```python
import functools

import jax
import jax.numpy as jnp
from jax import lax
from jax.experimental import pallas as pl
from jax.experimental.pallas import tpu as pltpu
from jax.sharding import PartitionSpec as P

F32, BF16 = jnp.float32, jnp.bfloat16
MESH = pl.DeviceIdType.MESH


def dot(a, b, dims):
    return lax.dot_general(a, b, (dims, ((), ())), preferred_element_type=F32)


def flip(a, d, count):
    out, bit = 0, 1
    while bit < count:
        mine = lax.rem(lax.div(a, bit), 2)
        turn = (d // bit) % 2 if isinstance(d, int) else lax.rem(lax.div(d, bit), 2)
        out += bit * (mine + turn - 2 * mine * turn)
        bit *= 2
    return out


def each(low, high, body):
    if high - low <= 16:
        for i in range(low, high):
            body(i)
    else:
        lax.fori_loop(low, high, lambda i, carry: (body(i), carry)[1], 0)


def kernel(
    lines, members, cap,
    join, tok, cot, ids, wts, wg, wu, wd,
    mixed, grad_gate, grad_up, grad_down,
    tokv, cotv, wfull, blk, recv1, rows_all, part, send2, recv2, all3, send4, recv4,
    local, swy, rwy, swc, rwc, swf, rwf, s1, r1, sx, rx, s2, r2, s3z, r3z, s3y, r3y, s3c, r3c, s4, r4,
):
    p, j = lax.axis_index("dp"), lax.axis_index("expert")
    line, side, core = lax.div(p, 4), lax.rem(lax.div(p, 2), 2), lax.rem(p, 2)
    quarter = 2 * side + core
    total = lines * members
    flat = line * members + j
    tok_count = tok.shape[0]
    depth, width = wg.shape
    line_depth = 4 * depth

    def device(z, y, c, member):
        return (4 * z + 2 * y + c, member)

    partner = device(line, side, 1 - core, j)
    across = device(line, 1 - side, core, j)

    def copy(src, dst, send, recv, target):
        return pltpu.make_async_remote_copy(
            src_ref=src, dst_ref=dst, send_sem=send, recv_sem=recv, device_id=target, device_id_type=MESH
        )

    def peer(t):
        if isinstance(t, int):
            dz, dj = t // members, t % members
        else:
            dz, dj = lax.div(t, members), lax.rem(t, members)
        return flip(line, dz, lines), flip(j, dj, members)

    def on_line(d):
        z = flip(line, d, lines)
        return z, device(z, side, core, j)

    near = [(0, 1), (1, 0), (1, 1)]

    def beside(n):
        y = 1 - side if near[n][0] else side
        c = 1 - core if near[n][1] else core
        return 2 * y + c, device(line, y, c, j)

    weights = (wg, wu, wd)
    loads = [(cot, cotv), (tok, tokv)] + [(w, wfull.at[n, quarter]) for n, w in enumerate(weights)]
    loads = [pltpu.make_async_copy(src, dst, local.at[n]) for n, (src, dst) in enumerate(loads)]
    for load in loads:
        load.start()

    barrier = pltpu.get_barrier_semaphore()

    def greet(t):
        z, member = peer(t)
        pl.semaphore_signal(barrier, inc=1, device_id=device(z, side, core, member), device_id_type=MESH)

    each(1, total, greet)
    for n in range(3):
        pl.semaphore_signal(barrier, inc=1, device_id=beside(n)[1], device_id_type=MESH)

    chosen = ids[...] == 0
    routed = jnp.max(jnp.where(chosen, 1.0, 0.0), axis=0, keepdims=True)
    weight = jnp.sum(jnp.where(chosen, wts[...], 0.0), axis=0, keepdims=True)
    upper = lax.broadcasted_iota(jnp.int32, (tok_count, tok_count), 0) <= lax.broadcasted_iota(
        jnp.int32, (tok_count, tok_count), 1
    )
    wide = jnp.broadcast_to(routed, (cap, tok_count))
    places = dot(wide.astype(BF16), jnp.where(upper, 1.0, 0.0).astype(BF16), ((1,), (0,))) - 1.0
    slot = lax.broadcasted_iota(jnp.int32, (cap, tok_count), 0).astype(F32)
    pick = jnp.where((places == slot) & (wide > 0.5), 1.0, 0.0)
    slot_weight = jnp.sum(pick * weight, axis=1, keepdims=True)
    spread = pick.T.astype(BF16)
    pick = pick.astype(BF16)
    active = 1.0 - join[p].astype(F32)
    loads[0].wait()
    dpicked_rows = (dot(pick, cotv[...], ((1,), (0,))) * (slot_weight * active)).astype(BF16)
    loads[1].wait()
    picked_rows = dot(pick, tokv[...], ((1,), (0,))).astype(BF16)
    for n, taken in enumerate((picked_rows, dpicked_rows)):
        for z in range(lines):
            for k in range(4):
                at = z * line_depth + k * depth
                blk[n, z, k] = taken[:, at : at + depth]
    for n in range(3):
        loads[2 + n].wait()

    pl.semaphore_wait(barrier, total - 1 + 3)

    def swap(n):
        return copy(wfull.at[n, quarter], wfull.at[n, quarter], swy.at[n], rwy.at[n], across)

    def lend(n):
        return copy(wfull.at[n, quarter], wfull.at[n, quarter], swc.at[n], rwc.at[n], partner)

    def relay(n):
        held = wfull.at[n, 2 * (1 - side) + core]
        return copy(held, held, swf.at[n], rwf.at[n], partner)

    def give(q, t):
        z, member = peer(t)
        return copy(blk.at[q, z], recv1.at[q, flat], s1.at[q, t], r1.at[q, t], device(z, side, core, member))

    def take(q, t):
        z, member = peer(t)
        place = recv1.at[q, z * members + member]
        copy(blk.at[q, 0], place, s1.at[q, t], r1.at[q, t], partner).wait_recv()

    def weights_in(n):
        swap(n).wait_recv()
        relay(n).start()
        lend(n).wait_recv()

    swap(0).start()
    each(1, total, lambda t: give(0, t).start())
    lend(0).start()
    swap(1).start()
    swap(2).start()
    each(1, total, lambda t: give(1, t).start())
    lend(1).start()
    lend(2).start()
    for q in range(2):
        recv1[q, flat] = blk[q, line]

    def product(n, q):
        left = jnp.concatenate([recv1[q, :, k].reshape(total * cap, depth) for k in range(4)], axis=1)
        term = dot(left, wfull[n].reshape(line_depth, width), ((1,), (0,)))
        term = term.reshape(lines, members * cap, width)
        part[n] = term
        send2[n] = term.astype(BF16)
        for d in range(1, lines):
            z, there = on_line(d)
            copy(send2.at[n, z], recv2.at[n, line], s2.at[n, d], r2.at[n, d], there).start()

    def summed(n):
        total_rows = part[n, line]
        for d in range(1, lines):
            z, there = on_line(d)
            copy(send2.at[n, 0], recv2.at[n, z], s2.at[n, d], r2.at[n, d], there).wait_recv()
            total_rows += recv2[n, z].astype(F32)
        return total_rows

    weights_in(0)
    each(1, total, functools.partial(take, 0))
    relay(0).wait_recv()
    product(0, 0)
    weights_in(1)
    relay(1).wait_recv()
    product(1, 0)
    weights_in(2)
    each(1, total, functools.partial(take, 1))
    relay(2).wait_recv()
    product(2, 1)

    def share(q, n):
        k, there = beside(n)
        return copy(recv1.at[q, :, k], rows_all.at[q, quarter], sx.at[q, n], rx.at[q, n], there)

    for q in range(2):
        for n in range(3):
            share(q, n).start()
        rows_all[q, quarter] = recv1[q, :, quarter]

    def held(n, z):
        return all3.at[n, quarter, z]

    def spread_out(n):
        for d in range(1, lines):
            _, there = on_line(d)
            copy(held(n, line), held(n, line), s3z.at[n, d], r3z.at[n, d], there).start()
        copy(held(n, line), held(n, line), s3y.at[n, 0], r3y.at[n, 0], across).start()

    def pass_on(n):
        for d in range(1, lines):
            z, there = on_line(d)
            copy(held(n, line), held(n, z), s3z.at[n, d], r3z.at[n, d], there).wait_recv()
            copy(held(n, z), held(n, z), s3y.at[n, d], r3y.at[n, d], across).start()
        mine = all3.at[n, quarter]
        copy(mine, mine, s3c.at[n, 0], r3c.at[n, 0], partner).start()

    def from_across(n):
        other = 2 * (1 - side) + core
        for d in range(lines):
            z, _ = on_line(d)
            copy(held(n, line), all3.at[n, other, z], s3y.at[n, d], r3y.at[n, d], across).wait_recv()
        theirs = all3.at[n, other]
        copy(theirs, theirs, s3c.at[n, 1], r3c.at[n, 1], partner).start()

    def from_partner(n):
        for h, y in enumerate((side, 1 - side)):
            place = all3.at[n, 2 * y + 1 - core]
            copy(place, place, s3c.at[n, h], r3c.at[n, h], partner).wait_recv()

    gate, up = summed(0), summed(1)
    sig = 1.0 / (1.0 + jnp.exp(-gate))
    all3[0, quarter, line] = (gate * sig * up).astype(BF16)
    spread_out(0)
    dhidden = summed(2)
    all3[1, quarter, line] = (dhidden * up * sig * (1.0 + gate * (1.0 - sig))).astype(BF16)
    spread_out(1)
    all3[2, quarter, line] = (dhidden * gate * sig).astype(BF16)
    spread_out(2)

    pass_on(0)
    hidden = all3[0, quarter].reshape(total * cap, width)
    out = dot(hidden, wfull[2].reshape(line_depth, width), ((1,), (1,)))
    send4[...] = out.astype(BF16).reshape(total, cap, line_depth)

    def return_rows(t):
        z, member = peer(t)
        there = device(z, side, core, member)
        return copy(send4.at[z * members + member], recv4.at[j, line], s4.at[t], r4.at[t], there)

    each(1, total, lambda t: return_rows(t).start())
    recv4[j, line] = send4[flat]
    pass_on(1)
    pass_on(2)
    for q in range(2):
        for n in range(3):
            k, there = beside(n)
            copy(rows_all.at[q, 0], rows_all.at[q, k], sx.at[q, n], rx.at[q, n], there).wait_recv()

    def gradient(n, q, result):
        from_partner(n)
        left = rows_all[q].reshape(4 * total * cap, depth)
        result[...] = dot(left, all3[n].reshape(4 * total * cap, width), ((0,), (0,))).astype(BF16)

    from_across(0)
    gradient(0, 1, grad_down)
    from_across(1)
    gradient(1, 0, grad_gate)
    from_across(2)

    def rows_back(t):
        z, member = peer(t)
        copy(send4.at[0], recv4.at[member, z], s4.at[t], r4.at[t], partner).wait_recv()

    each(1, total, rows_back)
    for z in range(lines):
        out_rows = recv4[0, z].astype(F32)
        for m in range(1, members):
            out_rows += recv4[m, z].astype(F32)
        placed = dot(spread, (out_rows * slot_weight).astype(BF16), ((1,), (0,)))
        mixed[:, z * line_depth : (z + 1) * line_depth] = placed.astype(BF16)
    gradient(2, 0, grad_up)

    def sent(t):
        for q in range(2):
            copy(blk.at[q, 0], recv1.at[q, 0], s1.at[q, t], r1.at[q, t], partner).wait_send()
        copy(send4.at[0], recv4.at[0, 0], s4.at[t], r4.at[t], partner).wait_send()

    each(1, total, sent)
    for n in range(3):
        swap(n).wait_send()
        lend(n).wait_send()
        relay(n).wait_send()
        for q in range(2):
            share(q, n).wait_send()
        for d in range(1, lines):
            copy(send2.at[n, 0], recv2.at[n, 0], s2.at[n, d], r2.at[n, d], partner).wait_send()
            copy(held(n, 0), held(n, 0), s3z.at[n, d], r3z.at[n, d], partner).wait_send()
        for d in range(lines):
            copy(held(n, 0), held(n, 0), s3y.at[n, d], r3y.at[n, d], across).wait_send()
        for h in range(2):
            copy(all3.at[n, 0], all3.at[n, 0], s3c.at[n, h], r3c.at[n, h], partner).wait_send()


def write_out(*refs):
    sems = refs[-1]
    copies = [pltpu.make_async_copy(refs[n], refs[4 + n], sems.at[n]) for n in range(4)]
    for c in copies:
        c.start()
    for c in copies:
        c.wait()


def per_device(lines, members, tokens, cotangent, expert_ids, route_weights, join_groups, w_gate, w_up, w_down):
    tok_count, model = tokens.shape
    depth, width = w_gate.shape
    cap = tok_count // 8
    total = lines * members
    rows = members * cap
    vmem = pl.BlockSpec(memory_space=pltpu.VMEM)
    hbm = pl.BlockSpec(memory_space=pl.ANY)
    dma = pltpu.SemaphoreType.DMA
    grad = pltpu.VMEM((depth, width), BF16)
    results = pl.pallas_call(
        functools.partial(kernel, lines, members, cap),
        out_shape=(pltpu.VMEM((tok_count, model), BF16), grad, grad, grad),
        in_specs=[pl.BlockSpec(memory_space=pltpu.SMEM), hbm, hbm, vmem, vmem, hbm, hbm, hbm],
        out_specs=(vmem,) * 4,
        scratch_shapes=[
            pltpu.VMEM((tok_count, model), BF16),
            pltpu.VMEM((tok_count, model), BF16),
            pltpu.VMEM((3, 4, depth, width), BF16),
            pltpu.VMEM((2, lines, 4, cap, depth), BF16),
            pltpu.VMEM((2, total, 4, cap, depth), BF16),
            pltpu.VMEM((2, 4, total, cap, depth), BF16),
            pltpu.VMEM((3, lines, rows, width), F32),
            pltpu.VMEM((3, lines, rows, width), BF16),
            pltpu.VMEM((3, lines, rows, width), BF16),
            pltpu.VMEM((3, 4, lines, rows, width), BF16),
            pltpu.VMEM((total, cap, 4 * depth), BF16),
            pltpu.VMEM((members, lines, cap, 4 * depth), BF16),
            dma((5,)),
            dma((3,)), dma((3,)), dma((3,)), dma((3,)), dma((3,)), dma((3,)),
            dma((2, total)), dma((2, total)),
            dma((2, 3)), dma((2, 3)),
            dma((3, lines)), dma((3, lines)),
            dma((3, lines)), dma((3, lines)),
            dma((3, lines)), dma((3, lines)),
            dma((3, 2)), dma((3, 2)),
            dma((total,)), dma((total,)),
        ],
        compiler_params=pltpu.CompilerParams(
            collective_id=0, has_side_effects=True, vmem_limit_bytes=60 * 1024 * 1024
        ),
        name="expert_step",
    )(join_groups, tokens, cotangent, expert_ids.T, route_weights.T, w_gate, w_up, w_down)
    return pl.pallas_call(
        write_out,
        out_shape=tuple(jax.ShapeDtypeStruct(r.shape, r.dtype) for r in results),
        in_specs=[vmem] * 4,
        out_specs=(hbm,) * 4,
        scratch_shapes=[dma((4,))],
        name="write_out",
    )(*(pltpu.with_memory_space_constraint(r, pltpu.VMEM) for r in results))


def solution(mesh):
    in_specs = (
        P(("dp", "expert"), None),
        P(("dp", "expert"), None),
        P(("dp", "expert"), None),
        P(("dp", "expert"), None),
        P(),
        P("dp", "expert"),
        P("dp", "expert"),
        P("dp", "expert"),
    )
    out_specs = (P(("dp", "expert"), None), P("dp", "expert"), P("dp", "expert"), P("dp", "expert"))
    body = functools.partial(per_device, mesh.shape["dp"] // 4, mesh.shape["expert"])
    return jax.shard_map(body, mesh=mesh, in_specs=in_specs, out_specs=out_specs, check_vma=False)
```

```python
import functools

import jax
import jax.numpy as jnp
from jax import lax
from jax.experimental import pallas as pl
from jax.experimental.pallas import tpu as pltpu
from jax.sharding import PartitionSpec as P

F32, BF16 = jnp.float32, jnp.bfloat16
MESH = pl.DeviceIdType.MESH


def dot(a, b, dims):
    return lax.dot_general(a, b, (dims, ((), ())), preferred_element_type=F32)


def flip(a, d, count):
    out, bit = 0, 1
    while bit < count:
        mine = lax.rem(lax.div(a, bit), 2)
        turn = (d // bit) % 2 if isinstance(d, int) else lax.rem(lax.div(d, bit), 2)
        out += bit * (mine + turn - 2 * mine * turn)
        bit *= 2
    return out


def each(low, high, body):
    if high - low <= 16:
        for i in range(low, high):
            body(i)
    else:
        lax.fori_loop(low, high, lambda i, carry: (body(i), carry)[1], 0)


def kernel(
    lines, members, cap,
    join, tok, cot, ids, wts, wg, wu, wd,
    mixed, grad_gate, grad_up, grad_down,
    joinv, idv, wtv, tokv, cotv, wfull, blk, recv1, rows_all, part, send2, recv2, all3, send4, recv4,
    local, out, rwy, rwp, r1, rx, r2, r3z, r3y, r3c, r4,
):
    p, j = lax.axis_index("dp"), lax.axis_index("expert")
    line, side, core = lax.div(p, 4), lax.rem(lax.div(p, 2), 2), lax.rem(p, 2)
    quarter = 2 * side + core
    total = lines * members
    flat = line * members + j
    tok_count = tok.shape[0]
    depth, width = wg.shape
    line_depth = 4 * depth

    def device(z, y, c, member):
        return (4 * z + 2 * y + c, member)

    partner = device(line, side, 1 - core, j)
    across = device(line, 1 - side, core, j)

    def copy(src, dst, send, recv, target):
        return pltpu.make_async_remote_copy(
            src_ref=src, dst_ref=dst, send_sem=send, recv_sem=recv, device_id=target, device_id_type=MESH
        )

    def peer(t):
        if isinstance(t, int):
            dz, dj = t // members, t % members
        else:
            dz, dj = lax.div(t, members), lax.rem(t, members)
        return flip(line, dz, lines), flip(j, dj, members)

    def on_line(d):
        z = flip(line, d, lines)
        return z, device(z, side, core, j)

    near = [(0, 1), (1, 0), (1, 1)]

    def beside(n):
        y = 1 - side if near[n][0] else side
        c = 1 - core if near[n][1] else core
        return 2 * y + c, device(line, y, c, j)

    barrier = pltpu.get_barrier_semaphore()

    def greet(t):
        z, member = peer(t)
        pl.semaphore_signal(barrier, inc=1, device_id=device(z, side, core, member), device_id_type=MESH)

    each(1, total, greet)
    for n in range(3):
        pl.semaphore_signal(barrier, inc=1, device_id=beside(n)[1], device_id_type=MESH)

    loads = [
        pltpu.make_async_copy(src, dst, local.at[n])
        for n, (src, dst) in enumerate(((ids, idv), (wts, wtv), (join, joinv), (tok, tokv), (cot, cotv)))
    ]
    own = [pltpu.make_async_copy(w, wfull.at[n, quarter], local.at[5]) for n, w in enumerate((wg, wu, wd))]
    for load in loads[:3] + own + loads[3:]:
        load.start()
    for load in loads[:2]:
        load.wait()

    chosen = idv[...] == 0
    routed = jnp.max(jnp.where(chosen, 1.0, 0.0), axis=0, keepdims=True)
    weight = jnp.sum(jnp.where(chosen, wtv[...], 0.0), axis=0, keepdims=True)
    upper = lax.broadcasted_iota(jnp.int32, (tok_count, tok_count), 0) <= lax.broadcasted_iota(
        jnp.int32, (tok_count, tok_count), 1
    )
    wide = jnp.broadcast_to(routed, (cap, tok_count))
    places = dot(wide.astype(BF16), jnp.where(upper, 1.0, 0.0).astype(BF16), ((1,), (0,))) - 1.0
    slot = lax.broadcasted_iota(jnp.int32, (cap, tok_count), 0).astype(F32)
    pick = jnp.where((places == slot) & (wide > 0.5), 1.0, 0.0)
    slot_weight = jnp.sum(pick * weight, axis=1, keepdims=True)
    spread = pick.T.astype(BF16)
    pick = pick.astype(BF16)
    loads[2].wait()
    active = 1.0 - joinv[p].astype(F32)
    mine = wfull.at[:, quarter]
    pltpu.make_async_copy(mine, mine, local.at[5]).wait()

    def swap(n):
        return copy(wfull.at[n, quarter], wfull.at[n, quarter], out.at[0], rwy.at[n], across)

    def lend(n):
        return copy(wfull.at[n, quarter], wfull.at[n, quarter], out.at[1], rwp.at[n], partner)

    def relay(n):
        held = wfull.at[n, 2 * (1 - side) + core]
        return copy(held, held, out.at[2], rwp.at[n], partner)

    def give(q, t):
        z, member = peer(t)
        copy(blk.at[q, z], recv1.at[q, flat], out.at[3], r1.at[q], device(z, side, core, member)).start()

    def cut(q, taken):
        for z in range(lines):
            for k in range(4):
                at = z * line_depth + k * depth
                blk[q, z, k] = taken[:, at : at + depth]

    def arrived(ref, recv):
        copy(ref, ref, out.at[0], recv, partner).wait_recv()

    def departed(ref, n):
        copy(ref, ref, out.at[n], rx, partner).wait_send()

    pl.semaphore_wait(barrier, total - 1 + 3)

    swap(0).start()
    loads[3].wait()
    cut(0, dot(pick, tokv[...], ((1,), (0,))).astype(BF16))
    each(1, total, functools.partial(give, 0))
    swap(1).start()
    lend(0).start()
    loads[4].wait()
    cut(1, (dot(pick, cotv[...], ((1,), (0,))) * (slot_weight * active)).astype(BF16))
    swap(2).start()
    each(1, total, functools.partial(give, 1))
    lend(1).start()
    lend(2).start()
    for q in range(2):
        recv1[q, flat] = blk[q, line]

    def product(n, q):
        left = jnp.concatenate([recv1[q, :, k].reshape(total * cap, depth) for k in range(4)], axis=1)
        term = dot(left, wfull[n].reshape(line_depth, width), ((1,), (0,)))
        term = term.reshape(lines, members * cap, width)
        part[n] = term
        send2[n] = term.astype(BF16)
        for d in range(1, lines):
            z, there = on_line(d)
            copy(send2.at[n, z], recv2.at[n, line], out.at[4], r2.at[n], there).start()

    def summed(n):
        arrived(send2.at[n, 1:], r2.at[n])
        total_rows = part[n, line]
        for d in range(1, lines):
            total_rows += recv2[n, on_line(d)[0]].astype(F32)
        return total_rows

    def stage(n, q):
        swap(n).wait_recv()
        relay(n).start()
        if n != 1:
            arrived(recv1.at[q, 1:], r1.at[q])
        arrived(wfull.at[n, 0:2], rwp.at[n])
        product(n, q)

    stage(0, 0)
    stage(1, 0)
    stage(2, 1)

    def share(q, n):
        k, there = beside(n)
        return copy(recv1.at[q, :, k], rows_all.at[q, quarter], out.at[5], rx, there)

    for q in range(2):
        for n in range(3):
            share(q, n).start()
        rows_all[q, quarter] = recv1[q, :, quarter]

    def held(n, z):
        return all3.at[n, quarter, z]

    def spread_out(n):
        for d in range(1, lines):
            _, there = on_line(d)
            copy(held(n, line), held(n, line), out.at[6], r3z.at[n, d - 1], there).start()
        copy(held(n, line), held(n, line), out.at[7], r3y.at[n], across).start()

    def pass_on(n):
        for d in range(1, lines):
            z, there = on_line(d)
            copy(held(n, line), held(n, z), out.at[6], r3z.at[n, d - 1], there).wait_recv()
            copy(held(n, z), held(n, z), out.at[7], r3y.at[n], across).start()
        mine = all3.at[n, quarter]
        copy(mine, mine, out.at[8], r3c.at[n], partner).start()

    def from_across(n):
        arrived(all3.at[n, 0], r3y.at[n])
        theirs = all3.at[n, 2 * (1 - side) + core]
        copy(theirs, theirs, out.at[8], r3c.at[n], partner).start()

    def gradient(n, q, result):
        arrived(all3.at[n, 0:2], r3c.at[n])
        left = rows_all[q].reshape(4 * total * cap, depth)
        result[...] = dot(left, all3[n].reshape(4 * total * cap, width), ((0,), (0,))).astype(BF16)

    gate, up = summed(0), summed(1)
    sig = 1.0 / (1.0 + jnp.exp(-gate))
    all3[0, quarter, line] = (gate * sig * up).astype(BF16)
    spread_out(0)
    dhidden = summed(2)
    all3[1, quarter, line] = (dhidden * up * sig * (1.0 + gate * (1.0 - sig))).astype(BF16)
    spread_out(1)
    all3[2, quarter, line] = (dhidden * gate * sig).astype(BF16)
    spread_out(2)

    pass_on(0)
    hidden = all3[0, quarter].reshape(total * cap, width)
    rows_out = dot(hidden, wfull[2].reshape(line_depth, width), ((1,), (1,)))
    send4[...] = rows_out.astype(BF16).reshape(total, cap, line_depth)

    def return_rows(t):
        z, member = peer(t)
        there = device(z, side, core, member)
        copy(send4.at[z * members + member], recv4.at[j, line], out.at[9], r4, there).start()

    each(1, total, return_rows)
    recv4[j, line] = send4[flat]
    pass_on(1)
    from_across(0)
    pass_on(2)
    arrived(rows_all.at[:, 0:3], rx)
    gradient(0, 1, grad_down)
    from_across(1)
    from_across(2)
    gradient(1, 0, grad_gate)
    arrived(send4.at[1:], r4)
    for z in range(lines):
        out_rows = recv4[0, z].astype(F32)
        for m in range(1, members):
            out_rows += recv4[m, z].astype(F32)
        placed = dot(spread, (out_rows * slot_weight).astype(BF16), ((1,), (0,)))
        mixed[:, z * line_depth : (z + 1) * line_depth] = placed.astype(BF16)
    gradient(2, 0, grad_up)

    for n in range(3):
        departed(wfull.at[:, 0], n)
    departed(recv1.at[:, 1:], 3)
    departed(send2.at[:, 1:], 4)
    departed(rows_all.at[:, 0:3], 5)
    departed(all3.at[:, 0, 1:], 6)
    departed(all3.at[:, 0], 7)
    departed(all3.at[:, 0:2], 8)
    departed(send4.at[1:], 9)


def write_out(*refs):
    sems = refs[-1]
    copies = [pltpu.make_async_copy(refs[n], refs[4 + n], sems.at[n]) for n in range(4)]
    for c in copies:
        c.start()
    for c in copies:
        c.wait()


def per_device(lines, members, tokens, cotangent, expert_ids, route_weights, join_groups, w_gate, w_up, w_down):
    tok_count, model = tokens.shape
    depth, width = w_gate.shape
    cap = tok_count // 8
    total = lines * members
    rows = members * cap
    vmem = pl.BlockSpec(memory_space=pltpu.VMEM)
    hbm = pl.BlockSpec(memory_space=pl.ANY)
    dma = pltpu.SemaphoreType.DMA
    grad = pltpu.VMEM((depth, width), BF16)
    results = pl.pallas_call(
        functools.partial(kernel, lines, members, cap),
        out_shape=(pltpu.VMEM((tok_count, model), BF16), grad, grad, grad),
        in_specs=[hbm] * 8,
        out_specs=(vmem,) * 4,
        scratch_shapes=[
            pltpu.SMEM(join_groups.shape, jnp.int32),
            pltpu.VMEM(expert_ids.shape[::-1], jnp.int32),
            pltpu.VMEM(route_weights.shape[::-1], F32),
            pltpu.VMEM((tok_count, model), BF16),
            pltpu.VMEM((tok_count, model), BF16),
            pltpu.VMEM((3, 4, depth, width), BF16),
            pltpu.VMEM((2, lines, 4, cap, depth), BF16),
            pltpu.VMEM((2, total, 4, cap, depth), BF16),
            pltpu.VMEM((2, 4, total, cap, depth), BF16),
            pltpu.VMEM((3, lines, rows, width), F32),
            pltpu.VMEM((3, lines, rows, width), BF16),
            pltpu.VMEM((3, lines, rows, width), BF16),
            pltpu.VMEM((3, 4, lines, rows, width), BF16),
            pltpu.VMEM((total, cap, 4 * depth), BF16),
            pltpu.VMEM((members, lines, cap, 4 * depth), BF16),
            dma((6,)), dma((10,)),
            dma((3,)), dma((3,)),
            dma((2,)), dma(()),
            dma((3,)),
            dma((3, lines - 1)), dma((3,)), dma((3,)),
            dma(()),
        ],
        compiler_params=pltpu.CompilerParams(
            collective_id=0, has_side_effects=True, vmem_limit_bytes=60 * 1024 * 1024
        ),
        name="expert_step",
    )(join_groups, tokens, cotangent, expert_ids.T, route_weights.T, w_gate, w_up, w_down)
    return pl.pallas_call(
        write_out,
        out_shape=tuple(jax.ShapeDtypeStruct(r.shape, r.dtype) for r in results),
        in_specs=[vmem] * 4,
        out_specs=(hbm,) * 4,
        scratch_shapes=[dma((4,))],
        name="write_out",
    )(*(pltpu.with_memory_space_constraint(r, pltpu.VMEM) for r in results))


def solution(mesh):
    in_specs = (
        P(("dp", "expert"), None),
        P(("dp", "expert"), None),
        P(("dp", "expert"), None),
        P(("dp", "expert"), None),
        P(),
        P("dp", "expert"),
        P("dp", "expert"),
        P("dp", "expert"),
    )
    out_specs = (P(("dp", "expert"), None), P("dp", "expert"), P("dp", "expert"), P("dp", "expert"))
    body = functools.partial(per_device, mesh.shape["dp"] // 4, mesh.shape["expert"])
    return jax.shard_map(body, mesh=mesh, in_specs=in_specs, out_specs=out_specs, check_vma=False)
```

```python
import functools

import jax
import jax.numpy as jnp
from jax import lax
from jax.experimental import pallas as pl
from jax.experimental.pallas import tpu as pltpu
from jax.sharding import PartitionSpec as P

F32, BF16 = jnp.float32, jnp.bfloat16
MESH = pl.DeviceIdType.MESH


def dot(a, b, dims):
    return lax.dot_general(a, b, (dims, ((), ())), preferred_element_type=F32)


def flip(a, d, count):
    out, bit = 0, 1
    while bit < count:
        mine = lax.rem(lax.div(a, bit), 2)
        turn = (d // bit) % 2 if isinstance(d, int) else lax.rem(lax.div(d, bit), 2)
        out += bit * (mine + turn - 2 * mine * turn)
        bit *= 2
    return out


def each(low, high, body):
    if high - low <= 16:
        for i in range(low, high):
            body(i)
    else:
        lax.fori_loop(low, high, lambda i, carry: (body(i), carry)[1], 0)


def kernel(
    lines, members, cap,
    join, tok, cot, ids, wts, wg, wu, wd,
    mixed, grad_gate, grad_up, grad_down,
    joinv, idv, wtv, tokv, cotv, wfull, blk, recv1, rows_all, part, send2, recv2, all3, send4, recv4,
    local, out, rwy, rwp, r1, rx, r2, r3z, r3y, r3c, r4,
):
    p, j = lax.axis_index("dp"), lax.axis_index("expert")
    line, side, core = lax.div(p, 4), lax.rem(lax.div(p, 2), 2), lax.rem(p, 2)
    quarter = 2 * side + core
    total = lines * members
    flat = line * members + j
    tok_count = tok.shape[0]
    depth, width = wg.shape
    line_depth = 4 * depth

    def device(z, y, c, member):
        return (4 * z + 2 * y + c, member)

    partner = device(line, side, 1 - core, j)
    across = device(line, 1 - side, core, j)

    def copy(src, dst, send, recv, target):
        return pltpu.make_async_remote_copy(
            src_ref=src, dst_ref=dst, send_sem=send, recv_sem=recv, device_id=target, device_id_type=MESH
        )

    def peer(t):
        if isinstance(t, int):
            dz, dj = t // members, t % members
        else:
            dz, dj = lax.div(t, members), lax.rem(t, members)
        return flip(line, dz, lines), flip(j, dj, members)

    def on_line(d):
        z = flip(line, d, lines)
        return z, device(z, side, core, j)

    near = [(0, 1), (1, 0), (1, 1)]

    def beside(n):
        y = 1 - side if near[n][0] else side
        c = 1 - core if near[n][1] else core
        return 2 * y + c, device(line, y, c, j)

    barrier = pltpu.get_barrier_semaphore()

    def greet(t):
        z, member = peer(t)
        pl.semaphore_signal(barrier, inc=1, device_id=device(z, side, core, member), device_id_type=MESH)

    each(1, total, greet)
    for n in range(3):
        pl.semaphore_signal(barrier, inc=1, device_id=beside(n)[1], device_id_type=MESH)

    loads = [
        pltpu.make_async_copy(src, dst, local.at[n])
        for n, (src, dst) in enumerate(((ids, idv), (wts, wtv), (join, joinv), (tok, tokv), (cot, cotv)))
    ]
    own = [pltpu.make_async_copy(w, wfull.at[n, quarter], local.at[5]) for n, w in enumerate((wg, wu, wd))]
    for load in loads[:3] + own + loads[3:]:
        load.start()
    for load in loads[:2]:
        load.wait()

    chosen = idv[...] == 0
    routed = jnp.max(jnp.where(chosen, 1.0, 0.0), axis=0, keepdims=True)
    weight = jnp.sum(jnp.where(chosen, wtv[...], 0.0), axis=0, keepdims=True)
    upper = lax.broadcasted_iota(jnp.int32, (tok_count, tok_count), 0) <= lax.broadcasted_iota(
        jnp.int32, (tok_count, tok_count), 1
    )
    wide = jnp.broadcast_to(routed, (cap, tok_count))
    places = dot(wide.astype(BF16), jnp.where(upper, 1.0, 0.0).astype(BF16), ((1,), (0,))) - 1.0
    slot = lax.broadcasted_iota(jnp.int32, (cap, tok_count), 0).astype(F32)
    pick = jnp.where((places == slot) & (wide > 0.5), 1.0, 0.0)
    slot_weight = jnp.sum(pick * weight, axis=1, keepdims=True)
    spread = pick.T.astype(BF16)
    pick = pick.astype(BF16)
    loads[2].wait()
    active = 1.0 - joinv[p].astype(F32)
    mine = wfull.at[:, quarter]
    pltpu.make_async_copy(mine, mine, local.at[5]).wait()

    def swap(n):
        return copy(wfull.at[n, quarter], wfull.at[n, quarter], out.at[0], rwy.at[n], across)

    def lend(n):
        return copy(wfull.at[n, quarter], wfull.at[n, quarter], out.at[1], rwp.at[n], partner)

    def relay(n):
        held = wfull.at[n, 2 * (1 - side) + core]
        return copy(held, held, out.at[2], rwp.at[n], partner)

    def give(q, t):
        z, member = peer(t)
        copy(blk.at[q, z], recv1.at[q, flat], out.at[3], r1.at[q], device(z, side, core, member)).start()

    def cut(q, taken):
        for z in range(lines):
            for k in range(4):
                at = z * line_depth + k * depth
                blk[q, z, k] = taken[:, at : at + depth]

    def arrived(ref, recv):
        copy(ref, ref, out.at[0], recv, partner).wait_recv()

    def departed(ref, n):
        copy(ref, ref, out.at[n], rx, partner).wait_send()

    pl.semaphore_wait(barrier, total - 1 + 3)

    swap(0).start()
    loads[3].wait()
    cut(0, dot(pick, tokv[...], ((1,), (0,))).astype(BF16))
    each(1, total, functools.partial(give, 0))
    swap(1).start()
    lend(0).start()
    loads[4].wait()
    cut(1, (dot(pick, cotv[...], ((1,), (0,))) * (slot_weight * active)).astype(BF16))
    swap(2).start()
    each(1, total, functools.partial(give, 1))
    lend(1).start()
    lend(2).start()
    for q in range(2):
        recv1[q, flat] = blk[q, line]

    def product(n, q):
        left = jnp.concatenate([recv1[q, :, k].reshape(total * cap, depth) for k in range(4)], axis=1)
        term = dot(left, wfull[n].reshape(line_depth, width), ((1,), (0,)))
        term = term.reshape(lines, members * cap, width)
        part[n] = term
        send2[n] = term.astype(BF16)
        for d in range(1, lines):
            z, there = on_line(d)
            copy(send2.at[n, z], recv2.at[n, line], out.at[4], r2.at[n], there).start()

    def summed(n):
        arrived(send2.at[n, 1:], r2.at[n])
        total_rows = part[n, line]
        for d in range(1, lines):
            total_rows += recv2[n, on_line(d)[0]].astype(F32)
        return total_rows

    def stage(n, q):
        swap(n).wait_recv()
        relay(n).start()
        if n != 1:
            arrived(recv1.at[q, 1:], r1.at[q])
        arrived(wfull.at[n, 0:2], rwp.at[n])
        product(n, q)

    stage(0, 0)
    stage(1, 0)
    stage(2, 1)

    def share(q, n):
        k, there = beside(n)
        return copy(recv1.at[q, :, k], rows_all.at[q, quarter], out.at[5], rx, there)

    for q in range(2):
        for n in range(3):
            share(q, n).start()
        rows_all[q, quarter] = recv1[q, :, quarter]

    def held(n, z):
        return all3.at[n, quarter, z]

    last = lines - 1
    at_end = (line == 0) | (line == last)
    beside_end = (line == 1) | (line == last - 1)

    def block(n, z, d, sem, there):
        return copy(held(n, z), held(n, z), sem, r3z.at[n, d - 1], there)

    def spread_out(*which):
        for d in [last - 1] + list(range(1, last - 1)):
            for n in which:
                block(n, line, d, out.at[6], on_line(d)[1]).start()
        for n in which:
            pl.when(jnp.logical_not(at_end))(block(n, line, last, out.at[10], on_line(last)[1]).start)
            copy(held(n, line), held(n, line), out.at[7], r3y.at[n], across).start()

    def pass_on(n):
        for d in range(1, lines):
            z, there = on_line(d)
            block(n, z, d, out.at[6], there).wait_recv()
            if d == last - 1:
                pl.when(beside_end)(block(n, z, last, out.at[11], on_line(1)[1]).start)
            copy(held(n, z), held(n, z), out.at[7], r3y.at[n], across).start()
        mine = all3.at[n, quarter]
        copy(mine, mine, out.at[8], r3c.at[n], partner).start()

    def from_across(n):
        arrived(all3.at[n, 0], r3y.at[n])
        theirs = all3.at[n, 2 * (1 - side) + core]
        copy(theirs, theirs, out.at[8], r3c.at[n], partner).start()

    def gradient(n, q, result):
        arrived(all3.at[n, 0:2], r3c.at[n])
        left = rows_all[q].reshape(4 * total * cap, depth)
        result[...] = dot(left, all3[n].reshape(4 * total * cap, width), ((0,), (0,))).astype(BF16)

    gate, up = summed(0), summed(1)
    sig = 1.0 / (1.0 + jnp.exp(-gate))
    all3[0, quarter, line] = (gate * sig * up).astype(BF16)
    spread_out(0)
    dhidden = summed(2)
    all3[1, quarter, line] = (dhidden * up * sig * (1.0 + gate * (1.0 - sig))).astype(BF16)
    all3[2, quarter, line] = (dhidden * gate * sig).astype(BF16)
    spread_out(1, 2)

    pass_on(0)
    hidden = all3[0, quarter].reshape(total * cap, width)
    rows_out = dot(hidden, wfull[2].reshape(line_depth, width), ((1,), (1,)))
    send4[...] = rows_out.astype(BF16).reshape(total, cap, line_depth)

    def return_rows(t):
        z, member = peer(t)
        there = device(z, side, core, member)
        copy(send4.at[z * members + member], recv4.at[j, line], out.at[9], r4, there).start()

    each(1, total, return_rows)
    recv4[j, line] = send4[flat]
    pass_on(1)
    from_across(0)
    pass_on(2)
    arrived(rows_all.at[:, 0:3], rx)
    gradient(0, 1, grad_down)
    from_across(1)
    from_across(2)
    gradient(1, 0, grad_gate)
    arrived(send4.at[1:], r4)
    for z in range(lines):
        out_rows = recv4[0, z].astype(F32)
        for m in range(1, members):
            out_rows += recv4[m, z].astype(F32)
        placed = dot(spread, (out_rows * slot_weight).astype(BF16), ((1,), (0,)))
        mixed[:, z * line_depth : (z + 1) * line_depth] = placed.astype(BF16)
    gradient(2, 0, grad_up)

    for n in range(3):
        departed(wfull.at[:, 0], n)
    departed(recv1.at[:, 1:], 3)
    departed(send2.at[:, 1:], 4)
    departed(rows_all.at[:, 0:3], 5)
    departed(all3.at[:, 0, 1:last], 6)
    pl.when(jnp.logical_not(at_end))(functools.partial(departed, all3.at[:, 0, 0], 10))
    pl.when(beside_end)(functools.partial(departed, all3.at[:, 0, 0], 11))
    departed(all3.at[:, 0], 7)
    departed(all3.at[:, 0:2], 8)
    departed(send4.at[1:], 9)


def write_out(*refs):
    sems = refs[-1]
    copies = [pltpu.make_async_copy(refs[n], refs[4 + n], sems.at[n]) for n in range(4)]
    for c in copies:
        c.start()
    for c in copies:
        c.wait()


def per_device(lines, members, tokens, cotangent, expert_ids, route_weights, join_groups, w_gate, w_up, w_down):
    tok_count, model = tokens.shape
    depth, width = w_gate.shape
    cap = tok_count // 8
    total = lines * members
    rows = members * cap
    vmem = pl.BlockSpec(memory_space=pltpu.VMEM)
    hbm = pl.BlockSpec(memory_space=pl.ANY)
    dma = pltpu.SemaphoreType.DMA
    grad = pltpu.VMEM((depth, width), BF16)
    results = pl.pallas_call(
        functools.partial(kernel, lines, members, cap),
        out_shape=(pltpu.VMEM((tok_count, model), BF16), grad, grad, grad),
        in_specs=[hbm] * 8,
        out_specs=(vmem,) * 4,
        scratch_shapes=[
            pltpu.SMEM(join_groups.shape, jnp.int32),
            pltpu.VMEM(expert_ids.shape[::-1], jnp.int32),
            pltpu.VMEM(route_weights.shape[::-1], F32),
            pltpu.VMEM((tok_count, model), BF16),
            pltpu.VMEM((tok_count, model), BF16),
            pltpu.VMEM((3, 4, depth, width), BF16),
            pltpu.VMEM((2, lines, 4, cap, depth), BF16),
            pltpu.VMEM((2, total, 4, cap, depth), BF16),
            pltpu.VMEM((2, 4, total, cap, depth), BF16),
            pltpu.VMEM((3, lines, rows, width), F32),
            pltpu.VMEM((3, lines, rows, width), BF16),
            pltpu.VMEM((3, lines, rows, width), BF16),
            pltpu.VMEM((3, 4, lines, rows, width), BF16),
            pltpu.VMEM((total, cap, 4 * depth), BF16),
            pltpu.VMEM((members, lines, cap, 4 * depth), BF16),
            dma((6,)), dma((12,)),
            dma((3,)), dma((3,)),
            dma((2,)), dma(()),
            dma((3,)),
            dma((3, lines - 1)), dma((3,)), dma((3,)),
            dma(()),
        ],
        compiler_params=pltpu.CompilerParams(
            collective_id=0, has_side_effects=True, vmem_limit_bytes=60 * 1024 * 1024
        ),
        name="expert_step",
    )(join_groups, tokens, cotangent, expert_ids.T, route_weights.T, w_gate, w_up, w_down)
    return pl.pallas_call(
        write_out,
        out_shape=tuple(jax.ShapeDtypeStruct(r.shape, r.dtype) for r in results),
        in_specs=[vmem] * 4,
        out_specs=(hbm,) * 4,
        scratch_shapes=[dma((4,))],
        name="write_out",
    )(*(pltpu.with_memory_space_constraint(r, pltpu.VMEM) for r in results))


def solution(mesh):
    in_specs = (
        P(("dp", "expert"), None),
        P(("dp", "expert"), None),
        P(("dp", "expert"), None),
        P(("dp", "expert"), None),
        P(),
        P("dp", "expert"),
        P("dp", "expert"),
        P("dp", "expert"),
    )
    out_specs = (P(("dp", "expert"), None), P("dp", "expert"), P("dp", "expert"), P("dp", "expert"))
    body = functools.partial(per_device, mesh.shape["dp"] // 4, mesh.shape["expert"])
    return jax.shard_map(body, mesh=mesh, in_specs=in_specs, out_specs=out_specs, check_vma=False)
```

```python
import functools

import jax
import jax.numpy as jnp
from jax import lax
from jax.experimental import pallas as pl
from jax.experimental.pallas import tpu as pltpu
from jax.sharding import PartitionSpec as P

F32, BF16 = jnp.float32, jnp.bfloat16
MESH = pl.DeviceIdType.MESH


def dot(a, b, dims):
    return lax.dot_general(a, b, (dims, ((), ())), preferred_element_type=F32)


def flip(a, d, count):
    out, bit = 0, 1
    while bit < count:
        mine = lax.rem(lax.div(a, bit), 2)
        turn = (d // bit) % 2 if isinstance(d, int) else lax.rem(lax.div(d, bit), 2)
        out += bit * (mine + turn - 2 * mine * turn)
        bit *= 2
    return out


def each(low, high, body):
    if high - low <= 16:
        for i in range(low, high):
            body(i)
    else:
        lax.fori_loop(low, high, lambda i, carry: (body(i), carry)[1], 0)


def kernel(
    lines, members, cap,
    join, tok, cot, ids, wts, wg, wu, wd,
    mixed, grad_gate, grad_up, grad_down,
    joinv, idv, wtv, tokv, cotv, wfull, blk, recv1, rows_all, part, send2, recv2, all3, send4, recv4,
    local, out, rwy, rwp, r1, rx, r2, r3z, r3y, r3c, r4,
):
    p, j = lax.axis_index("dp"), lax.axis_index("expert")
    line, side, core = lax.div(p, 4), lax.rem(lax.div(p, 2), 2), lax.rem(p, 2)
    quarter = 2 * side + core
    total = lines * members
    flat = line * members + j
    tok_count = tok.shape[0]
    depth, width = wg.shape
    line_depth = 4 * depth

    def device(z, y, c, member):
        return (4 * z + 2 * y + c, member)

    partner = device(line, side, 1 - core, j)
    across = device(line, 1 - side, core, j)

    def copy(src, dst, send, recv, target):
        return pltpu.make_async_remote_copy(
            src_ref=src, dst_ref=dst, send_sem=send, recv_sem=recv, device_id=target, device_id_type=MESH
        )

    def peer(t):
        if isinstance(t, int):
            dz, dj = t // members, t % members
        else:
            dz, dj = lax.div(t, members), lax.rem(t, members)
        return flip(line, dz, lines), flip(j, dj, members)

    def on_line(d):
        z = flip(line, d, lines)
        return z, device(z, side, core, j)

    near = [(0, 1), (1, 0), (1, 1)]

    def beside(n):
        y = 1 - side if near[n][0] else side
        c = 1 - core if near[n][1] else core
        return 2 * y + c, device(line, y, c, j)

    slanted = device(flip(line, 1, lines), 1 - side, core, j)
    barrier = pltpu.get_barrier_semaphore()

    def greet(t):
        z, member = peer(t)
        pl.semaphore_signal(barrier, inc=1, device_id=device(z, side, core, member), device_id_type=MESH)

    each(1, total, greet)
    for there in [beside(n)[1] for n in range(3)] + [slanted]:
        pl.semaphore_signal(barrier, inc=1, device_id=there, device_id_type=MESH)

    loads = [
        pltpu.make_async_copy(src, dst, local.at[n])
        for n, (src, dst) in enumerate(((ids, idv), (wts, wtv), (join, joinv), (tok, tokv), (cot, cotv)))
    ]
    own = [pltpu.make_async_copy(w, wfull.at[n, quarter], local.at[5]) for n, w in enumerate((wg, wu, wd))]
    for load in loads[:3] + own + loads[3:]:
        load.start()
    for load in loads[:2]:
        load.wait()

    chosen = idv[...] == 0
    routed = jnp.max(jnp.where(chosen, 1.0, 0.0), axis=0, keepdims=True)
    weight = jnp.sum(jnp.where(chosen, wtv[...], 0.0), axis=0, keepdims=True)
    upper = lax.broadcasted_iota(jnp.int32, (tok_count, tok_count), 0) <= lax.broadcasted_iota(
        jnp.int32, (tok_count, tok_count), 1
    )
    wide = jnp.broadcast_to(routed, (cap, tok_count))
    places = dot(wide.astype(BF16), jnp.where(upper, 1.0, 0.0).astype(BF16), ((1,), (0,))) - 1.0
    slot = lax.broadcasted_iota(jnp.int32, (cap, tok_count), 0).astype(F32)
    pick = jnp.where((places == slot) & (wide > 0.5), 1.0, 0.0)
    slot_weight = jnp.sum(pick * weight, axis=1, keepdims=True)
    spread = pick.T.astype(BF16)
    pick = pick.astype(BF16)
    loads[2].wait()
    active = 1.0 - joinv[p].astype(F32)
    mine = wfull.at[:, quarter]
    pltpu.make_async_copy(mine, mine, local.at[5]).wait()

    def swap(n):
        return copy(wfull.at[n, quarter], wfull.at[n, quarter], out.at[0], rwy.at[n], across)

    def lend(n):
        return copy(wfull.at[n, quarter], wfull.at[n, quarter], out.at[1], rwp.at[n], partner)

    def relay(n):
        held = wfull.at[n, 2 * (1 - side) + core]
        return copy(held, held, out.at[2], rwp.at[n], partner)

    def give(q, t):
        z, member = peer(t)
        copy(blk.at[q, z], recv1.at[q, flat], out.at[3], r1.at[q], device(z, side, core, member)).start()

    def cut(q, taken):
        for z in range(lines):
            for k in range(4):
                at = z * line_depth + k * depth
                blk[q, z, k] = taken[:, at : at + depth]

    def arrived(ref, recv):
        copy(ref, ref, out.at[0], recv, partner).wait_recv()

    def departed(ref, n):
        copy(ref, ref, out.at[n], rx, partner).wait_send()

    pl.semaphore_wait(barrier, total - 1 + 4)

    swap(0).start()
    loads[3].wait()
    cut(0, dot(pick, tokv[...], ((1,), (0,))).astype(BF16))
    each(1, total, functools.partial(give, 0))
    swap(1).start()
    lend(0).start()
    loads[4].wait()
    cut(1, (dot(pick, cotv[...], ((1,), (0,))) * (slot_weight * active)).astype(BF16))
    swap(2).start()
    each(1, total, functools.partial(give, 1))
    lend(1).start()
    lend(2).start()
    for q in range(2):
        recv1[q, flat] = blk[q, line]

    def product(n, q):
        left = jnp.concatenate([recv1[q, :, k].reshape(total * cap, depth) for k in range(4)], axis=1)
        term = dot(left, wfull[n].reshape(line_depth, width), ((1,), (0,)))
        term = term.reshape(lines, members * cap, width)
        part[n] = term
        send2[n] = term.astype(BF16)
        for d in range(1, lines):
            z, there = on_line(d)
            copy(send2.at[n, z], recv2.at[n, line], out.at[4], r2.at[n], there).start()

    def summed(n):
        arrived(send2.at[n, 1:], r2.at[n])
        total_rows = part[n, line]
        for d in range(1, lines):
            total_rows += recv2[n, on_line(d)[0]].astype(F32)
        return total_rows

    def stage(n, q):
        swap(n).wait_recv()
        relay(n).start()
        if n != 1:
            arrived(recv1.at[q, 1:], r1.at[q])
        arrived(wfull.at[n, 0:2], rwp.at[n])
        product(n, q)

    stage(0, 0)
    stage(1, 0)
    stage(2, 1)

    def share(q, n):
        k, there = beside(n)
        return copy(recv1.at[q, :, k], rows_all.at[q, quarter], out.at[5], rx, there)

    for q in range(2):
        for n in range(3):
            share(q, n).start()
        rows_all[q, quarter] = recv1[q, :, quarter]

    def held(n, z):
        return all3.at[n, quarter, z]

    last = lines - 1
    at_end = (line == 0) | (line == last)
    beside_end = (line == 1) | (line == last - 1)

    def block(n, z, d, sem, there):
        return copy(held(n, z), held(n, z), sem, r3z.at[n, d - 1], there)

    def spread_out(*which):
        for d in [last - 1] + list(range(1, last - 1)):
            for n in which:
                block(n, line, d, out.at[6], on_line(d)[1]).start()
        for n in which:
            pl.when(jnp.logical_not(at_end))(block(n, line, last, out.at[10], on_line(last)[1]).start)
            copy(held(n, line), held(n, line), out.at[7], r3y.at[n], across).start()

    def across_with(n, z, sem, there):
        return copy(held(n, z), held(n, z), sem, r3y.at[n], there)

    def take_in(n, d):
        z, there = on_line(d)
        block(n, z, d, out.at[6], there).wait_recv()
        if d == last - 1:

            @pl.when(beside_end)
            def _():
                block(n, z, last, out.at[11], on_line(1)[1]).start()
                across_with(n, z, out.at[12], slanted).start()

        if d == last:
            pl.when(jnp.logical_not(at_end))(across_with(n, z, out.at[13], across).start)
        else:
            across_with(n, z, out.at[7], across).start()

    def to_partner(n):
        mine = all3.at[n, quarter]
        copy(mine, mine, out.at[8], r3c.at[n], partner).start()

    def from_across(n):
        arrived(all3.at[n, 0], r3y.at[n])
        theirs = all3.at[n, 2 * (1 - side) + core]
        copy(theirs, theirs, out.at[8], r3c.at[n], partner).start()

    def gradient(n, q, result):
        arrived(all3.at[n, 0:2], r3c.at[n])
        left = rows_all[q].reshape(4 * total * cap, depth)
        result[...] = dot(left, all3[n].reshape(4 * total * cap, width), ((0,), (0,))).astype(BF16)

    gate, up = summed(0), summed(1)
    sig = 1.0 / (1.0 + jnp.exp(-gate))
    all3[0, quarter, line] = (gate * sig * up).astype(BF16)
    spread_out(0)
    dhidden = summed(2)
    all3[1, quarter, line] = (dhidden * up * sig * (1.0 + gate * (1.0 - sig))).astype(BF16)
    all3[2, quarter, line] = (dhidden * gate * sig).astype(BF16)
    spread_out(1, 2)

    def rows_out(steps):
        places = [flip(line, d, lines) for d in steps]
        hidden = jnp.concatenate([all3[0, quarter, z] for z in places], axis=0)
        rows = dot(hidden, wfull[2].reshape(line_depth, width), ((1,), (1,))).astype(BF16)
        rows = rows.reshape(len(places), members, cap, line_depth)
        for i, (d, z) in enumerate(zip(steps, places)):
            for m in range(members):
                send4[z * members + m] = rows[i, m]

            def send(dj, d=d, z=z):
                member = flip(j, dj, members)
                there = device(z, side, core, member)
                copy(send4.at[z * members + member], recv4.at[j, line], out.at[9], r4, there).start()

            for dj in range(0 if d else 1, members):
                send(dj)

    for d in range(1, last):
        take_in(0, d)
    rows_out(list(range(last)))
    for d in range(1, last):
        take_in(1, d)
        take_in(2, d)
    take_in(0, last)
    to_partner(0)
    rows_out([last])
    recv4[j, line] = send4[flat]
    for n in (1, 2):
        take_in(n, last)
        to_partner(n)
    from_across(0)
    from_across(1)
    arrived(rows_all.at[:, 0:3], rx)
    gradient(0, 1, grad_down)
    from_across(2)
    gradient(1, 0, grad_gate)
    arrived(send4.at[1:], r4)
    for z in range(lines):
        out_rows = recv4[0, z].astype(F32)
        for m in range(1, members):
            out_rows += recv4[m, z].astype(F32)
        placed = dot(spread, (out_rows * slot_weight).astype(BF16), ((1,), (0,)))
        mixed[:, z * line_depth : (z + 1) * line_depth] = placed.astype(BF16)
    gradient(2, 0, grad_up)

    for n in range(3):
        departed(wfull.at[:, 0], n)
    departed(recv1.at[:, 1:], 3)
    departed(send2.at[:, 1:], 4)
    departed(rows_all.at[:, 0:3], 5)
    departed(all3.at[:, 0, 1:last], 6)
    pl.when(jnp.logical_not(at_end))(functools.partial(departed, all3.at[:, 0, 0], 10))
    pl.when(jnp.logical_not(at_end))(functools.partial(departed, all3.at[:, 0, 0], 13))
    pl.when(beside_end)(functools.partial(departed, all3.at[:, 0, 0], 11))
    pl.when(beside_end)(functools.partial(departed, all3.at[:, 0, 0], 12))
    departed(all3.at[:, 0, 0:last], 7)
    departed(all3.at[:, 0:2], 8)
    departed(send4.at[1:], 9)


def write_out(*refs):
    sems = refs[-1]
    copies = [pltpu.make_async_copy(refs[n], refs[4 + n], sems.at[n]) for n in range(4)]
    for c in copies:
        c.start()
    for c in copies:
        c.wait()


def per_device(lines, members, tokens, cotangent, expert_ids, route_weights, join_groups, w_gate, w_up, w_down):
    tok_count, model = tokens.shape
    depth, width = w_gate.shape
    cap = tok_count // 8
    total = lines * members
    rows = members * cap
    vmem = pl.BlockSpec(memory_space=pltpu.VMEM)
    hbm = pl.BlockSpec(memory_space=pl.ANY)
    dma = pltpu.SemaphoreType.DMA
    grad = pltpu.VMEM((depth, width), BF16)
    results = pl.pallas_call(
        functools.partial(kernel, lines, members, cap),
        out_shape=(pltpu.VMEM((tok_count, model), BF16), grad, grad, grad),
        in_specs=[hbm] * 8,
        out_specs=(vmem,) * 4,
        scratch_shapes=[
            pltpu.SMEM(join_groups.shape, jnp.int32),
            pltpu.VMEM(expert_ids.shape[::-1], jnp.int32),
            pltpu.VMEM(route_weights.shape[::-1], F32),
            pltpu.VMEM((tok_count, model), BF16),
            pltpu.VMEM((tok_count, model), BF16),
            pltpu.VMEM((3, 4, depth, width), BF16),
            pltpu.VMEM((2, lines, 4, cap, depth), BF16),
            pltpu.VMEM((2, total, 4, cap, depth), BF16),
            pltpu.VMEM((2, 4, total, cap, depth), BF16),
            pltpu.VMEM((3, lines, rows, width), F32),
            pltpu.VMEM((3, lines, rows, width), BF16),
            pltpu.VMEM((3, lines, rows, width), BF16),
            pltpu.VMEM((3, 4, lines, rows, width), BF16),
            pltpu.VMEM((total, cap, 4 * depth), BF16),
            pltpu.VMEM((members, lines, cap, 4 * depth), BF16),
            dma((6,)), dma((14,)),
            dma((3,)), dma((3,)),
            dma((2,)), dma(()),
            dma((3,)),
            dma((3, lines - 1)), dma((3,)), dma((3,)),
            dma(()),
        ],
        compiler_params=pltpu.CompilerParams(
            collective_id=0, has_side_effects=True, vmem_limit_bytes=60 * 1024 * 1024
        ),
        name="expert_step",
    )(join_groups, tokens, cotangent, expert_ids.T, route_weights.T, w_gate, w_up, w_down)
    return pl.pallas_call(
        write_out,
        out_shape=tuple(jax.ShapeDtypeStruct(r.shape, r.dtype) for r in results),
        in_specs=[vmem] * 4,
        out_specs=(hbm,) * 4,
        scratch_shapes=[dma((4,))],
        name="write_out",
    )(*(pltpu.with_memory_space_constraint(r, pltpu.VMEM) for r in results))


def solution(mesh):
    in_specs = (
        P(("dp", "expert"), None),
        P(("dp", "expert"), None),
        P(("dp", "expert"), None),
        P(("dp", "expert"), None),
        P(),
        P("dp", "expert"),
        P("dp", "expert"),
        P("dp", "expert"),
    )
    out_specs = (P(("dp", "expert"), None), P("dp", "expert"), P("dp", "expert"), P("dp", "expert"))
    body = functools.partial(per_device, mesh.shape["dp"] // 4, mesh.shape["expert"])
    return jax.shard_map(body, mesh=mesh, in_specs=in_specs, out_specs=out_specs, check_vma=False)
```

```python
import functools

import jax
import jax.numpy as jnp
from jax import lax
from jax.experimental import pallas as pl
from jax.experimental.pallas import tpu as pltpu
from jax.sharding import PartitionSpec as P

F32, BF16 = jnp.float32, jnp.bfloat16
MESH = pl.DeviceIdType.MESH


def dot(a, b, dims):
    return lax.dot_general(a, b, (dims, ((), ())), preferred_element_type=F32)


def flip(a, d, count):
    out, bit = 0, 1
    while bit < count:
        mine = lax.rem(lax.div(a, bit), 2)
        turn = (d // bit) % 2 if isinstance(d, int) else lax.rem(lax.div(d, bit), 2)
        out += bit * (mine + turn - 2 * mine * turn)
        bit *= 2
    return out


def each(low, high, body):
    if high - low <= 16:
        for i in range(low, high):
            body(i)
    else:
        lax.fori_loop(low, high, lambda i, carry: (body(i), carry)[1], 0)


def kernel(
    lines, members, cap,
    join, tok, cot, ids, wts, wg, wu, wd,
    mixed, grad_gate, grad_up, grad_down,
    joinv, idv, wtv, tokv, cotv, wfull, blk, recv1, rows_all, part, send2, recv2, all3, send4, recv4,
    local, out, rwy, rwp, r1, rx, r2, r3z, r3y, r3c, r4,
):
    p, j = lax.axis_index("dp"), lax.axis_index("expert")
    line, side, core = lax.div(p, 4), lax.rem(lax.div(p, 2), 2), lax.rem(p, 2)
    quarter = 2 * side + core
    total = lines * members
    flat = line * members + j
    tok_count = tok.shape[0]
    depth, width = wg.shape
    line_depth = 4 * depth

    def device(z, y, c, member):
        return (4 * z + 2 * y + c, member)

    partner = device(line, side, 1 - core, j)
    across = device(line, 1 - side, core, j)

    def copy(src, dst, send, recv, target):
        return pltpu.make_async_remote_copy(
            src_ref=src, dst_ref=dst, send_sem=send, recv_sem=recv, device_id=target, device_id_type=MESH
        )

    def peer(t):
        if isinstance(t, int):
            dz, dj = t // members, t % members
        else:
            dz, dj = lax.div(t, members), lax.rem(t, members)
        return flip(line, dz, lines), flip(j, dj, members)

    def on_line(d):
        z = flip(line, d, lines)
        return z, device(z, side, core, j)

    near = [(0, 1), (1, 0), (1, 1)]

    def beside(n):
        y = 1 - side if near[n][0] else side
        c = 1 - core if near[n][1] else core
        return 2 * y + c, device(line, y, c, j)

    slanted = device(flip(line, 1, lines), 1 - side, core, j)
    barrier = pltpu.get_barrier_semaphore()

    def greet(t):
        z, member = peer(t)
        pl.semaphore_signal(barrier, inc=1, device_id=device(z, side, core, member), device_id_type=MESH)

    each(1, total, greet)
    for there in [beside(n)[1] for n in range(3)] + [slanted]:
        pl.semaphore_signal(barrier, inc=1, device_id=there, device_id_type=MESH)

    loads = [
        pltpu.make_async_copy(src, dst, local.at[n])
        for n, (src, dst) in enumerate(((ids, idv), (wts, wtv), (join, joinv), (tok, tokv), (cot, cotv)))
    ]
    own = [pltpu.make_async_copy(w, wfull.at[n, quarter], local.at[5]) for n, w in enumerate((wg, wu, wd))]
    for load in loads[:3] + own + loads[3:]:
        load.start()
    for load in loads[:2]:
        load.wait()

    chosen = idv[...] == 0
    routed = jnp.max(jnp.where(chosen, 1.0, 0.0), axis=0, keepdims=True)
    weight = jnp.sum(jnp.where(chosen, wtv[...], 0.0), axis=0, keepdims=True)
    upper = lax.broadcasted_iota(jnp.int32, (tok_count, tok_count), 0) <= lax.broadcasted_iota(
        jnp.int32, (tok_count, tok_count), 1
    )
    wide = jnp.broadcast_to(routed, (cap, tok_count))
    places = dot(wide.astype(BF16), jnp.where(upper, 1.0, 0.0).astype(BF16), ((1,), (0,))) - 1.0
    slot = lax.broadcasted_iota(jnp.int32, (cap, tok_count), 0).astype(F32)
    pick = jnp.where((places == slot) & (wide > 0.5), 1.0, 0.0)
    slot_weight = jnp.sum(pick * weight, axis=1, keepdims=True)
    spread = pick.T.astype(BF16)
    pick = pick.astype(BF16)
    loads[2].wait()
    active = 1.0 - joinv[p].astype(F32)
    mine = wfull.at[:, quarter]
    pltpu.make_async_copy(mine, mine, local.at[5]).wait()

    def swap(n):
        return copy(wfull.at[n, quarter], wfull.at[n, quarter], out.at[0], rwy.at[n], across)

    def lend(n):
        return copy(wfull.at[n, quarter], wfull.at[n, quarter], out.at[1], rwp.at[n], partner)

    def relay(n):
        held = wfull.at[n, 2 * (1 - side) + core]
        return copy(held, held, out.at[2], rwp.at[n], partner)

    def give(q, t):
        z, member = peer(t)
        copy(blk.at[q, z], recv1.at[q, flat], out.at[3], r1.at[q], device(z, side, core, member)).start()

    def cut(q, taken):
        for z in range(lines):
            for k in range(4):
                at = z * line_depth + k * depth
                blk[q, z, k] = taken[:, at : at + depth]

    def arrived(ref, recv):
        copy(ref, ref, out.at[0], recv, partner).wait_recv()

    def departed(ref, n):
        copy(ref, ref, out.at[n], rx, partner).wait_send()

    pl.semaphore_wait(barrier, total - 1 + 4)

    swap(0).start()
    loads[3].wait()
    cut(0, dot(pick, tokv[...], ((1,), (0,))).astype(BF16))
    each(1, total, functools.partial(give, 0))
    swap(1).start()
    lend(0).start()
    loads[4].wait()
    cut(1, (dot(pick, cotv[...], ((1,), (0,))) * (slot_weight * active)).astype(BF16))
    swap(2).start()
    each(1, total, functools.partial(give, 1))
    lend(1).start()
    lend(2).start()
    for q in range(2):
        recv1[q, flat] = blk[q, line]

    def product(n, q):
        left = jnp.concatenate([recv1[q, :, k].reshape(total * cap, depth) for k in range(4)], axis=1)
        term = dot(left, wfull[n].reshape(line_depth, width), ((1,), (0,)))
        term = term.reshape(lines, members * cap, width)
        part[n] = term
        send2[n] = term.astype(BF16)
        for d in range(1, lines):
            z, there = on_line(d)
            copy(send2.at[n, z], recv2.at[n, line], out.at[4], r2.at[n], there).start()

    def summed(n):
        arrived(send2.at[n, 1:], r2.at[n])
        total_rows = part[n, line]
        for d in range(1, lines):
            total_rows += recv2[n, on_line(d)[0]].astype(F32)
        return total_rows

    def stage(n, q):
        swap(n).wait_recv()
        relay(n).start()
        if n != 1:
            arrived(recv1.at[q, 1:], r1.at[q])
        arrived(wfull.at[n, 0:2], rwp.at[n])
        product(n, q)

    stage(0, 0)
    stage(1, 0)
    stage(2, 1)

    def share(q, n):
        k, there = beside(n)
        return copy(recv1.at[q, :, k], rows_all.at[q, quarter], out.at[5], rx, there)

    for q in range(2):
        for n in range(3):
            share(q, n).start()
        rows_all[q, quarter] = recv1[q, :, quarter]

    def held(n, z):
        return all3.at[n, quarter, z]

    last = lines - 1
    at_end = (line == 0) | (line == last)
    beside_end = (line == 1) | (line == last - 1)

    def block(n, z, d, sem, there):
        return copy(held(n, z), held(n, z), sem, r3z.at[n, d - 1], there)

    def spread_out(*which):
        for d in [last - 1] + list(range(1, last - 1)):
            for n in which:
                block(n, line, d, out.at[6], on_line(d)[1]).start()
        for n in which:
            pl.when(jnp.logical_not(at_end))(block(n, line, last, out.at[10], on_line(last)[1]).start)
            copy(held(n, line), held(n, line), out.at[7], r3y.at[n], across).start()

    def across_with(n, z, sem, there):
        return copy(held(n, z), held(n, z), sem, r3y.at[n], there)

    def take_in(n, d):
        z, there = on_line(d)
        block(n, z, d, out.at[6], there).wait_recv()
        if d == last - 1:

            @pl.when(beside_end)
            def _():
                block(n, z, last, out.at[11], on_line(1)[1]).start()
                across_with(n, z, out.at[12], slanted).start()

        if d == last:
            pl.when(jnp.logical_not(at_end))(across_with(n, z, out.at[13], across).start)
        else:
            across_with(n, z, out.at[7], across).start()

    def to_partner(n):
        mine = all3.at[n, quarter]
        copy(mine, mine, out.at[8], r3c.at[n], partner).start()

    def from_across(n):
        arrived(all3.at[n, 0], r3y.at[n])
        theirs = all3.at[n, 2 * (1 - side) + core]
        copy(theirs, theirs, out.at[8], r3c.at[n], partner).start()

    def gradient(n, q, result):
        arrived(all3.at[n, 0:2], r3c.at[n])
        left = rows_all[q].reshape(4 * total * cap, depth)
        result[...] = dot(left, all3[n].reshape(4 * total * cap, width), ((0,), (0,))).astype(BF16)

    gate, up = summed(0), summed(1)
    sig = 1.0 / (1.0 + jnp.exp(-gate))
    all3[0, quarter, line] = (gate * sig * up).astype(BF16)
    spread_out(0)
    dhidden = summed(2)
    all3[1, quarter, line] = (dhidden * up * sig * (1.0 + gate * (1.0 - sig))).astype(BF16)
    all3[2, quarter, line] = (dhidden * gate * sig).astype(BF16)
    spread_out(1, 2)

    def rows_out(steps):
        places = [flip(line, d, lines) for d in steps]
        hidden = jnp.concatenate([all3[0, quarter, z] for z in places], axis=0)
        rows = dot(hidden, wfull[2].reshape(line_depth, width), ((1,), (1,))).astype(BF16)
        rows = rows.reshape(len(places), members, cap, line_depth)
        for i, (d, z) in enumerate(zip(steps, places)):
            for m in range(members):
                send4[z * members + m] = rows[i, m]

            def send(dj, d=d, z=z):
                member = flip(j, dj, members)
                there = device(z, side, core, member)
                copy(send4.at[z * members + member], recv4.at[j, line], out.at[9], r4, there).start()

            for dj in range(0 if d else 1, members):
                send(dj)

    for d in range(1, last):
        take_in(0, d)
    for d in range(1, last):
        take_in(1, d)
        take_in(2, d)
    take_in(0, last)
    to_partner(0)
    rows_out(list(range(lines)))
    recv4[j, line] = send4[flat]
    for n in (1, 2):
        take_in(n, last)
        to_partner(n)
    from_across(0)
    from_across(1)
    arrived(rows_all.at[:, 0:3], rx)
    gradient(0, 1, grad_down)
    from_across(2)
    gradient(1, 0, grad_gate)
    arrived(send4.at[1:], r4)
    for z in range(lines):
        out_rows = recv4[0, z].astype(F32)
        for m in range(1, members):
            out_rows += recv4[m, z].astype(F32)
        placed = dot(spread, (out_rows * slot_weight).astype(BF16), ((1,), (0,)))
        mixed[:, z * line_depth : (z + 1) * line_depth] = placed.astype(BF16)
    gradient(2, 0, grad_up)

    for n in range(3):
        departed(wfull.at[:, 0], n)
    departed(recv1.at[:, 1:], 3)
    departed(send2.at[:, 1:], 4)
    departed(rows_all.at[:, 0:3], 5)
    departed(all3.at[:, 0, 1:last], 6)
    pl.when(jnp.logical_not(at_end))(functools.partial(departed, all3.at[:, 0, 0], 10))
    pl.when(jnp.logical_not(at_end))(functools.partial(departed, all3.at[:, 0, 0], 13))
    pl.when(beside_end)(functools.partial(departed, all3.at[:, 0, 0], 11))
    pl.when(beside_end)(functools.partial(departed, all3.at[:, 0, 0], 12))
    departed(all3.at[:, 0, 0:last], 7)
    departed(all3.at[:, 0:2], 8)
    departed(send4.at[1:], 9)


def write_out(*refs):
    sems = refs[-1]
    copies = [pltpu.make_async_copy(refs[n], refs[4 + n], sems.at[n]) for n in range(4)]
    for c in copies:
        c.start()
    for c in copies:
        c.wait()


def per_device(lines, members, tokens, cotangent, expert_ids, route_weights, join_groups, w_gate, w_up, w_down):
    tok_count, model = tokens.shape
    depth, width = w_gate.shape
    cap = tok_count // 8
    total = lines * members
    rows = members * cap
    vmem = pl.BlockSpec(memory_space=pltpu.VMEM)
    hbm = pl.BlockSpec(memory_space=pl.ANY)
    dma = pltpu.SemaphoreType.DMA
    grad = pltpu.VMEM((depth, width), BF16)
    results = pl.pallas_call(
        functools.partial(kernel, lines, members, cap),
        out_shape=(pltpu.VMEM((tok_count, model), BF16), grad, grad, grad),
        in_specs=[hbm] * 8,
        out_specs=(vmem,) * 4,
        scratch_shapes=[
            pltpu.SMEM(join_groups.shape, jnp.int32),
            pltpu.VMEM(expert_ids.shape[::-1], jnp.int32),
            pltpu.VMEM(route_weights.shape[::-1], F32),
            pltpu.VMEM((tok_count, model), BF16),
            pltpu.VMEM((tok_count, model), BF16),
            pltpu.VMEM((3, 4, depth, width), BF16),
            pltpu.VMEM((2, lines, 4, cap, depth), BF16),
            pltpu.VMEM((2, total, 4, cap, depth), BF16),
            pltpu.VMEM((2, 4, total, cap, depth), BF16),
            pltpu.VMEM((3, lines, rows, width), F32),
            pltpu.VMEM((3, lines, rows, width), BF16),
            pltpu.VMEM((3, lines, rows, width), BF16),
            pltpu.VMEM((3, 4, lines, rows, width), BF16),
            pltpu.VMEM((total, cap, 4 * depth), BF16),
            pltpu.VMEM((members, lines, cap, 4 * depth), BF16),
            dma((6,)), dma((14,)),
            dma((3,)), dma((3,)),
            dma((2,)), dma(()),
            dma((3,)),
            dma((3, lines - 1)), dma((3,)), dma((3,)),
            dma(()),
        ],
        compiler_params=pltpu.CompilerParams(
            collective_id=0, has_side_effects=True, vmem_limit_bytes=60 * 1024 * 1024
        ),
        name="expert_step",
    )(join_groups, tokens, cotangent, expert_ids.T, route_weights.T, w_gate, w_up, w_down)
    return pl.pallas_call(
        write_out,
        out_shape=tuple(jax.ShapeDtypeStruct(r.shape, r.dtype) for r in results),
        in_specs=[vmem] * 4,
        out_specs=(hbm,) * 4,
        scratch_shapes=[dma((4,))],
        name="write_out",
    )(*(pltpu.with_memory_space_constraint(r, pltpu.VMEM) for r in results))


def solution(mesh):
    in_specs = (
        P(("dp", "expert"), None),
        P(("dp", "expert"), None),
        P(("dp", "expert"), None),
        P(("dp", "expert"), None),
        P(),
        P("dp", "expert"),
        P("dp", "expert"),
        P("dp", "expert"),
    )
    out_specs = (P(("dp", "expert"), None), P("dp", "expert"), P("dp", "expert"), P("dp", "expert"))
    body = functools.partial(per_device, mesh.shape["dp"] // 4, mesh.shape["expert"])
    return jax.shard_map(body, mesh=mesh, in_specs=in_specs, out_specs=out_specs, check_vma=False)
```

```python
import functools

import jax
import jax.numpy as jnp
from jax import lax
from jax.experimental import pallas as pl
from jax.experimental.pallas import tpu as pltpu
from jax.sharding import PartitionSpec as P

F32, BF16 = jnp.float32, jnp.bfloat16
MESH = pl.DeviceIdType.MESH
RELAYED, SLANTED = (0, 2), (2,)


def dot(a, b, dims):
    return lax.dot_general(a, b, (dims, ((), ())), preferred_element_type=F32)


def flip(a, d, count):
    out, bit = 0, 1
    while bit < count:
        mine = lax.rem(lax.div(a, bit), 2)
        turn = (d // bit) % 2 if isinstance(d, int) else lax.rem(lax.div(d, bit), 2)
        out += bit * (mine + turn - 2 * mine * turn)
        bit *= 2
    return out


def each(low, high, body):
    if high - low <= 16:
        for i in range(low, high):
            body(i)
    else:
        lax.fori_loop(low, high, lambda i, carry: (body(i), carry)[1], 0)


def kernel(
    lines, members, cap,
    join, tok, cot, ids, wts, wg, wu, wd,
    mixed, grad_gate, grad_up, grad_down,
    joinv, idv, wtv, tokv, cotv, wfull, blk, recv1, rows_all, part, send2, recv2, all3, send4, recv4,
    local, out, rwy, rwp, r1, rx, r2, r3z, r3y, r3c, r4,
):
    p, j = lax.axis_index("dp"), lax.axis_index("expert")
    line, side, core = lax.div(p, 4), lax.rem(lax.div(p, 2), 2), lax.rem(p, 2)
    quarter = 2 * side + core
    total = lines * members
    flat = line * members + j
    tok_count = tok.shape[0]
    depth, width = wg.shape
    line_depth = 4 * depth

    def device(z, y, c, member):
        return (4 * z + 2 * y + c, member)

    partner = device(line, side, 1 - core, j)
    across = device(line, 1 - side, core, j)

    def copy(src, dst, send, recv, target):
        return pltpu.make_async_remote_copy(
            src_ref=src, dst_ref=dst, send_sem=send, recv_sem=recv, device_id=target, device_id_type=MESH
        )

    def peer(t):
        if isinstance(t, int):
            dz, dj = t // members, t % members
        else:
            dz, dj = lax.div(t, members), lax.rem(t, members)
        return flip(line, dz, lines), flip(j, dj, members)

    def on_line(d):
        z = flip(line, d, lines)
        return z, device(z, side, core, j)

    near = [(0, 1), (1, 0), (1, 1)]

    def beside(n):
        y = 1 - side if near[n][0] else side
        c = 1 - core if near[n][1] else core
        return 2 * y + c, device(line, y, c, j)

    slanted = device(flip(line, 1, lines), 1 - side, core, j)
    barrier = pltpu.get_barrier_semaphore()

    def greet(t):
        z, member = peer(t)
        pl.semaphore_signal(barrier, inc=1, device_id=device(z, side, core, member), device_id_type=MESH)

    each(1, total, greet)
    for there in [beside(n)[1] for n in range(3)] + [slanted]:
        pl.semaphore_signal(barrier, inc=1, device_id=there, device_id_type=MESH)

    loads = [
        pltpu.make_async_copy(src, dst, local.at[n])
        for n, (src, dst) in enumerate(((ids, idv), (wts, wtv), (join, joinv), (tok, tokv), (cot, cotv)))
    ]
    own = [pltpu.make_async_copy(w, wfull.at[n, quarter], local.at[5]) for n, w in enumerate((wg, wu, wd))]
    for load in loads[:3] + own + loads[3:]:
        load.start()
    for load in loads[:2]:
        load.wait()

    chosen = idv[...] == 0
    routed = jnp.max(jnp.where(chosen, 1.0, 0.0), axis=0, keepdims=True)
    weight = jnp.sum(jnp.where(chosen, wtv[...], 0.0), axis=0, keepdims=True)
    upper = lax.broadcasted_iota(jnp.int32, (tok_count, tok_count), 0) <= lax.broadcasted_iota(
        jnp.int32, (tok_count, tok_count), 1
    )
    wide = jnp.broadcast_to(routed, (cap, tok_count))
    places = dot(wide.astype(BF16), jnp.where(upper, 1.0, 0.0).astype(BF16), ((1,), (0,))) - 1.0
    slot = lax.broadcasted_iota(jnp.int32, (cap, tok_count), 0).astype(F32)
    pick = jnp.where((places == slot) & (wide > 0.5), 1.0, 0.0)
    slot_weight = jnp.sum(pick * weight, axis=1, keepdims=True)
    spread = pick.T.astype(BF16)
    pick = pick.astype(BF16)
    loads[2].wait()
    active = 1.0 - joinv[p].astype(F32)
    mine = wfull.at[:, quarter]
    pltpu.make_async_copy(mine, mine, local.at[5]).wait()

    def swap(n):
        return copy(wfull.at[n, quarter], wfull.at[n, quarter], out.at[0], rwy.at[n], across)

    def lend(n):
        return copy(wfull.at[n, quarter], wfull.at[n, quarter], out.at[1], rwp.at[n], partner)

    def relay(n):
        held = wfull.at[n, 2 * (1 - side) + core]
        return copy(held, held, out.at[2], rwp.at[n], partner)

    def give(q, t):
        z, member = peer(t)
        copy(blk.at[q, z], recv1.at[q, flat], out.at[3], r1.at[q], device(z, side, core, member)).start()

    def cut(q, taken):
        for z in range(lines):
            for k in range(4):
                at = z * line_depth + k * depth
                blk[q, z, k] = taken[:, at : at + depth]

    def arrived(ref, recv):
        copy(ref, ref, out.at[0], recv, partner).wait_recv()

    def departed(ref, n):
        copy(ref, ref, out.at[n], rx, partner).wait_send()

    pl.semaphore_wait(barrier, total - 1 + 4)

    swap(0).start()
    loads[3].wait()
    cut(0, dot(pick, tokv[...], ((1,), (0,))).astype(BF16))
    each(1, total, functools.partial(give, 0))
    swap(1).start()
    lend(0).start()
    loads[4].wait()
    cut(1, (dot(pick, cotv[...], ((1,), (0,))) * (slot_weight * active)).astype(BF16))
    swap(2).start()
    each(1, total, functools.partial(give, 1))
    lend(1).start()
    lend(2).start()
    for q in range(2):
        recv1[q, flat] = blk[q, line]

    def product(n, q):
        left = jnp.concatenate([recv1[q, :, k].reshape(total * cap, depth) for k in range(4)], axis=1)
        term = dot(left, wfull[n].reshape(line_depth, width), ((1,), (0,)))
        term = term.reshape(lines, members * cap, width)
        part[n] = term
        send2[n] = term.astype(BF16)
        for d in range(1, lines):
            z, there = on_line(d)
            copy(send2.at[n, z], recv2.at[n, line], out.at[4], r2.at[n], there).start()

    def summed(n):
        arrived(send2.at[n, 1:], r2.at[n])
        total_rows = part[n, line]
        for d in range(1, lines):
            total_rows += recv2[n, on_line(d)[0]].astype(F32)
        return total_rows

    def stage(n, q):
        swap(n).wait_recv()
        relay(n).start()
        if n != 1:
            arrived(recv1.at[q, 1:], r1.at[q])
        arrived(wfull.at[n, 0:2], rwp.at[n])
        product(n, q)

    stage(0, 0)
    stage(1, 0)
    stage(2, 1)

    def share(q, n):
        k, there = beside(n)
        return copy(recv1.at[q, :, k], rows_all.at[q, quarter], out.at[5], rx, there)

    for q in range(2):
        for n in range(3):
            share(q, n).start()
        rows_all[q, quarter] = recv1[q, :, quarter]

    def held(n, z):
        return all3.at[n, quarter, z]

    last = lines - 1
    at_end = (line == 0) | (line == last)
    beside_end = (line == 1) | (line == last - 1)

    def block(n, z, d, sem, there):
        return copy(held(n, z), held(n, z), sem, r3z.at[n, d - 1], there)

    def spread_out(*which):
        for d in [last - 1] + list(range(1, last - 1)):
            for n in which:
                block(n, line, d, out.at[6], on_line(d)[1]).start()
        for n in which:
            if n in RELAYED:
                pl.when(jnp.logical_not(at_end))(block(n, line, last, out.at[10], on_line(last)[1]).start)
            else:
                block(n, line, last, out.at[14], on_line(last)[1]).start()
            copy(held(n, line), held(n, line), out.at[7], r3y.at[n], across).start()

    def across_with(n, z, sem, there):
        return copy(held(n, z), held(n, z), sem, r3y.at[n], there)

    def take_in(n, d):
        z, there = on_line(d)
        block(n, z, d, out.at[6], there).wait_recv()
        if d == last - 1 and n in RELAYED:
            pl.when(beside_end)(block(n, z, last, out.at[11], on_line(1)[1]).start)
            if n in SLANTED:
                pl.when(beside_end)(across_with(n, z, out.at[12], slanted).start)
        if d == last and n in SLANTED:
            pl.when(jnp.logical_not(at_end))(across_with(n, z, out.at[13], across).start)
        else:
            across_with(n, z, out.at[7 if d < last else 15], across).start()

    def to_partner(n):
        mine = all3.at[n, quarter]
        copy(mine, mine, out.at[8], r3c.at[n], partner).start()

    def from_across(n):
        arrived(all3.at[n, 0], r3y.at[n])
        theirs = all3.at[n, 2 * (1 - side) + core]
        copy(theirs, theirs, out.at[8], r3c.at[n], partner).start()

    def gradient(n, q, result):
        arrived(all3.at[n, 0:2], r3c.at[n])
        left = rows_all[q].reshape(4 * total * cap, depth)
        result[...] = dot(left, all3[n].reshape(4 * total * cap, width), ((0,), (0,))).astype(BF16)

    gate, up = summed(0), summed(1)
    sig = 1.0 / (1.0 + jnp.exp(-gate))
    all3[0, quarter, line] = (gate * sig * up).astype(BF16)
    spread_out(0)
    dhidden = summed(2)
    all3[1, quarter, line] = (dhidden * up * sig * (1.0 + gate * (1.0 - sig))).astype(BF16)
    all3[2, quarter, line] = (dhidden * gate * sig).astype(BF16)
    spread_out(1, 2)

    def rows_out(steps):
        places = [flip(line, d, lines) for d in steps]
        hidden = jnp.concatenate([all3[0, quarter, z] for z in places], axis=0)
        rows = dot(hidden, wfull[2].reshape(line_depth, width), ((1,), (1,))).astype(BF16)
        rows = rows.reshape(len(places), members, cap, line_depth)
        for i, (d, z) in enumerate(zip(steps, places)):
            for m in range(members):
                send4[z * members + m] = rows[i, m]

            def send(dj, d=d, z=z):
                member = flip(j, dj, members)
                there = device(z, side, core, member)
                copy(send4.at[z * members + member], recv4.at[j, line], out.at[9], r4, there).start()

            for dj in range(0 if d else 1, members):
                send(dj)

    for d in range(1, last):
        take_in(0, d)
    for d in range(1, last):
        take_in(1, d)
        take_in(2, d)
    take_in(0, last)
    to_partner(0)
    rows_out(list(range(lines)))
    recv4[j, line] = send4[flat]
    for n in (1, 2):
        take_in(n, last)
        to_partner(n)
    from_across(0)
    from_across(1)
    arrived(rows_all.at[:, 0:3], rx)
    gradient(0, 1, grad_down)
    from_across(2)
    gradient(1, 0, grad_gate)
    arrived(send4.at[1:], r4)
    for z in range(lines):
        out_rows = recv4[0, z].astype(F32)
        for m in range(1, members):
            out_rows += recv4[m, z].astype(F32)
        placed = dot(spread, (out_rows * slot_weight).astype(BF16), ((1,), (0,)))
        mixed[:, z * line_depth : (z + 1) * line_depth] = placed.astype(BF16)
    gradient(2, 0, grad_up)

    for n in range(3):
        departed(wfull.at[:, 0], n)
    departed(recv1.at[:, 1:], 3)
    departed(send2.at[:, 1:], 4)
    departed(rows_all.at[:, 0:3], 5)
    departed(all3.at[:, 0, 1:last], 6)
    inner = jnp.logical_not(at_end)
    for n, count, who in (
        (10, len(RELAYED), inner), (11, len(RELAYED), beside_end), (12, len(SLANTED), beside_end),
        (13, len(SLANTED), inner), (14, 3 - len(RELAYED), None), (15, 3 - len(SLANTED), None),
    ):
        if count:
            finish = functools.partial(departed, all3.at[0:count, 0, 0], n)
            finish() if who is None else pl.when(who)(finish)
    departed(all3.at[:, 0, 0:last], 7)
    departed(all3.at[:, 0:2], 8)
    departed(send4.at[1:], 9)


def write_out(*refs):
    sems = refs[-1]
    copies = [pltpu.make_async_copy(refs[n], refs[4 + n], sems.at[n]) for n in range(4)]
    for c in copies:
        c.start()
    for c in copies:
        c.wait()


def per_device(lines, members, tokens, cotangent, expert_ids, route_weights, join_groups, w_gate, w_up, w_down):
    tok_count, model = tokens.shape
    depth, width = w_gate.shape
    cap = tok_count // 8
    total = lines * members
    rows = members * cap
    vmem = pl.BlockSpec(memory_space=pltpu.VMEM)
    hbm = pl.BlockSpec(memory_space=pl.ANY)
    dma = pltpu.SemaphoreType.DMA
    grad = pltpu.VMEM((depth, width), BF16)
    results = pl.pallas_call(
        functools.partial(kernel, lines, members, cap),
        out_shape=(pltpu.VMEM((tok_count, model), BF16), grad, grad, grad),
        in_specs=[hbm] * 8,
        out_specs=(vmem,) * 4,
        scratch_shapes=[
            pltpu.SMEM(join_groups.shape, jnp.int32),
            pltpu.VMEM(expert_ids.shape[::-1], jnp.int32),
            pltpu.VMEM(route_weights.shape[::-1], F32),
            pltpu.VMEM((tok_count, model), BF16),
            pltpu.VMEM((tok_count, model), BF16),
            pltpu.VMEM((3, 4, depth, width), BF16),
            pltpu.VMEM((2, lines, 4, cap, depth), BF16),
            pltpu.VMEM((2, total, 4, cap, depth), BF16),
            pltpu.VMEM((2, 4, total, cap, depth), BF16),
            pltpu.VMEM((3, lines, rows, width), F32),
            pltpu.VMEM((3, lines, rows, width), BF16),
            pltpu.VMEM((3, lines, rows, width), BF16),
            pltpu.VMEM((3, 4, lines, rows, width), BF16),
            pltpu.VMEM((total, cap, 4 * depth), BF16),
            pltpu.VMEM((members, lines, cap, 4 * depth), BF16),
            dma((6,)), dma((16,)),
            dma((3,)), dma((3,)),
            dma((2,)), dma(()),
            dma((3,)),
            dma((3, lines - 1)), dma((3,)), dma((3,)),
            dma(()),
        ],
        compiler_params=pltpu.CompilerParams(
            collective_id=0, has_side_effects=True, vmem_limit_bytes=60 * 1024 * 1024
        ),
        name="expert_step",
    )(join_groups, tokens, cotangent, expert_ids.T, route_weights.T, w_gate, w_up, w_down)
    return pl.pallas_call(
        write_out,
        out_shape=tuple(jax.ShapeDtypeStruct(r.shape, r.dtype) for r in results),
        in_specs=[vmem] * 4,
        out_specs=(hbm,) * 4,
        scratch_shapes=[dma((4,))],
        name="write_out",
    )(*(pltpu.with_memory_space_constraint(r, pltpu.VMEM) for r in results))


def solution(mesh):
    in_specs = (
        P(("dp", "expert"), None),
        P(("dp", "expert"), None),
        P(("dp", "expert"), None),
        P(("dp", "expert"), None),
        P(),
        P("dp", "expert"),
        P("dp", "expert"),
        P("dp", "expert"),
    )
    out_specs = (P(("dp", "expert"), None), P("dp", "expert"), P("dp", "expert"), P("dp", "expert"))
    body = functools.partial(per_device, mesh.shape["dp"] // 4, mesh.shape["expert"])
    return jax.shard_map(body, mesh=mesh, in_specs=in_specs, out_specs=out_specs, check_vma=False)
```

```python
import functools

import jax
import jax.numpy as jnp
from jax import lax
from jax.experimental import pallas as pl
from jax.experimental.pallas import tpu as pltpu
from jax.sharding import PartitionSpec as P

F32, BF16 = jnp.float32, jnp.bfloat16
MESH = pl.DeviceIdType.MESH


def dot(a, b, dims):
    return lax.dot_general(a, b, (dims, ((), ())), preferred_element_type=F32)


def flip(a, d, count):
    out, bit = 0, 1
    while bit < count:
        mine = lax.rem(lax.div(a, bit), 2)
        turn = (d // bit) % 2 if isinstance(d, int) else lax.rem(lax.div(d, bit), 2)
        out += bit * (mine + turn - 2 * mine * turn)
        bit *= 2
    return out


def each(low, high, body):
    if high - low <= 16:
        for i in range(low, high):
            body(i)
    else:
        lax.fori_loop(low, high, lambda i, carry: (body(i), carry)[1], 0)


def kernel(
    lines, members, cap,
    join, tok, cot, ids, wts, wg, wu, wd,
    mixed, grad_gate, grad_up, grad_down,
    joinv, idv, wtv, tokv, cotv, wfull, blk, recv1, rows_all, part, send2, recv2, all3, send4, recv4,
    local, out, rwy, rwp, r1, rx, r2, r3z, r3y, r3c, r4,
):
    p, j = lax.axis_index("dp"), lax.axis_index("expert")
    line, side, core = lax.div(p, 4), lax.rem(lax.div(p, 2), 2), lax.rem(p, 2)
    quarter = 2 * side + core
    total = lines * members
    flat = line * members + j
    tok_count = tok.shape[0]
    depth, width = wg.shape
    line_depth = 4 * depth

    def device(z, y, c, member):
        return (4 * z + 2 * y + c, member)

    partner = device(line, side, 1 - core, j)
    across = device(line, 1 - side, core, j)

    def copy(src, dst, send, recv, target):
        return pltpu.make_async_remote_copy(
            src_ref=src, dst_ref=dst, send_sem=send, recv_sem=recv, device_id=target, device_id_type=MESH
        )

    def peer(t):
        if isinstance(t, int):
            dz, dj = t // members, t % members
        else:
            dz, dj = lax.div(t, members), lax.rem(t, members)
        return flip(line, dz, lines), flip(j, dj, members)

    def on_line(d):
        z = flip(line, d, lines)
        return z, device(z, side, core, j)

    near = [(0, 1), (1, 0), (1, 1)]

    def beside(n):
        y = 1 - side if near[n][0] else side
        c = 1 - core if near[n][1] else core
        return 2 * y + c, device(line, y, c, j)

    barrier = pltpu.get_barrier_semaphore()

    def greet(t):
        z, member = peer(t)
        pl.semaphore_signal(barrier, inc=1, device_id=device(z, side, core, member), device_id_type=MESH)

    each(1, total, greet)
    for there in [beside(n)[1] for n in range(3)]:
        pl.semaphore_signal(barrier, inc=1, device_id=there, device_id_type=MESH)

    loads = [
        pltpu.make_async_copy(src, dst, local.at[n])
        for n, (src, dst) in enumerate(((ids, idv), (wts, wtv), (join, joinv), (tok, tokv), (cot, cotv)))
    ]
    own = [pltpu.make_async_copy(w, wfull.at[n, quarter], local.at[5]) for n, w in enumerate((wg, wu, wd))]
    for load in loads[:3] + own + loads[3:]:
        load.start()
    for load in loads[:2]:
        load.wait()

    chosen = idv[...] == 0
    routed = jnp.max(jnp.where(chosen, 1.0, 0.0), axis=0, keepdims=True)
    weight = jnp.sum(jnp.where(chosen, wtv[...], 0.0), axis=0, keepdims=True)
    upper = lax.broadcasted_iota(jnp.int32, (tok_count, tok_count), 0) <= lax.broadcasted_iota(
        jnp.int32, (tok_count, tok_count), 1
    )
    wide = jnp.broadcast_to(routed, (cap, tok_count))
    places = dot(wide.astype(BF16), jnp.where(upper, 1.0, 0.0).astype(BF16), ((1,), (0,))) - 1.0
    slot = lax.broadcasted_iota(jnp.int32, (cap, tok_count), 0).astype(F32)
    pick = jnp.where((places == slot) & (wide > 0.5), 1.0, 0.0)
    slot_weight = jnp.sum(pick * weight, axis=1, keepdims=True)
    spread = pick.T.astype(BF16)
    pick = pick.astype(BF16)
    loads[2].wait()
    active = 1.0 - joinv[p].astype(F32)
    mine = wfull.at[:, quarter]
    pltpu.make_async_copy(mine, mine, local.at[5]).wait()

    def swap(n):
        return copy(wfull.at[n, quarter], wfull.at[n, quarter], out.at[0], rwy.at[n], across)

    def lend(n):
        return copy(wfull.at[n, quarter], wfull.at[n, quarter], out.at[1], rwp.at[n], partner)

    def relay(n):
        held = wfull.at[n, 2 * (1 - side) + core]
        return copy(held, held, out.at[2], rwp.at[n], partner)

    def give(q, t):
        z, member = peer(t)
        copy(blk.at[q, z], recv1.at[q, flat], out.at[3], r1.at[q], device(z, side, core, member)).start()

    def cut(q, taken):
        for z in range(lines):
            for k in range(4):
                at = z * line_depth + k * depth
                blk[q, z, k] = taken[:, at : at + depth]

    def arrived(ref, recv):
        copy(ref, ref, out.at[0], recv, partner).wait_recv()

    def departed(ref, n):
        copy(ref, ref, out.at[n], rx, partner).wait_send()

    pl.semaphore_wait(barrier, total - 1 + 3)

    swap(0).start()
    loads[3].wait()
    cut(0, dot(pick, tokv[...], ((1,), (0,))).astype(BF16))
    each(1, total, functools.partial(give, 0))
    swap(1).start()
    lend(0).start()
    loads[4].wait()
    cut(1, (dot(pick, cotv[...], ((1,), (0,))) * (slot_weight * active)).astype(BF16))
    swap(2).start()
    each(1, total, functools.partial(give, 1))
    lend(1).start()
    lend(2).start()
    for q in range(2):
        recv1[q, flat] = blk[q, line]

    def product(n, q):
        left = jnp.concatenate([recv1[q, :, k].reshape(total * cap, depth) for k in range(4)], axis=1)
        term = dot(left, wfull[n].reshape(line_depth, width), ((1,), (0,)))
        term = term.reshape(lines, members * cap, width)
        part[n] = term
        send2[n] = term.astype(BF16)
        for d in range(1, lines):
            z, there = on_line(d)
            copy(send2.at[n, z], recv2.at[n, line], out.at[4], r2.at[n], there).start()

    def summed(n):
        arrived(send2.at[n, 1:], r2.at[n])
        total_rows = part[n, line]
        for d in range(1, lines):
            total_rows += recv2[n, on_line(d)[0]].astype(F32)
        return total_rows

    def stage(n, q):
        swap(n).wait_recv()
        relay(n).start()
        if n != 1:
            arrived(recv1.at[q, 1:], r1.at[q])
        arrived(wfull.at[n, 0:2], rwp.at[n])
        product(n, q)

    stage(0, 0)
    stage(1, 0)
    stage(2, 1)

    def share(q, n):
        k, there = beside(n)
        return copy(recv1.at[q, :, k], rows_all.at[q, quarter], out.at[5], rx, there)

    for q in range(2):
        for n in range(3):
            share(q, n).start()
        rows_all[q, quarter] = recv1[q, :, quarter]

    def held(n, z):
        return all3.at[n, quarter, z]

    last = lines - 1
    at_end = (line == 0) | (line == last)
    inner = jnp.logical_not(at_end)
    beside_end = (line == 1) | (line == last - 1)

    def block(n, z, d, sem, there):
        return copy(held(n, z), held(n, z), sem, r3z.at[n, d - 1], there)

    def spread_out(*which):
        for d in [last - 1] + list(range(1, last - 1)):
            for n in which:
                block(n, line, d, out.at[6], on_line(d)[1]).start()
        for n in which:
            pl.when(inner)(block(n, line, last, out.at[10], on_line(last)[1]).start)
            copy(held(n, line), held(n, line), out.at[7], r3y.at[n], across).start()

    def take_in(n, d):
        z, there = on_line(d)
        block(n, z, d, out.at[6], there).wait_recv()
        if d == last - 1:
            pl.when(beside_end)(block(n, z, last, out.at[11], on_line(1)[1]).start)
        copy(held(n, z), held(n, z), out.at[7], r3y.at[n], across).start()

    def to_partner(n):
        mine = all3.at[n, quarter]
        copy(mine, mine, out.at[8], r3c.at[n], partner).start()

    def from_across(n):
        arrived(all3.at[n, 0], r3y.at[n])
        theirs = all3.at[n, 2 * (1 - side) + core]
        copy(theirs, theirs, out.at[8], r3c.at[n], partner).start()

    def gradient(n, q, result):
        arrived(all3.at[n, 0:2], r3c.at[n])
        left = rows_all[q].reshape(4 * total * cap, depth)
        result[...] = dot(left, all3[n].reshape(4 * total * cap, width), ((0,), (0,))).astype(BF16)

    gate, up = summed(0), summed(1)
    sig = 1.0 / (1.0 + jnp.exp(-gate))
    all3[0, quarter, line] = (gate * sig * up).astype(BF16)
    spread_out(0)
    dhidden = summed(2)
    all3[1, quarter, line] = (dhidden * up * sig * (1.0 + gate * (1.0 - sig))).astype(BF16)
    all3[2, quarter, line] = (dhidden * gate * sig).astype(BF16)
    spread_out(1, 2)

    def finish(n):
        take_in(n, last)
        to_partner(n)

    def output_rows():
        places = [flip(line, d, lines) for d in range(lines)]
        hidden = jnp.concatenate([all3[0, quarter, z] for z in places], axis=0)
        rows = dot(hidden, wfull[2].reshape(line_depth, width), ((1,), (1,))).astype(BF16)
        rows = rows.reshape(lines, members, cap, line_depth)
        for i, z in enumerate(places):
            for m in range(members):
                send4[z * members + m] = rows[i, m]
            for dj in range(0 if i else 1, members):
                member = flip(j, dj, members)
                there = device(z, side, core, member)
                copy(send4.at[z * members + member], recv4.at[j, line], out.at[9], r4, there).start()
        recv4[j, line] = send4[flat]

    far = last - 1

    @pl.when(at_end)
    def _():
        for d in range(1, far + 1):
            take_in(0, d)
        for d in range(1, far):
            take_in(1, d)
            take_in(2, d)
        finish(0)
        output_rows()
        take_in(1, far)
        take_in(2, far)
        finish(1)
        finish(2)

    @pl.when(inner)
    def _():
        for d in range(1, last):
            take_in(0, d)
        finish(0)
        for d in range(1, last):
            take_in(1, d)
            take_in(2, d)
        output_rows()
        finish(1)
        finish(2)

    from_across(0)
    from_across(1)
    arrived(rows_all.at[:, 0:3], rx)
    gradient(0, 1, grad_down)
    from_across(2)
    gradient(1, 0, grad_gate)
    arrived(send4.at[1:], r4)
    for z in range(lines):
        out_rows = recv4[0, z].astype(F32)
        for m in range(1, members):
            out_rows += recv4[m, z].astype(F32)
        placed = dot(spread, (out_rows * slot_weight).astype(BF16), ((1,), (0,)))
        mixed[:, z * line_depth : (z + 1) * line_depth] = placed.astype(BF16)
    gradient(2, 0, grad_up)

    for n in range(3):
        departed(wfull.at[:, 0], n)
    departed(recv1.at[:, 1:], 3)
    departed(send2.at[:, 1:], 4)
    departed(rows_all.at[:, 0:3], 5)
    departed(all3.at[:, 0, 1:last], 6)
    pl.when(inner)(functools.partial(departed, all3.at[:, 0, 0], 10))
    pl.when(beside_end)(functools.partial(departed, all3.at[:, 0, 0], 11))
    departed(all3.at[:, 0], 7)
    departed(all3.at[:, 0:2], 8)
    departed(send4.at[1:], 9)


def write_out(*refs):
    sems = refs[-1]
    copies = [pltpu.make_async_copy(refs[n], refs[4 + n], sems.at[n]) for n in range(4)]
    for c in copies:
        c.start()
    for c in copies:
        c.wait()


def per_device(lines, members, tokens, cotangent, expert_ids, route_weights, join_groups, w_gate, w_up, w_down):
    tok_count, model = tokens.shape
    depth, width = w_gate.shape
    cap = tok_count // 8
    total = lines * members
    rows = members * cap
    vmem = pl.BlockSpec(memory_space=pltpu.VMEM)
    hbm = pl.BlockSpec(memory_space=pl.ANY)
    dma = pltpu.SemaphoreType.DMA
    grad = pltpu.VMEM((depth, width), BF16)
    results = pl.pallas_call(
        functools.partial(kernel, lines, members, cap),
        out_shape=(pltpu.VMEM((tok_count, model), BF16), grad, grad, grad),
        in_specs=[hbm] * 8,
        out_specs=(vmem,) * 4,
        scratch_shapes=[
            pltpu.SMEM(join_groups.shape, jnp.int32),
            pltpu.VMEM(expert_ids.shape[::-1], jnp.int32),
            pltpu.VMEM(route_weights.shape[::-1], F32),
            pltpu.VMEM((tok_count, model), BF16),
            pltpu.VMEM((tok_count, model), BF16),
            pltpu.VMEM((3, 4, depth, width), BF16),
            pltpu.VMEM((2, lines, 4, cap, depth), BF16),
            pltpu.VMEM((2, total, 4, cap, depth), BF16),
            pltpu.VMEM((2, 4, total, cap, depth), BF16),
            pltpu.VMEM((3, lines, rows, width), F32),
            pltpu.VMEM((3, lines, rows, width), BF16),
            pltpu.VMEM((3, lines, rows, width), BF16),
            pltpu.VMEM((3, 4, lines, rows, width), BF16),
            pltpu.VMEM((total, cap, 4 * depth), BF16),
            pltpu.VMEM((members, lines, cap, 4 * depth), BF16),
            dma((6,)), dma((12,)),
            dma((3,)), dma((3,)),
            dma((2,)), dma(()),
            dma((3,)),
            dma((3, lines - 1)), dma((3,)), dma((3,)),
            dma(()),
        ],
        compiler_params=pltpu.CompilerParams(
            collective_id=0, has_side_effects=True, vmem_limit_bytes=60 * 1024 * 1024
        ),
        name="expert_step",
    )(join_groups, tokens, cotangent, expert_ids.T, route_weights.T, w_gate, w_up, w_down)
    return pl.pallas_call(
        write_out,
        out_shape=tuple(jax.ShapeDtypeStruct(r.shape, r.dtype) for r in results),
        in_specs=[vmem] * 4,
        out_specs=(hbm,) * 4,
        scratch_shapes=[dma((4,))],
        name="write_out",
    )(*(pltpu.with_memory_space_constraint(r, pltpu.VMEM) for r in results))


def solution(mesh):
    in_specs = (
        P(("dp", "expert"), None),
        P(("dp", "expert"), None),
        P(("dp", "expert"), None),
        P(("dp", "expert"), None),
        P(),
        P("dp", "expert"),
        P("dp", "expert"),
        P("dp", "expert"),
    )
    out_specs = (P(("dp", "expert"), None), P("dp", "expert"), P("dp", "expert"), P("dp", "expert"))
    body = functools.partial(per_device, mesh.shape["dp"] // 4, mesh.shape["expert"])
    return jax.shard_map(body, mesh=mesh, in_specs=in_specs, out_specs=out_specs, check_vma=False)
```

```python
import functools

import jax
import jax.numpy as jnp
from jax import lax
from jax.experimental import pallas as pl
from jax.experimental.pallas import tpu as pltpu
from jax.sharding import PartitionSpec as P

F32, BF16 = jnp.float32, jnp.bfloat16
MESH = pl.DeviceIdType.MESH
SPLIT = (1, 1, 2)


def dot(a, b, dims):
    return lax.dot_general(a, b, (dims, ((), ())), preferred_element_type=F32)


def flip(a, d, count):
    out, bit = 0, 1
    while bit < count:
        mine = lax.rem(lax.div(a, bit), 2)
        turn = (d // bit) % 2 if isinstance(d, int) else lax.rem(lax.div(d, bit), 2)
        out += bit * (mine + turn - 2 * mine * turn)
        bit *= 2
    return out


def each(low, high, body):
    if high - low <= 16:
        for i in range(low, high):
            body(i)
    else:
        lax.fori_loop(low, high, lambda i, carry: (body(i), carry)[1], 0)


def kernel(
    lines, members, cap,
    join, tok, cot, ids, wts, wg, wu, wd,
    mixed, grad_gate, grad_up, grad_down,
    joinv, idv, wtv, tokv, cotv, wfull, blk, recv1, rows_all, part, send2, recv2, all3, half_sum, send4, recv4,
    local, out, rwy, rwp, r1, rx, r2, r3z, r3y, r3c, r4,
):
    p, j = lax.axis_index("dp"), lax.axis_index("expert")
    line, side, core = lax.div(p, 4), lax.rem(lax.div(p, 2), 2), lax.rem(p, 2)
    quarter = 2 * side + core
    total = lines * members
    flat = line * members + j
    tok_count = tok.shape[0]
    depth, width = wg.shape
    line_depth = 4 * depth

    def device(z, y, c, member):
        return (4 * z + 2 * y + c, member)

    partner = device(line, side, 1 - core, j)
    across = device(line, 1 - side, core, j)

    def copy(src, dst, send, recv, target):
        return pltpu.make_async_remote_copy(
            src_ref=src, dst_ref=dst, send_sem=send, recv_sem=recv, device_id=target, device_id_type=MESH
        )

    def peer(t):
        if isinstance(t, int):
            dz, dj = t // members, t % members
        else:
            dz, dj = lax.div(t, members), lax.rem(t, members)
        return flip(line, dz, lines), flip(j, dj, members)

    def on_line(d):
        z = flip(line, d, lines)
        return z, device(z, side, core, j)

    near = [(0, 1), (1, 0), (1, 1)]

    def beside(n):
        y = 1 - side if near[n][0] else side
        c = 1 - core if near[n][1] else core
        return 2 * y + c, device(line, y, c, j)

    barrier = pltpu.get_barrier_semaphore()

    def greet(t):
        z, member = peer(t)
        pl.semaphore_signal(barrier, inc=1, device_id=device(z, side, core, member), device_id_type=MESH)

    each(1, total, greet)
    for there in [beside(n)[1] for n in range(3)]:
        pl.semaphore_signal(barrier, inc=1, device_id=there, device_id_type=MESH)

    loads = [
        pltpu.make_async_copy(src, dst, local.at[n])
        for n, (src, dst) in enumerate(((ids, idv), (wts, wtv), (join, joinv), (tok, tokv), (cot, cotv)))
    ]
    own = [pltpu.make_async_copy(w, wfull.at[n, quarter], local.at[5]) for n, w in enumerate((wg, wu, wd))]
    for load in loads[:3] + own + loads[3:]:
        load.start()
    for load in loads[:2]:
        load.wait()

    chosen = idv[...] == 0
    routed = jnp.max(jnp.where(chosen, 1.0, 0.0), axis=0, keepdims=True)
    weight = jnp.sum(jnp.where(chosen, wtv[...], 0.0), axis=0, keepdims=True)
    upper = lax.broadcasted_iota(jnp.int32, (tok_count, tok_count), 0) <= lax.broadcasted_iota(
        jnp.int32, (tok_count, tok_count), 1
    )
    wide = jnp.broadcast_to(routed, (cap, tok_count))
    places = dot(wide.astype(BF16), jnp.where(upper, 1.0, 0.0).astype(BF16), ((1,), (0,))) - 1.0
    slot = lax.broadcasted_iota(jnp.int32, (cap, tok_count), 0).astype(F32)
    pick = jnp.where((places == slot) & (wide > 0.5), 1.0, 0.0)
    slot_weight = jnp.sum(pick * weight, axis=1, keepdims=True)
    spread = pick.T.astype(BF16)
    pick = pick.astype(BF16)
    loads[2].wait()
    active = 1.0 - joinv[p].astype(F32)
    mine = wfull.at[:, quarter]
    pltpu.make_async_copy(mine, mine, local.at[5]).wait()

    def swap(n):
        return copy(wfull.at[n, quarter], wfull.at[n, quarter], out.at[0], rwy.at[n], across)

    def lend(n):
        return copy(wfull.at[n, quarter], wfull.at[n, quarter], out.at[1], rwp.at[n], partner)

    def relay(n):
        held = wfull.at[n, 2 * (1 - side) + core]
        return copy(held, held, out.at[2], rwp.at[n], partner)

    def give(q, t):
        z, member = peer(t)
        copy(blk.at[q, z], recv1.at[q, flat], out.at[3], r1.at[q], device(z, side, core, member)).start()

    def cut(q, taken):
        for z in range(lines):
            for k in range(4):
                at = z * line_depth + k * depth
                blk[q, z, k] = taken[:, at : at + depth]

    def arrived(ref, recv):
        copy(ref, ref, out.at[0], recv, partner).wait_recv()

    def departed(ref, n):
        copy(ref, ref, out.at[n], rx, partner).wait_send()

    pl.semaphore_wait(barrier, total - 1 + 3)

    swap(0).start()
    loads[3].wait()
    cut(0, dot(pick, tokv[...], ((1,), (0,))).astype(BF16))
    each(1, total, functools.partial(give, 0))
    swap(1).start()
    lend(0).start()
    loads[4].wait()
    cut(1, (dot(pick, cotv[...], ((1,), (0,))) * (slot_weight * active)).astype(BF16))
    swap(2).start()
    each(1, total, functools.partial(give, 1))
    lend(1).start()
    lend(2).start()
    for q in range(2):
        recv1[q, flat] = blk[q, line]

    def product(n, q):
        left = jnp.concatenate([recv1[q, :, k].reshape(total * cap, depth) for k in range(4)], axis=1)
        term = dot(left, wfull[n].reshape(line_depth, width), ((1,), (0,)))
        term = term.reshape(lines, members * cap, width)
        part[n] = term
        send2[n] = term.astype(BF16)
        for e in range(SPLIT[n]):
            span = band(n, e)
            for d in range(1, lines):
                z, there = on_line(d)
                recv = r2.at[n + e]
                copy(send2.at[n, z, span], recv2.at[n, line, span], out.at[4], recv, there).start()

    def band(n, e):
        height = members * cap // SPLIT[n]
        return slice(e * height, (e + 1) * height)

    def summed(n, e=0):
        span = band(n, e)
        arrived(send2.at[n, 1:, span], r2.at[n + e])
        total_rows = part[n, line, span]
        for d in range(1, lines):
            total_rows += recv2[n, on_line(d)[0], span].astype(F32)
        return total_rows

    def stage(n, q):
        swap(n).wait_recv()
        relay(n).start()
        if n != 1:
            arrived(recv1.at[q, 1:], r1.at[q])
        arrived(wfull.at[n, 0:2], rwp.at[n])
        product(n, q)

    stage(0, 0)
    stage(1, 0)
    stage(2, 1)

    def share(q, n):
        k, there = beside(n)
        return copy(recv1.at[q, :, k], rows_all.at[q, quarter], out.at[5], rx, there)

    for q in range(2):
        for n in range(3):
            share(q, n).start()
        rows_all[q, quarter] = recv1[q, :, quarter]

    def unit(n, *place):
        return all3.at[(0, *place)] if n == 0 else all3.at[(slice(1, 3), *place, band(2, n - 1))]

    def held(n, z):
        return unit(n, quarter, z)

    last = lines - 1
    at_end = (line == 0) | (line == last)
    inner = jnp.logical_not(at_end)
    beside_end = (line == 1) | (line == last - 1)

    def block(n, z, d, sem, there):
        return copy(held(n, z), held(n, z), sem, r3z.at[n, d - 1], there)

    def spread_out(*which):
        for d in [last - 1] + list(range(1, last - 1)):
            for n in which:
                block(n, line, d, out.at[6], on_line(d)[1]).start()
        for n in which:
            pl.when(inner)(block(n, line, last, out.at[10], on_line(last)[1]).start)
            copy(held(n, line), held(n, line), out.at[7], r3y.at[n], across).start()

    def take_in(n, d):
        z, there = on_line(d)
        block(n, z, d, out.at[6], there).wait_recv()
        if d == last - 1:
            pl.when(beside_end)(block(n, z, last, out.at[11], on_line(1)[1]).start)
        copy(held(n, z), held(n, z), out.at[7], r3y.at[n], across).start()

    def to_partner(n):
        mine = unit(n, quarter, slice(None)) if n else unit(0, quarter)
        copy(mine, mine, out.at[8], r3c.at[n], partner).start()

    def from_across(n):
        arrived(all3.at[n, 0], r3y.at[n])
        other = 2 * (1 - side) + core
        theirs = unit(n, other, slice(None)) if n else unit(0, other)
        copy(theirs, theirs, out.at[8], r3c.at[n], partner).start()

    def gradient(n, q, e, parts):
        height = members * cap // parts
        span = slice(e * height, (e + 1) * height)
        left = rows_all[q].reshape(4, lines, members * cap, depth)[:, :, span]
        right = all3[n, :, :, span]
        count = 4 * lines * height
        return dot(left.reshape(count, depth), right.reshape(count, width), ((0,), (0,)))

    gate, up = summed(0), summed(1)
    sig = 1.0 / (1.0 + jnp.exp(-gate))
    all3[0, quarter, line] = (gate * sig * up).astype(BF16)
    spread_out(0)
    to_gate, to_up = up * sig * (1.0 + gate * (1.0 - sig)), gate * sig
    for e in range(2):
        dhidden, span = summed(2, e), band(2, e)
        all3[1, quarter, line, span] = (dhidden * to_gate[span]).astype(BF16)
        all3[2, quarter, line, span] = (dhidden * to_up[span]).astype(BF16)
        spread_out(1 + e)

    def finish(n):
        take_in(n, last)
        to_partner(n)

    def output_rows():
        places = [flip(line, d, lines) for d in range(lines)]
        hidden = jnp.concatenate([all3[0, quarter, z] for z in places], axis=0)
        rows = dot(hidden, wfull[2].reshape(line_depth, width), ((1,), (1,))).astype(BF16)
        rows = rows.reshape(lines, members, cap, line_depth)
        for i, z in enumerate(places):
            for m in range(members):
                send4[z * members + m] = rows[i, m]
            for dj in range(0 if i else 1, members):
                member = flip(j, dj, members)
                there = device(z, side, core, member)
                copy(send4.at[z * members + member], recv4.at[j, line], out.at[9], r4, there).start()
        recv4[j, line] = send4[flat]

    far = last - 1

    @pl.when(at_end)
    def _():
        for d in range(1, far + 1):
            take_in(0, d)
        for d in range(1, far):
            take_in(1, d)
            take_in(2, d)
        finish(0)
        output_rows()
        take_in(1, far)
        take_in(2, far)
        finish(1)
        finish(2)

    @pl.when(inner)
    def _():
        for d in range(1, last):
            take_in(0, d)
        finish(0)
        for d in range(1, last):
            take_in(1, d)
            take_in(2, d)
        output_rows()
        finish(1)
        finish(2)

    from_across(0)
    from_across(1)
    arrived(rows_all.at[:, 0:3], rx)
    arrived(all3.at[0, 0:2], r3c.at[0])
    grad_down[...] = gradient(0, 1, 0, 1).astype(BF16)
    arrived(all3.at[0, 0:2], r3c.at[1])
    for n in range(2):
        half_sum[n] = gradient(1 + n, 0, 0, 2)
    from_across(2)
    arrived(send4.at[1:], r4)
    for z in range(lines):
        out_rows = recv4[0, z].astype(F32)
        for m in range(1, members):
            out_rows += recv4[m, z].astype(F32)
        placed = dot(spread, (out_rows * slot_weight).astype(BF16), ((1,), (0,)))
        mixed[:, z * line_depth : (z + 1) * line_depth] = placed.astype(BF16)
    arrived(all3.at[0, 0:2], r3c.at[2])
    for n, result in enumerate((grad_gate, grad_up)):
        result[...] = (half_sum[n] + gradient(1 + n, 0, 1, 2)).astype(BF16)

    for n in range(3):
        departed(wfull.at[:, 0], n)
    departed(recv1.at[:, 1:], 3)
    departed(send2.at[:, 1:], 4)
    departed(rows_all.at[:, 0:3], 5)
    departed(all3.at[:, 0, 1:last], 6)
    pl.when(inner)(functools.partial(departed, all3.at[:, 0, 0], 10))
    pl.when(beside_end)(functools.partial(departed, all3.at[:, 0, 0], 11))
    departed(all3.at[:, 0], 7)
    departed(all3.at[:, 0:2], 8)
    departed(send4.at[1:], 9)


def write_out(*refs):
    sems = refs[-1]
    copies = [pltpu.make_async_copy(refs[n], refs[4 + n], sems.at[n]) for n in range(4)]
    for c in copies:
        c.start()
    for c in copies:
        c.wait()


def per_device(lines, members, tokens, cotangent, expert_ids, route_weights, join_groups, w_gate, w_up, w_down):
    tok_count, model = tokens.shape
    depth, width = w_gate.shape
    cap = tok_count // 8
    total = lines * members
    rows = members * cap
    vmem = pl.BlockSpec(memory_space=pltpu.VMEM)
    hbm = pl.BlockSpec(memory_space=pl.ANY)
    dma = pltpu.SemaphoreType.DMA
    grad = pltpu.VMEM((depth, width), BF16)
    results = pl.pallas_call(
        functools.partial(kernel, lines, members, cap),
        out_shape=(pltpu.VMEM((tok_count, model), BF16), grad, grad, grad),
        in_specs=[hbm] * 8,
        out_specs=(vmem,) * 4,
        scratch_shapes=[
            pltpu.SMEM(join_groups.shape, jnp.int32),
            pltpu.VMEM(expert_ids.shape[::-1], jnp.int32),
            pltpu.VMEM(route_weights.shape[::-1], F32),
            pltpu.VMEM((tok_count, model), BF16),
            pltpu.VMEM((tok_count, model), BF16),
            pltpu.VMEM((3, 4, depth, width), BF16),
            pltpu.VMEM((2, lines, 4, cap, depth), BF16),
            pltpu.VMEM((2, total, 4, cap, depth), BF16),
            pltpu.VMEM((2, 4, total, cap, depth), BF16),
            pltpu.VMEM((3, lines, rows, width), F32),
            pltpu.VMEM((3, lines, rows, width), BF16),
            pltpu.VMEM((3, lines, rows, width), BF16),
            pltpu.VMEM((3, 4, lines, rows, width), BF16),
            pltpu.VMEM((2, depth, width), F32),
            pltpu.VMEM((total, cap, 4 * depth), BF16),
            pltpu.VMEM((members, lines, cap, 4 * depth), BF16),
            dma((6,)), dma((12,)),
            dma((3,)), dma((3,)),
            dma((2,)), dma(()),
            dma((4,)),
            dma((3, lines - 1)), dma((3,)), dma((3,)),
            dma(()),
        ],
        compiler_params=pltpu.CompilerParams(
            collective_id=0, has_side_effects=True, vmem_limit_bytes=60 * 1024 * 1024
        ),
        name="expert_step",
    )(join_groups, tokens, cotangent, expert_ids.T, route_weights.T, w_gate, w_up, w_down)
    return pl.pallas_call(
        write_out,
        out_shape=tuple(jax.ShapeDtypeStruct(r.shape, r.dtype) for r in results),
        in_specs=[vmem] * 4,
        out_specs=(hbm,) * 4,
        scratch_shapes=[dma((4,))],
        name="write_out",
    )(*(pltpu.with_memory_space_constraint(r, pltpu.VMEM) for r in results))


def solution(mesh):
    in_specs = (
        P(("dp", "expert"), None),
        P(("dp", "expert"), None),
        P(("dp", "expert"), None),
        P(("dp", "expert"), None),
        P(),
        P("dp", "expert"),
        P("dp", "expert"),
        P("dp", "expert"),
    )
    out_specs = (P(("dp", "expert"), None), P("dp", "expert"), P("dp", "expert"), P("dp", "expert"))
    body = functools.partial(per_device, mesh.shape["dp"] // 4, mesh.shape["expert"])
    return jax.shard_map(body, mesh=mesh, in_specs=in_specs, out_specs=out_specs, check_vma=False)
```

```python
import functools

import jax
import jax.numpy as jnp
from jax import lax
from jax.experimental import pallas as pl
from jax.experimental.pallas import tpu as pltpu
from jax.sharding import PartitionSpec as P

F32, BF16 = jnp.float32, jnp.bfloat16
MESH = pl.DeviceIdType.MESH
SPLIT = (1, 1, 2)


def dot(a, b, dims):
    return lax.dot_general(a, b, (dims, ((), ())), preferred_element_type=F32)


def flip(a, d, count):
    out, bit = 0, 1
    while bit < count:
        mine = lax.rem(lax.div(a, bit), 2)
        turn = (d // bit) % 2 if isinstance(d, int) else lax.rem(lax.div(d, bit), 2)
        out += bit * (mine + turn - 2 * mine * turn)
        bit *= 2
    return out


def each(low, high, body):
    if high - low <= 16:
        for i in range(low, high):
            body(i)
    else:
        lax.fori_loop(low, high, lambda i, carry: (body(i), carry)[1], 0)


def kernel(
    lines, members, cap,
    join, tok, cot, ids, wts, wg, wu, wd,
    mixed, grad_gate, grad_up, grad_down,
    joinv, idv, wtv, tokv, cotv, wfull, blk, recv1, rows_all, part, send2, recv2, all3, half_sum, send4, recv4,
    local, out, rwy, rwp, r1, rx, r2, r3z, r3y, r3c, r4,
):
    p, j = lax.axis_index("dp"), lax.axis_index("expert")
    line, side, core = lax.div(p, 4), lax.rem(lax.div(p, 2), 2), lax.rem(p, 2)
    quarter = 2 * side + core
    total = lines * members
    flat = line * members + j
    tok_count = tok.shape[0]
    depth, width = wg.shape
    line_depth = 4 * depth

    def device(z, y, c, member):
        return (4 * z + 2 * y + c, member)

    partner = device(line, side, 1 - core, j)
    across = device(line, 1 - side, core, j)

    def copy(src, dst, send, recv, target):
        return pltpu.make_async_remote_copy(
            src_ref=src, dst_ref=dst, send_sem=send, recv_sem=recv, device_id=target, device_id_type=MESH
        )

    def peer(t):
        if isinstance(t, int):
            dz, dj = t // members, t % members
        else:
            dz, dj = lax.div(t, members), lax.rem(t, members)
        return flip(line, dz, lines), flip(j, dj, members)

    def on_line(d):
        z = flip(line, d, lines)
        return z, device(z, side, core, j)

    near = [(0, 1), (1, 0), (1, 1)]

    def beside(n):
        y = 1 - side if near[n][0] else side
        c = 1 - core if near[n][1] else core
        return 2 * y + c, device(line, y, c, j)

    barrier = pltpu.get_barrier_semaphore()

    def greet(t):
        z, member = peer(t)
        pl.semaphore_signal(barrier, inc=1, device_id=device(z, side, core, member), device_id_type=MESH)

    each(1, total, greet)
    for there in [beside(n)[1] for n in range(3)]:
        pl.semaphore_signal(barrier, inc=1, device_id=there, device_id_type=MESH)

    loads = [
        pltpu.make_async_copy(src, dst, local.at[n])
        for n, (src, dst) in enumerate(((ids, idv), (wts, wtv), (join, joinv), (tok, tokv), (cot, cotv)))
    ]
    own = [pltpu.make_async_copy(w, wfull.at[n, quarter], local.at[5]) for n, w in enumerate((wg, wu, wd))]
    for load in loads[:3] + own + loads[3:]:
        load.start()
    for load in loads[:2]:
        load.wait()

    chosen = idv[...] == 0
    routed = jnp.max(jnp.where(chosen, 1.0, 0.0), axis=0, keepdims=True)
    weight = jnp.sum(jnp.where(chosen, wtv[...], 0.0), axis=0, keepdims=True)
    upper = lax.broadcasted_iota(jnp.int32, (tok_count, tok_count), 0) <= lax.broadcasted_iota(
        jnp.int32, (tok_count, tok_count), 1
    )
    wide = jnp.broadcast_to(routed, (cap, tok_count))
    places = dot(wide.astype(BF16), jnp.where(upper, 1.0, 0.0).astype(BF16), ((1,), (0,))) - 1.0
    slot = lax.broadcasted_iota(jnp.int32, (cap, tok_count), 0).astype(F32)
    pick = jnp.where((places == slot) & (wide > 0.5), 1.0, 0.0)
    slot_weight = jnp.sum(pick * weight, axis=1, keepdims=True)
    spread = pick.T.astype(BF16)
    pick = pick.astype(BF16)
    loads[2].wait()
    active = 1.0 - joinv[p].astype(F32)
    mine = wfull.at[:, quarter]
    pltpu.make_async_copy(mine, mine, local.at[5]).wait()

    def swap(n):
        return copy(wfull.at[n, quarter], wfull.at[n, quarter], out.at[0], rwy.at[n], across)

    def lend(n):
        return copy(wfull.at[n, quarter], wfull.at[n, quarter], out.at[1], rwp.at[n], partner)

    def relay(n):
        held = wfull.at[n, 2 * (1 - side) + core]
        return copy(held, held, out.at[2], rwp.at[n], partner)

    def give(q, t):
        z, member = peer(t)
        copy(blk.at[q, z], recv1.at[q, flat], out.at[3], r1.at[q], device(z, side, core, member)).start()

    def cut(q, taken):
        for z in range(lines):
            for k in range(4):
                at = z * line_depth + k * depth
                blk[q, z, k] = taken[:, at : at + depth]

    def arrived(ref, recv):
        copy(ref, ref, out.at[0], recv, partner).wait_recv()

    def departed(ref, n):
        copy(ref, ref, out.at[n], rx, partner).wait_send()

    pl.semaphore_wait(barrier, total - 1 + 3)

    swap(0).start()
    loads[3].wait()
    cut(0, dot(pick, tokv[...], ((1,), (0,))).astype(BF16))
    each(1, total, functools.partial(give, 0))
    swap(1).start()
    lend(0).start()
    loads[4].wait()
    cut(1, (dot(pick, cotv[...], ((1,), (0,))) * (slot_weight * active)).astype(BF16))
    swap(2).start()
    each(1, total, functools.partial(give, 1))
    lend(1).start()
    lend(2).start()
    for q in range(2):
        recv1[q, flat] = blk[q, line]

    def product(n, q):
        left = jnp.concatenate([recv1[q, :, k].reshape(total * cap, depth) for k in range(4)], axis=1)
        term = dot(left, wfull[n].reshape(line_depth, width), ((1,), (0,)))
        term = term.reshape(lines, members * cap, width)
        part[n] = term
        send2[n] = term.astype(BF16)
        for e in range(SPLIT[n]):
            span = band(n, e)
            for d in range(1, lines):
                z, there = on_line(d)
                recv = r2.at[n + e]
                copy(send2.at[n, z, span], recv2.at[n, line, span], out.at[4], recv, there).start()

    def band(n, e):
        height = members * cap // SPLIT[n]
        return slice(e * height, (e + 1) * height)

    def summed(n, e=0):
        span = band(n, e)
        arrived(send2.at[n, 1:, span], r2.at[n + e])
        total_rows = part[n, line, span]
        for d in range(1, lines):
            total_rows += recv2[n, on_line(d)[0], span].astype(F32)
        return total_rows

    def stage(n, q):
        swap(n).wait_recv()
        relay(n).start()
        if n != 1:
            arrived(recv1.at[q, 1:], r1.at[q])
        arrived(wfull.at[n, 0:2], rwp.at[n])
        product(n, q)

    stage(0, 0)
    stage(1, 0)
    stage(2, 1)

    def share(q, n):
        k, there = beside(n)
        return copy(recv1.at[q, :, k], rows_all.at[q, quarter], out.at[5], rx, there)

    for q in range(2):
        for n in range(3):
            share(q, n).start()
        rows_all[q, quarter] = recv1[q, :, quarter]

    def unit(n, *place):
        return all3.at[(0, *place)] if n == 0 else all3.at[(slice(1, 3), *place, band(2, n - 1))]

    def held(n, z):
        return unit(n, quarter, z)

    last = lines - 1
    at_end = (line == 0) | (line == last)
    inner = jnp.logical_not(at_end)
    beside_end = (line == 1) | (line == last - 1)

    def block(n, z, d, sem, there):
        return copy(held(n, z), held(n, z), sem, r3z.at[n, d - 1], there)

    def spread_out(*which):
        for d in [last - 1] + list(range(1, last - 1)):
            for n in which:
                block(n, line, d, out.at[6], on_line(d)[1]).start()
        for n in which:
            pl.when(inner)(block(n, line, last, out.at[10], on_line(last)[1]).start)
            copy(held(n, line), held(n, line), out.at[7], r3y.at[n], across).start()

    def take_in(n, d):
        z, there = on_line(d)
        block(n, z, d, out.at[6], there).wait_recv()
        if d == last - 1:
            pl.when(beside_end)(block(n, z, last, out.at[11], on_line(1)[1]).start)
        copy(held(n, z), held(n, z), out.at[7], r3y.at[n], across).start()

    def to_partner(n):
        mine = unit(n, quarter, slice(None)) if n else unit(0, quarter)
        copy(mine, mine, out.at[8], r3c.at[n], partner).start()

    def from_across(n):
        arrived(all3.at[n, 0], r3y.at[n])
        other = 2 * (1 - side) + core
        theirs = unit(n, other, slice(None)) if n else unit(0, other)
        copy(theirs, theirs, out.at[8], r3c.at[n], partner).start()

    def gradient(n, q, span, quarters):
        count = lines * (span.stop - span.start)
        left = [rows_all[q, k].reshape(lines, members * cap, depth)[:, span].reshape(count, depth) for k in quarters]
        right = [all3[n, k, :, span].reshape(count, width) for k in quarters]
        return dot(jnp.concatenate(left, axis=0), jnp.concatenate(right, axis=0), ((0,), (0,)))

    gate, up = summed(0), summed(1)
    sig = 1.0 / (1.0 + jnp.exp(-gate))
    all3[0, quarter, line] = (gate * sig * up).astype(BF16)
    spread_out(0)
    to_gate, to_up = up * sig * (1.0 + gate * (1.0 - sig)), gate * sig
    for e in range(2):
        dhidden, span = summed(2, e), band(2, e)
        all3[1, quarter, line, span] = (dhidden * to_gate[span]).astype(BF16)
        all3[2, quarter, line, span] = (dhidden * to_up[span]).astype(BF16)
        spread_out(1 + e)

    def finish(n):
        take_in(n, last)
        to_partner(n)

    def output_rows():
        places = [flip(line, d, lines) for d in range(lines)]
        hidden = jnp.concatenate([all3[0, quarter, z] for z in places], axis=0)
        rows = dot(hidden, wfull[2].reshape(line_depth, width), ((1,), (1,))).astype(BF16)
        rows = rows.reshape(lines, members, cap, line_depth)
        for i, z in enumerate(places):
            for m in range(members):
                send4[z * members + m] = rows[i, m]
            for dj in range(0 if i else 1, members):
                member = flip(j, dj, members)
                there = device(z, side, core, member)
                copy(send4.at[z * members + member], recv4.at[j, line], out.at[9], r4, there).start()
        recv4[j, line] = send4[flat]

    far = last - 1

    @pl.when(at_end)
    def _():
        for d in range(1, far + 1):
            take_in(0, d)
        for d in range(1, far):
            take_in(1, d)
            take_in(2, d)
        finish(0)
        output_rows()
        for n in (1, 2):
            take_in(n, far)
            finish(n)

    @pl.when(inner)
    def _():
        for d in range(1, last):
            take_in(0, d)
        finish(0)
        for n in (1, 2):
            for d in range(1, last):
                take_in(n, d)
        output_rows()
        finish(1)
        finish(2)

    from_across(0)
    from_across(1)
    arrived(rows_all.at[:, 0:3], rx)
    arrived(all3.at[0, 0:2], r3c.at[0])
    grad_down[...] = gradient(0, 1, slice(0, members * cap), range(4)).astype(BF16)
    arrived(all3.at[0, 0:2], r3c.at[1])
    for n in range(2):
        half_sum[n] = gradient(1 + n, 0, band(2, 0), range(4))
    from_across(2)
    for n in range(2):
        half_sum[n] += gradient(1 + n, 0, band(2, 1), (core, 2 + core))
    arrived(send4.at[1:], r4)
    for z in range(lines):
        out_rows = recv4[0, z].astype(F32)
        for m in range(1, members):
            out_rows += recv4[m, z].astype(F32)
        placed = dot(spread, (out_rows * slot_weight).astype(BF16), ((1,), (0,)))
        mixed[:, z * line_depth : (z + 1) * line_depth] = placed.astype(BF16)
    arrived(all3.at[0, 0:2], r3c.at[2])
    for n, result in enumerate((grad_gate, grad_up)):
        result[...] = (half_sum[n] + gradient(1 + n, 0, band(2, 1), (1 - core, 3 - core))).astype(BF16)

    for n in range(3):
        departed(wfull.at[:, 0], n)
    departed(recv1.at[:, 1:], 3)
    departed(send2.at[:, 1:], 4)
    departed(rows_all.at[:, 0:3], 5)
    departed(all3.at[:, 0, 1:last], 6)
    pl.when(inner)(functools.partial(departed, all3.at[:, 0, 0], 10))
    pl.when(beside_end)(functools.partial(departed, all3.at[:, 0, 0], 11))
    departed(all3.at[:, 0], 7)
    departed(all3.at[:, 0:2], 8)
    departed(send4.at[1:], 9)


def write_out(*refs):
    sems = refs[-1]
    copies = [pltpu.make_async_copy(refs[n], refs[4 + n], sems.at[n]) for n in range(4)]
    for c in copies:
        c.start()
    for c in copies:
        c.wait()


def per_device(lines, members, tokens, cotangent, expert_ids, route_weights, join_groups, w_gate, w_up, w_down):
    tok_count, model = tokens.shape
    depth, width = w_gate.shape
    cap = tok_count // 8
    total = lines * members
    rows = members * cap
    vmem = pl.BlockSpec(memory_space=pltpu.VMEM)
    hbm = pl.BlockSpec(memory_space=pl.ANY)
    dma = pltpu.SemaphoreType.DMA
    grad = pltpu.VMEM((depth, width), BF16)
    results = pl.pallas_call(
        functools.partial(kernel, lines, members, cap),
        out_shape=(pltpu.VMEM((tok_count, model), BF16), grad, grad, grad),
        in_specs=[hbm] * 8,
        out_specs=(vmem,) * 4,
        scratch_shapes=[
            pltpu.SMEM(join_groups.shape, jnp.int32),
            pltpu.VMEM(expert_ids.shape[::-1], jnp.int32),
            pltpu.VMEM(route_weights.shape[::-1], F32),
            pltpu.VMEM((tok_count, model), BF16),
            pltpu.VMEM((tok_count, model), BF16),
            pltpu.VMEM((3, 4, depth, width), BF16),
            pltpu.VMEM((2, lines, 4, cap, depth), BF16),
            pltpu.VMEM((2, total, 4, cap, depth), BF16),
            pltpu.VMEM((2, 4, total, cap, depth), BF16),
            pltpu.VMEM((3, lines, rows, width), F32),
            pltpu.VMEM((3, lines, rows, width), BF16),
            pltpu.VMEM((3, lines, rows, width), BF16),
            pltpu.VMEM((3, 4, lines, rows, width), BF16),
            pltpu.VMEM((2, depth, width), F32),
            pltpu.VMEM((total, cap, 4 * depth), BF16),
            pltpu.VMEM((members, lines, cap, 4 * depth), BF16),
            dma((6,)), dma((12,)),
            dma((3,)), dma((3,)),
            dma((2,)), dma(()),
            dma((4,)),
            dma((3, lines - 1)), dma((3,)), dma((3,)),
            dma(()),
        ],
        compiler_params=pltpu.CompilerParams(
            collective_id=0, has_side_effects=True, vmem_limit_bytes=60 * 1024 * 1024
        ),
        name="expert_step",
    )(join_groups, tokens, cotangent, expert_ids.T, route_weights.T, w_gate, w_up, w_down)
    return pl.pallas_call(
        write_out,
        out_shape=tuple(jax.ShapeDtypeStruct(r.shape, r.dtype) for r in results),
        in_specs=[vmem] * 4,
        out_specs=(hbm,) * 4,
        scratch_shapes=[dma((4,))],
        name="write_out",
    )(*(pltpu.with_memory_space_constraint(r, pltpu.VMEM) for r in results))


def solution(mesh):
    in_specs = (
        P(("dp", "expert"), None),
        P(("dp", "expert"), None),
        P(("dp", "expert"), None),
        P(("dp", "expert"), None),
        P(),
        P("dp", "expert"),
        P("dp", "expert"),
        P("dp", "expert"),
    )
    out_specs = (P(("dp", "expert"), None), P("dp", "expert"), P("dp", "expert"), P("dp", "expert"))
    body = functools.partial(per_device, mesh.shape["dp"] // 4, mesh.shape["expert"])
    return jax.shard_map(body, mesh=mesh, in_specs=in_specs, out_specs=out_specs, check_vma=False)
```

```python
import functools

import jax
import jax.numpy as jnp
from jax import lax
from jax.experimental import pallas as pl
from jax.experimental.pallas import tpu as pltpu
from jax.sharding import PartitionSpec as P

F32, BF16 = jnp.float32, jnp.bfloat16
MESH = pl.DeviceIdType.MESH
SPLIT, FIRST = (1, 2, 2), (0, 1, 3)


def dot(a, b, dims):
    return lax.dot_general(a, b, (dims, ((), ())), preferred_element_type=F32)


def flip(a, d, count):
    out, bit = 0, 1
    while bit < count:
        mine = lax.rem(lax.div(a, bit), 2)
        turn = (d // bit) % 2 if isinstance(d, int) else lax.rem(lax.div(d, bit), 2)
        out += bit * (mine + turn - 2 * mine * turn)
        bit *= 2
    return out


def each(low, high, body):
    if high - low <= 16:
        for i in range(low, high):
            body(i)
    else:
        lax.fori_loop(low, high, lambda i, carry: (body(i), carry)[1], 0)


def product_of_rows(rows_all, all3, n, q, span, quarters):
    lines, height, width = all3.shape[2:]
    count, depth = lines * (span.stop - span.start), rows_all.shape[-1]
    left = [rows_all[q, k].reshape(lines, height, depth)[:, span].reshape(count, depth) for k in quarters]
    right = [all3[n, k, :, span].reshape(count, width) for k in quarters]
    return dot(jnp.concatenate(left, axis=0), jnp.concatenate(right, axis=0), ((0,), (0,)))


def kernel(
    lines, members, cap,
    join, tok, cot, ids, wts, wg, wu, wd,
    mixed, grad_down, half_sum, all3, rows_all,
    joinv, idv, wtv, tokv, cotv, wfull, blk, recv1, part, send2, recv2, send4, recv4,
    local, out, rwy, rwp, r1, rx, r2, r3z, r3y, r3c, r4,
):
    p, j = lax.axis_index("dp"), lax.axis_index("expert")
    line, side, core = lax.div(p, 4), lax.rem(lax.div(p, 2), 2), lax.rem(p, 2)
    quarter = 2 * side + core
    total = lines * members
    flat = line * members + j
    tok_count = tok.shape[0]
    depth, width = wg.shape
    line_depth = 4 * depth

    def device(z, y, c, member):
        return (4 * z + 2 * y + c, member)

    partner = device(line, side, 1 - core, j)
    across = device(line, 1 - side, core, j)

    def copy(src, dst, send, recv, target):
        return pltpu.make_async_remote_copy(
            src_ref=src, dst_ref=dst, send_sem=send, recv_sem=recv, device_id=target, device_id_type=MESH
        )

    def peer(t):
        if isinstance(t, int):
            dz, dj = t // members, t % members
        else:
            dz, dj = lax.div(t, members), lax.rem(t, members)
        return flip(line, dz, lines), flip(j, dj, members)

    def on_line(d):
        z = flip(line, d, lines)
        return z, device(z, side, core, j)

    near = [(0, 1), (1, 0), (1, 1)]

    def beside(n):
        y = 1 - side if near[n][0] else side
        c = 1 - core if near[n][1] else core
        return 2 * y + c, device(line, y, c, j)

    barrier = pltpu.get_barrier_semaphore()

    def greet(t):
        z, member = peer(t)
        pl.semaphore_signal(barrier, inc=1, device_id=device(z, side, core, member), device_id_type=MESH)

    each(1, total, greet)
    for there in [beside(n)[1] for n in range(3)]:
        pl.semaphore_signal(barrier, inc=1, device_id=there, device_id_type=MESH)

    loads = [
        pltpu.make_async_copy(src, dst, local.at[n])
        for n, (src, dst) in enumerate(((ids, idv), (wts, wtv), (join, joinv), (tok, tokv), (cot, cotv)))
    ]
    own = [pltpu.make_async_copy(w, wfull.at[n, quarter], local.at[5]) for n, w in enumerate((wg, wu, wd))]
    for load in loads[:3] + own + loads[3:]:
        load.start()
    for load in loads[:2]:
        load.wait()

    chosen = idv[...] == 0
    routed = jnp.max(jnp.where(chosen, 1.0, 0.0), axis=0, keepdims=True)
    weight = jnp.sum(jnp.where(chosen, wtv[...], 0.0), axis=0, keepdims=True)
    upper = lax.broadcasted_iota(jnp.int32, (tok_count, tok_count), 0) <= lax.broadcasted_iota(
        jnp.int32, (tok_count, tok_count), 1
    )
    wide = jnp.broadcast_to(routed, (cap, tok_count))
    places = dot(wide.astype(BF16), jnp.where(upper, 1.0, 0.0).astype(BF16), ((1,), (0,))) - 1.0
    slot = lax.broadcasted_iota(jnp.int32, (cap, tok_count), 0).astype(F32)
    pick = jnp.where((places == slot) & (wide > 0.5), 1.0, 0.0)
    slot_weight = jnp.sum(pick * weight, axis=1, keepdims=True)
    spread = pick.T.astype(BF16)
    pick = pick.astype(BF16)
    loads[2].wait()
    active = 1.0 - joinv[p].astype(F32)
    mine = wfull.at[:, quarter]
    pltpu.make_async_copy(mine, mine, local.at[5]).wait()

    def swap(n):
        return copy(wfull.at[n, quarter], wfull.at[n, quarter], out.at[0], rwy.at[n], across)

    def lend(n):
        return copy(wfull.at[n, quarter], wfull.at[n, quarter], out.at[1], rwp.at[n], partner)

    def relay(n):
        held = wfull.at[n, 2 * (1 - side) + core]
        return copy(held, held, out.at[2], rwp.at[n], partner)

    def give(q, t):
        z, member = peer(t)
        copy(blk.at[q, z], recv1.at[q, flat], out.at[3], r1.at[q], device(z, side, core, member)).start()

    def cut(q, taken):
        for z in range(lines):
            for k in range(4):
                at = z * line_depth + k * depth
                blk[q, z, k] = taken[:, at : at + depth]

    def arrived(ref, recv):
        copy(ref, ref, out.at[0], recv, partner).wait_recv()

    def departed(ref, n):
        copy(ref, ref, out.at[n], rx, partner).wait_send()

    pl.semaphore_wait(barrier, total - 1 + 3)

    swap(0).start()
    loads[3].wait()
    cut(0, dot(pick, tokv[...], ((1,), (0,))).astype(BF16))
    each(1, total, functools.partial(give, 0))
    swap(1).start()
    lend(0).start()
    loads[4].wait()
    cut(1, (dot(pick, cotv[...], ((1,), (0,))) * (slot_weight * active)).astype(BF16))
    swap(2).start()
    each(1, total, functools.partial(give, 1))
    lend(1).start()
    lend(2).start()
    for q in range(2):
        recv1[q, flat] = blk[q, line]

    def product(n, q):
        left = jnp.concatenate([recv1[q, :, k].reshape(total * cap, depth) for k in range(4)], axis=1)
        term = dot(left, wfull[n].reshape(line_depth, width), ((1,), (0,)))
        term = term.reshape(lines, members * cap, width)
        part[n] = term
        send2[n] = term.astype(BF16)
        for e in range(SPLIT[n]):
            span = band(n, e)
            for d in range(1, lines):
                z, there = on_line(d)
                recv = r2.at[FIRST[n] + e]
                copy(send2.at[n, z, span], recv2.at[n, line, span], out.at[4], recv, there).start()

    def band(n, e):
        height = members * cap // SPLIT[n]
        return slice(e * height, (e + 1) * height)

    def summed(n, e=0):
        span = band(n, e)
        arrived(send2.at[n, 1:, span], r2.at[FIRST[n] + e])
        total_rows = part[n, line, span]
        for d in range(1, lines):
            total_rows += recv2[n, on_line(d)[0], span].astype(F32)
        return total_rows

    def stage(n, q):
        swap(n).wait_recv()
        relay(n).start()
        if n != 1:
            arrived(recv1.at[q, 1:], r1.at[q])
        arrived(wfull.at[n, 0:2], rwp.at[n])
        product(n, q)

    stage(0, 0)
    stage(1, 0)
    stage(2, 1)

    def share(q, n):
        k, there = beside(n)
        return copy(recv1.at[q, :, k], rows_all.at[q, quarter], out.at[5], rx, there)

    for q in range(2):
        for n in range(3):
            share(q, n).start()
        rows_all[q, quarter] = recv1[q, :, quarter]

    def unit(n, *place):
        return all3.at[(0 if n < 2 else slice(1, 3), *place, band(2, n % 2))]

    def held(n, z):
        return unit(n, quarter, z)

    last = lines - 1
    at_end = (line == 0) | (line == last)
    inner = jnp.logical_not(at_end)
    beside_end = (line == 1) | (line == last - 1)

    def block(n, z, d, sem, there):
        return copy(held(n, z), held(n, z), sem, r3z.at[n, d - 1], there)

    def spread_out(*which):
        for d in [last - 1] + list(range(1, last - 1)):
            for n in which:
                block(n, line, d, out.at[6], on_line(d)[1]).start()
        for n in which:
            pl.when(inner)(block(n, line, last, out.at[10], on_line(last)[1]).start)
            copy(held(n, line), held(n, line), out.at[7], r3y.at[n], across).start()

    def take_in(n, d):
        z, there = on_line(d)
        block(n, z, d, out.at[6], there).wait_recv()
        if d == last - 1:
            pl.when(beside_end)(block(n, z, last, out.at[11], on_line(1)[1]).start)
        copy(held(n, z), held(n, z), out.at[7], r3y.at[n], across).start()

    def to_partner(n):
        mine = unit(n, quarter, slice(None))
        copy(mine, mine, out.at[8], r3c.at[n], partner).start()

    def from_across(n):
        arrived(unit(n, 0, slice(None)), r3y.at[n])
        other = 2 * (1 - side) + core
        theirs = unit(n, other, slice(None))
        copy(theirs, theirs, out.at[8], r3c.at[n], partner).start()

    gate = summed(0)
    sig = 1.0 / (1.0 + jnp.exp(-gate))
    to_hidden, slope = gate * sig, sig * (1.0 + gate * (1.0 - sig))
    to_gate = []
    for e in range(2):
        up, span = summed(1, e), band(2, e)
        all3[0, quarter, line, span] = (to_hidden[span] * up).astype(BF16)
        spread_out(e)
        to_gate.append(up * slope[span])
    for e in range(2):
        dhidden, span = summed(2, e), band(2, e)
        all3[1, quarter, line, span] = (dhidden * to_gate[e]).astype(BF16)
        all3[2, quarter, line, span] = (dhidden * to_hidden[span]).astype(BF16)
        spread_out(2 + e)

    def finish(n):
        take_in(n, last)
        to_partner(n)

    def output_rows():
        places = [flip(line, d, lines) for d in range(lines)]
        hidden = jnp.concatenate([all3[0, quarter, z] for z in places], axis=0)
        rows = dot(hidden, wfull[2].reshape(line_depth, width), ((1,), (1,))).astype(BF16)
        rows = rows.reshape(lines, members, cap, line_depth)
        for i, z in enumerate(places):
            for m in range(members):
                send4[z * members + m] = rows[i, m]
            for dj in range(0 if i else 1, members):
                member = flip(j, dj, members)
                there = device(z, side, core, member)
                copy(send4.at[z * members + member], recv4.at[j, line], out.at[9], r4, there).start()
        recv4[j, line] = send4[flat]

    far = last - 1

    @pl.when(at_end)
    def _():
        for n in (0, 1):
            for d in range(1, last):
                take_in(n, d)
        for n in (2, 3):
            for d in range(1, far):
                take_in(n, d)
        finish(0)
        finish(1)
        output_rows()
        for n in (2, 3):
            take_in(n, far)
            finish(n)

    @pl.when(inner)
    def _():
        for n in (0, 1):
            for d in range(1, last):
                take_in(n, d)
        finish(0)
        finish(1)
        for n in (2, 3):
            for d in range(1, last):
                take_in(n, d)
        output_rows()
        finish(2)
        finish(3)

    for n in range(3):
        from_across(n)
    arrived(rows_all.at[:, 0:3], rx)
    for n in range(2):
        arrived(unit(n, slice(0, 2), slice(None)), r3c.at[n])
    grad_down[...] = product_of_rows(rows_all, all3, 0, 1, slice(0, members * cap), range(4)).astype(BF16)
    arrived(unit(2, slice(0, 2), slice(None)), r3c.at[2])
    for n in range(2):
        half_sum[n] = product_of_rows(rows_all, all3, 1 + n, 0, band(2, 0), range(4))
    from_across(3)
    for n in range(2):
        half_sum[n] += product_of_rows(rows_all, all3, 1 + n, 0, band(2, 1), (core, 2 + core))
    arrived(send4.at[1:], r4)
    for z in range(lines):
        out_rows = recv4[0, z].astype(F32)
        for m in range(1, members):
            out_rows += recv4[m, z].astype(F32)
        placed = dot(spread, (out_rows * slot_weight).astype(BF16), ((1,), (0,)))
        mixed[:, z * line_depth : (z + 1) * line_depth] = placed.astype(BF16)
    arrived(unit(3, slice(0, 2), slice(None)), r3c.at[3])

    for n in range(3):
        departed(wfull.at[:, 0], n)
    departed(recv1.at[:, 1:], 3)
    departed(send2.at[:, 1:], 4)
    departed(rows_all.at[:, 0:3], 5)
    departed(all3.at[:, 0, 1:last], 6)
    pl.when(inner)(functools.partial(departed, all3.at[:, 0, 0], 10))
    pl.when(beside_end)(functools.partial(departed, all3.at[:, 0, 0], 11))
    departed(all3.at[:, 0], 7)
    departed(all3.at[:, 0:2], 8)
    departed(send4.at[1:], 9)


def write_out(mixed, grad_down, half_sum, all3, rows_all, mixed_out, gate_out, up_out, down_out, last_two, sems):
    core = lax.rem(lax.axis_index("dp"), 2)
    height = all3.shape[3]
    copies = [
        pltpu.make_async_copy(src, dst, sems.at[n])
        for n, (src, dst) in enumerate(
            ((mixed, mixed_out), (grad_down, down_out), (last_two.at[0], gate_out), (last_two.at[1], up_out))
        )
    ]
    copies[0].start()
    copies[1].start()
    for n in range(2):
        rest = product_of_rows(rows_all, all3, 1 + n, 0, slice(height // 2, height), (1 - core, 3 - core))
        last_two[n] = (half_sum[n] + rest).astype(BF16)
        copies[2 + n].start()
    for c in copies:
        c.wait()


def per_device(lines, members, tokens, cotangent, expert_ids, route_weights, join_groups, w_gate, w_up, w_down):
    tok_count, model = tokens.shape
    depth, width = w_gate.shape
    cap = tok_count // 8
    total = lines * members
    rows = members * cap
    vmem = pl.BlockSpec(memory_space=pltpu.VMEM)
    hbm = pl.BlockSpec(memory_space=pltpu.HBM)
    dma = pltpu.SemaphoreType.DMA
    grad = jax.ShapeDtypeStruct((depth, width), BF16)
    results = pl.pallas_call(
        functools.partial(kernel, lines, members, cap),
        out_shape=(
            pltpu.VMEM((tok_count, model), BF16),
            pltpu.VMEM((depth, width), BF16),
            pltpu.VMEM((2, depth, width), F32),
            pltpu.VMEM((3, 4, lines, rows, width), BF16),
            pltpu.VMEM((2, 4, total, cap, depth), BF16),
        ),
        in_specs=[hbm] * 8,
        out_specs=(vmem,) * 5,
        scratch_shapes=[
            pltpu.SMEM(join_groups.shape, jnp.int32),
            pltpu.VMEM(expert_ids.shape[::-1], jnp.int32),
            pltpu.VMEM(route_weights.shape[::-1], F32),
            pltpu.VMEM((tok_count, model), BF16),
            pltpu.VMEM((tok_count, model), BF16),
            pltpu.VMEM((3, 4, depth, width), BF16),
            pltpu.VMEM((2, lines, 4, cap, depth), BF16),
            pltpu.VMEM((2, total, 4, cap, depth), BF16),
            pltpu.VMEM((3, lines, rows, width), F32),
            pltpu.VMEM((3, lines, rows, width), BF16),
            pltpu.VMEM((3, lines, rows, width), BF16),
            pltpu.VMEM((total, cap, 4 * depth), BF16),
            pltpu.VMEM((members, lines, cap, 4 * depth), BF16),
            dma((6,)), dma((12,)),
            dma((3,)), dma((3,)),
            dma((2,)), dma(()),
            dma((5,)),
            dma((4, lines - 1)), dma((4,)), dma((4,)),
            dma(()),
        ],
        compiler_params=pltpu.CompilerParams(
            collective_id=0, has_side_effects=True, vmem_limit_bytes=44 * 1024 * 1024
        ),
        name="expert_step",
    )(
        *(
            pltpu.with_memory_space_constraint(x, pltpu.HBM)
            for x in (join_groups, tokens, cotangent, expert_ids.T, route_weights.T, w_gate, w_up, w_down)
        )
    )
    return pl.pallas_call(
        write_out,
        out_shape=(jax.ShapeDtypeStruct((tok_count, model), BF16), grad, grad, grad),
        in_specs=[vmem] * 5,
        out_specs=(hbm,) * 4,
        scratch_shapes=[pltpu.VMEM((2, depth, width), BF16), dma((4,))],
        compiler_params=pltpu.CompilerParams(vmem_limit_bytes=16 * 1024 * 1024),
        name="write_out",
    )(*(pltpu.with_memory_space_constraint(r, pltpu.VMEM) for r in results))


def solution(mesh):
    in_specs = (
        P(("dp", "expert"), None),
        P(("dp", "expert"), None),
        P(("dp", "expert"), None),
        P(("dp", "expert"), None),
        P(),
        P("dp", "expert"),
        P("dp", "expert"),
        P("dp", "expert"),
    )
    out_specs = (P(("dp", "expert"), None), P("dp", "expert"), P("dp", "expert"), P("dp", "expert"))
    body = functools.partial(per_device, mesh.shape["dp"] // 4, mesh.shape["expert"])
    return jax.shard_map(body, mesh=mesh, in_specs=in_specs, out_specs=out_specs, check_vma=False)
```

```python
import functools

import jax
import jax.numpy as jnp
from jax import lax
from jax.experimental import pallas as pl
from jax.experimental.pallas import tpu as pltpu
from jax.sharding import PartitionSpec as P

F32, BF16 = jnp.float32, jnp.bfloat16
MESH = pl.DeviceIdType.MESH
SPLIT, FIRST = (1, 2, 2), (0, 1, 3)


def dot(a, b, dims):
    return lax.dot_general(a, b, (dims, ((), ())), preferred_element_type=F32)


def flip(a, d, count):
    out, bit = 0, 1
    while bit < count:
        mine = lax.rem(lax.div(a, bit), 2)
        turn = (d // bit) % 2 if isinstance(d, int) else lax.rem(lax.div(d, bit), 2)
        out += bit * (mine + turn - 2 * mine * turn)
        bit *= 2
    return out


def each(low, high, body):
    if high - low <= 16:
        for i in range(low, high):
            body(i)
    else:
        lax.fori_loop(low, high, lambda i, carry: (body(i), carry)[1], 0)


def product_of_rows(rows_all, all3, n, q, span, quarters):
    lines, height, width = all3.shape[2:]
    count, depth = lines * (span.stop - span.start), rows_all.shape[-1]
    left = [rows_all[q, k].reshape(lines, height, depth)[:, span].reshape(count, depth) for k in quarters]
    right = [all3[n, k, :, span].reshape(count, width) for k in quarters]
    return dot(jnp.concatenate(left, axis=0), jnp.concatenate(right, axis=0), ((0,), (0,)))


def kernel(
    lines, members, cap,
    join, tok, cot, ids, wts, wg, wu, wd,
    mixed, grad_down, half_sum, all3, rows_all,
    joinv, idv, wtv, tokv, cotv, wfull, blk, recv1, part, send2, recv2, send4, recv4,
    local, out, rwy, rwp, r1, rx, r2, r3z, r3y, r3c, r4,
):
    p, j = lax.axis_index("dp"), lax.axis_index("expert")
    line, side, core = lax.div(p, 4), lax.rem(lax.div(p, 2), 2), lax.rem(p, 2)
    quarter = 2 * side + core
    total = lines * members
    flat = line * members + j
    tok_count = tok.shape[0]
    depth, width = wg.shape
    line_depth = 4 * depth

    def device(z, y, c, member):
        return (4 * z + 2 * y + c, member)

    partner = device(line, side, 1 - core, j)
    across = device(line, 1 - side, core, j)

    def copy(src, dst, send, recv, target):
        return pltpu.make_async_remote_copy(
            src_ref=src, dst_ref=dst, send_sem=send, recv_sem=recv, device_id=target, device_id_type=MESH
        )

    def peer(t):
        if isinstance(t, int):
            dz, dj = t // members, t % members
        else:
            dz, dj = lax.div(t, members), lax.rem(t, members)
        return flip(line, dz, lines), flip(j, dj, members)

    def on_line(d):
        z = flip(line, d, lines)
        return z, device(z, side, core, j)

    near = [(0, 1), (1, 0), (1, 1)]

    def beside(n):
        y = 1 - side if near[n][0] else side
        c = 1 - core if near[n][1] else core
        return 2 * y + c, device(line, y, c, j)

    barrier = pltpu.get_barrier_semaphore()

    def greet(t):
        z, member = peer(t)
        pl.semaphore_signal(barrier, inc=1, device_id=device(z, side, core, member), device_id_type=MESH)

    each(1, total, greet)
    for there in [beside(n)[1] for n in range(3)]:
        pl.semaphore_signal(barrier, inc=1, device_id=there, device_id_type=MESH)

    loads = [
        pltpu.make_async_copy(src, dst, local.at[n])
        for n, (src, dst) in enumerate(((ids, idv), (wts, wtv), (join, joinv), (tok, tokv), (cot, cotv)))
    ]
    own = [pltpu.make_async_copy(w, wfull.at[n, quarter], local.at[5]) for n, w in enumerate((wg, wu, wd))]
    for load in loads[:3] + own + loads[3:]:
        load.start()
    for load in loads[:2]:
        load.wait()

    chosen = idv[...] == 0
    routed = jnp.max(jnp.where(chosen, 1.0, 0.0), axis=0, keepdims=True)
    weight = jnp.sum(jnp.where(chosen, wtv[...], 0.0), axis=0, keepdims=True)
    upper = lax.broadcasted_iota(jnp.int32, (tok_count, tok_count), 0) <= lax.broadcasted_iota(
        jnp.int32, (tok_count, tok_count), 1
    )
    wide = jnp.broadcast_to(routed, (cap, tok_count))
    places = dot(wide.astype(BF16), jnp.where(upper, 1.0, 0.0).astype(BF16), ((1,), (0,))) - 1.0
    slot = lax.broadcasted_iota(jnp.int32, (cap, tok_count), 0).astype(F32)
    pick = jnp.where((places == slot) & (wide > 0.5), 1.0, 0.0)
    slot_weight = jnp.sum(pick * weight, axis=1, keepdims=True)
    spread = pick.T.astype(BF16)
    pick = pick.astype(BF16)
    loads[2].wait()
    active = 1.0 - joinv[p].astype(F32)
    mine = wfull.at[:, quarter]
    pltpu.make_async_copy(mine, mine, local.at[5]).wait()

    def swap(n):
        return copy(wfull.at[n, quarter], wfull.at[n, quarter], out.at[0], rwy.at[n], across)

    def lend(n):
        return copy(wfull.at[n, quarter], wfull.at[n, quarter], out.at[1], rwp.at[n], partner)

    def relay(n):
        held = wfull.at[n, 2 * (1 - side) + core]
        return copy(held, held, out.at[2], rwp.at[n], partner)

    def give(q, t):
        z, member = peer(t)
        copy(blk.at[q, z], recv1.at[q, flat], out.at[3], r1.at[q], device(z, side, core, member)).start()

    def cut(q, taken):
        for z in range(lines):
            for k in range(4):
                at = z * line_depth + k * depth
                blk[q, z, k] = taken[:, at : at + depth]

    def arrived(ref, recv):
        copy(ref, ref, out.at[0], recv, partner).wait_recv()

    def departed(ref, n):
        copy(ref, ref, out.at[n], rx, partner).wait_send()

    pl.semaphore_wait(barrier, total - 1 + 3)

    swap(0).start()
    loads[3].wait()
    cut(0, dot(pick, tokv[...], ((1,), (0,))).astype(BF16))
    each(1, total, functools.partial(give, 0))
    swap(1).start()
    lend(0).start()
    loads[4].wait()
    cut(1, (dot(pick, cotv[...], ((1,), (0,))) * (slot_weight * active)).astype(BF16))
    swap(2).start()
    each(1, total, functools.partial(give, 1))
    lend(1).start()
    lend(2).start()
    for q in range(2):
        recv1[q, flat] = blk[q, line]

    def product(n, q):
        left = jnp.concatenate([recv1[q, :, k].reshape(total * cap, depth) for k in range(4)], axis=1)
        term = dot(left, wfull[n].reshape(line_depth, width), ((1,), (0,)))
        term = term.reshape(lines, members * cap, width)
        part[n] = term
        send2[n] = term.astype(BF16)
        for e in range(SPLIT[n]):
            span = band(n, e)
            for d in range(1, lines):
                z, there = on_line(d)
                recv = r2.at[FIRST[n] + e]
                copy(send2.at[n, z, span], recv2.at[n, line, span], out.at[4], recv, there).start()

    def band(n, e):
        height = members * cap // SPLIT[n]
        return slice(e * height, (e + 1) * height)

    def summed(n, e=0):
        span = band(n, e)
        arrived(send2.at[n, 1:, span], r2.at[FIRST[n] + e])
        total_rows = part[n, line, span]
        for d in range(1, lines):
            total_rows += recv2[n, on_line(d)[0], span].astype(F32)
        return total_rows

    def stage(n, q):
        swap(n).wait_recv()
        relay(n).start()
        if n != 1:
            arrived(recv1.at[q, 1:], r1.at[q])
        arrived(wfull.at[n, 0:2], rwp.at[n])
        product(n, q)

    stage(0, 0)
    stage(1, 0)
    stage(2, 1)

    def share(q, n):
        k, there = beside(n)
        return copy(recv1.at[q, :, k], rows_all.at[q, quarter], out.at[5], rx, there)

    for q in range(2):
        for n in range(3):
            share(q, n).start()
        rows_all[q, quarter] = recv1[q, :, quarter]

    def unit(n, *place):
        return all3.at[(0 if n < 2 else slice(1, 3), *place, band(2, n % 2))]

    def held(n, z):
        return unit(n, quarter, z)

    last = lines - 1
    at_end = (line == 0) | (line == last)
    inner = jnp.logical_not(at_end)
    beside_end = (line == 1) | (line == last - 1)

    def block(n, z, d, sem, there):
        return copy(held(n, z), held(n, z), sem, r3z.at[n, d - 1], there)

    def spread_out(*which):
        for d in [last - 1] + list(range(1, last - 1)):
            for n in which:
                block(n, line, d, out.at[6], on_line(d)[1]).start()
        for n in which:
            pl.when(inner)(block(n, line, last, out.at[10], on_line(last)[1]).start)
            copy(held(n, line), held(n, line), out.at[7], r3y.at[n], across).start()

    def take_in(n, d):
        z, there = on_line(d)
        block(n, z, d, out.at[6], there).wait_recv()
        if d == last - 1:
            pl.when(beside_end)(block(n, z, last, out.at[11], on_line(1)[1]).start)
        copy(held(n, z), held(n, z), out.at[7], r3y.at[n], across).start()

    def to_partner(n):
        mine = unit(n, quarter, slice(None))
        copy(mine, mine, out.at[8], r3c.at[n], partner).start()

    def from_across(n):
        arrived(unit(n, 0, slice(None)), r3y.at[n])
        other = 2 * (1 - side) + core
        theirs = unit(n, other, slice(None))
        copy(theirs, theirs, out.at[8], r3c.at[n], partner).start()

    gate = summed(0)
    sig = 1.0 / (1.0 + jnp.exp(-gate))
    to_hidden, slope = gate * sig, sig * (1.0 + gate * (1.0 - sig))
    to_gate = []
    for e in range(2):
        up, span = summed(1, e), band(2, e)
        all3[0, quarter, line, span] = (to_hidden[span] * up).astype(BF16)
        spread_out(e)
        to_gate.append(up * slope[span])
    for e in range(2):
        dhidden, span = summed(2, e), band(2, e)
        all3[1, quarter, line, span] = (dhidden * to_gate[e]).astype(BF16)
        all3[2, quarter, line, span] = (dhidden * to_hidden[span]).astype(BF16)
        spread_out(2 + e)

    def finish(n):
        take_in(n, last)
        to_partner(n)

    def output_rows():
        places = [flip(line, d, lines) for d in range(lines)]
        hidden = jnp.concatenate([all3[0, quarter, z] for z in places], axis=0)
        rows = dot(hidden, wfull[2].reshape(line_depth, width), ((1,), (1,))).astype(BF16)
        rows = rows.reshape(lines, members, cap, line_depth)
        for i, z in enumerate(places):
            for m in range(members):
                send4[z * members + m] = rows[i, m]
            for dj in range(0 if i else 1, members):
                member = flip(j, dj, members)
                there = device(z, side, core, member)
                copy(send4.at[z * members + member], recv4.at[j, line], out.at[9], r4, there).start()
        recv4[j, line] = send4[flat]

    far = last - 1

    @pl.when(at_end)
    def _():
        for n in (0, 1):
            for d in range(1, last):
                take_in(n, d)
        for n in (2, 3):
            for d in range(1, far):
                take_in(n, d)
        finish(0)
        finish(1)
        output_rows()
        for n in (2, 3):
            take_in(n, far)
            finish(n)

    @pl.when(inner)
    def _():
        for n in (0, 1):
            for d in range(1, last):
                take_in(n, d)
        finish(0)
        finish(1)
        for n in (2, 3):
            for d in range(1, last):
                take_in(n, d)
        output_rows()
        finish(2)
        finish(3)

    for n in range(4):
        from_across(n)
    arrived(rows_all.at[:, 0:3], rx)
    for n in range(2):
        half_sum[n] = product_of_rows(rows_all, all3, 1 + n, 0, band(2, 1), (core, 2 + core))
    for n in range(2):
        arrived(unit(n, slice(0, 2), slice(None)), r3c.at[n])
    grad_down[...] = product_of_rows(rows_all, all3, 0, 1, slice(0, members * cap), range(4)).astype(BF16)
    arrived(unit(2, slice(0, 2), slice(None)), r3c.at[2])
    for n in range(2):
        half_sum[n] += product_of_rows(rows_all, all3, 1 + n, 0, band(2, 0), range(4))
    arrived(send4.at[1:], r4)
    for z in range(lines):
        out_rows = recv4[0, z].astype(F32)
        for m in range(1, members):
            out_rows += recv4[m, z].astype(F32)
        placed = dot(spread, (out_rows * slot_weight).astype(BF16), ((1,), (0,)))
        mixed[:, z * line_depth : (z + 1) * line_depth] = placed.astype(BF16)
    arrived(unit(3, slice(0, 2), slice(None)), r3c.at[3])

    for n in range(3):
        departed(wfull.at[:, 0], n)
    departed(recv1.at[:, 1:], 3)
    departed(send2.at[:, 1:], 4)
    departed(rows_all.at[:, 0:3], 5)
    departed(all3.at[:, 0, 1:last], 6)
    pl.when(inner)(functools.partial(departed, all3.at[:, 0, 0], 10))
    pl.when(beside_end)(functools.partial(departed, all3.at[:, 0, 0], 11))
    departed(all3.at[:, 0], 7)
    departed(all3.at[:, 0:2], 8)
    departed(send4.at[1:], 9)


def write_out(mixed, grad_down, half_sum, all3, rows_all, mixed_out, gate_out, up_out, down_out, last_two, sems):
    core = lax.rem(lax.axis_index("dp"), 2)
    height = all3.shape[3]
    copies = [
        pltpu.make_async_copy(src, dst, sems.at[n])
        for n, (src, dst) in enumerate(
            ((mixed, mixed_out), (grad_down, down_out), (last_two.at[0], gate_out), (last_two.at[1], up_out))
        )
    ]
    copies[0].start()
    copies[1].start()
    for n in range(2):
        rest = product_of_rows(rows_all, all3, 1 + n, 0, slice(height // 2, height), (1 - core, 3 - core))
        last_two[n] = (half_sum[n] + rest).astype(BF16)
        copies[2 + n].start()
    for c in copies:
        c.wait()


def per_device(lines, members, tokens, cotangent, expert_ids, route_weights, join_groups, w_gate, w_up, w_down):
    tok_count, model = tokens.shape
    depth, width = w_gate.shape
    cap = tok_count // 8
    total = lines * members
    rows = members * cap
    vmem = pl.BlockSpec(memory_space=pltpu.VMEM)
    hbm = pl.BlockSpec(memory_space=pltpu.HBM)
    dma = pltpu.SemaphoreType.DMA
    grad = jax.ShapeDtypeStruct((depth, width), BF16)
    results = pl.pallas_call(
        functools.partial(kernel, lines, members, cap),
        out_shape=(
            pltpu.VMEM((tok_count, model), BF16),
            pltpu.VMEM((depth, width), BF16),
            pltpu.VMEM((2, depth, width), F32),
            pltpu.VMEM((3, 4, lines, rows, width), BF16),
            pltpu.VMEM((2, 4, total, cap, depth), BF16),
        ),
        in_specs=[hbm] * 8,
        out_specs=(vmem,) * 5,
        scratch_shapes=[
            pltpu.SMEM(join_groups.shape, jnp.int32),
            pltpu.VMEM(expert_ids.shape[::-1], jnp.int32),
            pltpu.VMEM(route_weights.shape[::-1], F32),
            pltpu.VMEM((tok_count, model), BF16),
            pltpu.VMEM((tok_count, model), BF16),
            pltpu.VMEM((3, 4, depth, width), BF16),
            pltpu.VMEM((2, lines, 4, cap, depth), BF16),
            pltpu.VMEM((2, total, 4, cap, depth), BF16),
            pltpu.VMEM((3, lines, rows, width), F32),
            pltpu.VMEM((3, lines, rows, width), BF16),
            pltpu.VMEM((3, lines, rows, width), BF16),
            pltpu.VMEM((total, cap, 4 * depth), BF16),
            pltpu.VMEM((members, lines, cap, 4 * depth), BF16),
            dma((6,)), dma((12,)),
            dma((3,)), dma((3,)),
            dma((2,)), dma(()),
            dma((5,)),
            dma((4, lines - 1)), dma((4,)), dma((4,)),
            dma(()),
        ],
        compiler_params=pltpu.CompilerParams(
            collective_id=0, has_side_effects=True, vmem_limit_bytes=44 * 1024 * 1024
        ),
        name="expert_step",
    )(
        *(
            pltpu.with_memory_space_constraint(x, pltpu.HBM)
            for x in (join_groups, tokens, cotangent, expert_ids.T, route_weights.T, w_gate, w_up, w_down)
        )
    )
    return pl.pallas_call(
        write_out,
        out_shape=(jax.ShapeDtypeStruct((tok_count, model), BF16), grad, grad, grad),
        in_specs=[vmem] * 5,
        out_specs=(hbm,) * 4,
        scratch_shapes=[pltpu.VMEM((2, depth, width), BF16), dma((4,))],
        compiler_params=pltpu.CompilerParams(vmem_limit_bytes=16 * 1024 * 1024),
        name="write_out",
    )(*(pltpu.with_memory_space_constraint(r, pltpu.VMEM) for r in results))


def solution(mesh):
    in_specs = (
        P(("dp", "expert"), None),
        P(("dp", "expert"), None),
        P(("dp", "expert"), None),
        P(("dp", "expert"), None),
        P(),
        P("dp", "expert"),
        P("dp", "expert"),
        P("dp", "expert"),
    )
    out_specs = (P(("dp", "expert"), None), P("dp", "expert"), P("dp", "expert"), P("dp", "expert"))
    body = functools.partial(per_device, mesh.shape["dp"] // 4, mesh.shape["expert"])
    return jax.shard_map(body, mesh=mesh, in_specs=in_specs, out_specs=out_specs, check_vma=False)
```

```python
import functools

import jax
import jax.numpy as jnp
from jax import lax
from jax.experimental import pallas as pl
from jax.experimental.pallas import tpu as pltpu
from jax.sharding import PartitionSpec as P

F32, BF16 = jnp.float32, jnp.bfloat16
MESH = pl.DeviceIdType.MESH
SPLIT, FIRST = (1, 2, 2), (0, 1, 3)


def dot(a, b, dims):
    return lax.dot_general(a, b, (dims, ((), ())), preferred_element_type=F32)


def flip(a, d, count):
    out, bit = 0, 1
    while bit < count:
        mine = lax.rem(lax.div(a, bit), 2)
        turn = (d // bit) % 2 if isinstance(d, int) else lax.rem(lax.div(d, bit), 2)
        out += bit * (mine + turn - 2 * mine * turn)
        bit *= 2
    return out


def each(low, high, body):
    if high - low <= 16:
        for i in range(low, high):
            body(i)
    else:
        lax.fori_loop(low, high, lambda i, carry: (body(i), carry)[1], 0)


def product_of_rows(rows_all, all3, n, q, span, quarters):
    lines, height, width = all3.shape[2:]
    count, depth = lines * (span.stop - span.start), rows_all.shape[-1]
    left = [rows_all[q, k].reshape(lines, height, depth)[:, span].reshape(count, depth) for k in quarters]
    right = [all3[n, k, :, span].reshape(count, width) for k in quarters]
    return dot(jnp.concatenate(left, axis=0), jnp.concatenate(right, axis=0), ((0,), (0,)))


def kernel(
    lines, members, cap,
    join, tok, cot, ids, wts, wg, wu, wd,
    mixed, grad_down, half_sum, all3, rows_all,
    joinv, idv, wtv, tokv, cotv, wfull, blk, recv1, part, send2, recv2, send4, recv4,
    local, out, rwy, rwp, r1, rx, r2, r3z, r3y, r3c, r4,
):
    p, j = lax.axis_index("dp"), lax.axis_index("expert")
    line, side, core = lax.div(p, 4), lax.rem(lax.div(p, 2), 2), lax.rem(p, 2)
    quarter = 2 * side + core
    total = lines * members
    flat = line * members + j
    tok_count = tok.shape[0]
    depth, width = wg.shape
    line_depth = 4 * depth

    def device(z, y, c, member):
        return (4 * z + 2 * y + c, member)

    partner = device(line, side, 1 - core, j)
    across = device(line, 1 - side, core, j)

    def copy(src, dst, send, recv, target):
        return pltpu.make_async_remote_copy(
            src_ref=src, dst_ref=dst, send_sem=send, recv_sem=recv, device_id=target, device_id_type=MESH
        )

    def peer(t):
        if isinstance(t, int):
            dz, dj = t // members, t % members
        else:
            dz, dj = lax.div(t, members), lax.rem(t, members)
        return flip(line, dz, lines), flip(j, dj, members)

    def on_line(d):
        z = flip(line, d, lines)
        return z, device(z, side, core, j)

    near = [(0, 1), (1, 0), (1, 1)]

    def beside(n):
        y = 1 - side if near[n][0] else side
        c = 1 - core if near[n][1] else core
        return 2 * y + c, device(line, y, c, j)

    barrier = pltpu.get_barrier_semaphore()

    def greet(t):
        z, member = peer(t)
        pl.semaphore_signal(barrier, inc=1, device_id=device(z, side, core, member), device_id_type=MESH)

    each(1, total, greet)
    slanted = device(flip(line, 1, lines), 1 - side, core, j)
    for there in [beside(n)[1] for n in range(3)] + [slanted]:
        pl.semaphore_signal(barrier, inc=1, device_id=there, device_id_type=MESH)

    loads = [
        pltpu.make_async_copy(src, dst, local.at[n])
        for n, (src, dst) in enumerate(((ids, idv), (wts, wtv), (join, joinv), (tok, tokv), (cot, cotv)))
    ]
    own = [pltpu.make_async_copy(w, wfull.at[n, quarter], local.at[5]) for n, w in enumerate((wg, wu, wd))]
    for load in loads[:3] + own + loads[3:]:
        load.start()
    for load in loads[:2]:
        load.wait()

    chosen = idv[...] == 0
    routed = jnp.max(jnp.where(chosen, 1.0, 0.0), axis=0, keepdims=True)
    weight = jnp.sum(jnp.where(chosen, wtv[...], 0.0), axis=0, keepdims=True)
    upper = lax.broadcasted_iota(jnp.int32, (tok_count, tok_count), 0) <= lax.broadcasted_iota(
        jnp.int32, (tok_count, tok_count), 1
    )
    wide = jnp.broadcast_to(routed, (cap, tok_count))
    places = dot(wide.astype(BF16), jnp.where(upper, 1.0, 0.0).astype(BF16), ((1,), (0,))) - 1.0
    slot = lax.broadcasted_iota(jnp.int32, (cap, tok_count), 0).astype(F32)
    pick = jnp.where((places == slot) & (wide > 0.5), 1.0, 0.0)
    slot_weight = jnp.sum(pick * weight, axis=1, keepdims=True)
    spread = pick.T.astype(BF16)
    pick = pick.astype(BF16)
    loads[2].wait()
    active = 1.0 - joinv[p].astype(F32)
    mine = wfull.at[:, quarter]
    pltpu.make_async_copy(mine, mine, local.at[5]).wait()

    def swap(n):
        return copy(wfull.at[n, quarter], wfull.at[n, quarter], out.at[0], rwy.at[n], across)

    def lend(n):
        return copy(wfull.at[n, quarter], wfull.at[n, quarter], out.at[1], rwp.at[n], partner)

    def relay(n):
        held = wfull.at[n, 2 * (1 - side) + core]
        return copy(held, held, out.at[2], rwp.at[n], partner)

    def give(q, t):
        z, member = peer(t)
        copy(blk.at[q, z], recv1.at[q, flat], out.at[3], r1.at[q], device(z, side, core, member)).start()

    def cut(q, taken):
        for z in range(lines):
            for k in range(4):
                at = z * line_depth + k * depth
                blk[q, z, k] = taken[:, at : at + depth]

    def arrived(ref, recv):
        copy(ref, ref, out.at[0], recv, partner).wait_recv()

    def departed(ref, n):
        copy(ref, ref, out.at[n], rx, partner).wait_send()

    pl.semaphore_wait(barrier, total - 1 + 4)

    swap(0).start()
    loads[3].wait()
    cut(0, dot(pick, tokv[...], ((1,), (0,))).astype(BF16))
    each(1, total, functools.partial(give, 0))
    swap(1).start()
    lend(0).start()
    loads[4].wait()
    cut(1, (dot(pick, cotv[...], ((1,), (0,))) * (slot_weight * active)).astype(BF16))
    swap(2).start()
    each(1, total, functools.partial(give, 1))
    lend(1).start()
    lend(2).start()
    for q in range(2):
        recv1[q, flat] = blk[q, line]

    def product(n, q):
        left = jnp.concatenate([recv1[q, :, k].reshape(total * cap, depth) for k in range(4)], axis=1)
        term = dot(left, wfull[n].reshape(line_depth, width), ((1,), (0,)))
        term = term.reshape(lines, members * cap, width)
        part[n] = term
        send2[n] = term.astype(BF16)
        for e in range(SPLIT[n]):
            span = band(n, e)
            for d in range(1, lines):
                z, there = on_line(d)
                recv = r2.at[FIRST[n] + e]
                copy(send2.at[n, z, span], recv2.at[n, line, span], out.at[4], recv, there).start()

    def band(n, e):
        height = members * cap // SPLIT[n]
        return slice(e * height, (e + 1) * height)

    def summed(n, e=0):
        span = band(n, e)
        arrived(send2.at[n, 1:, span], r2.at[FIRST[n] + e])
        total_rows = part[n, line, span]
        for d in range(1, lines):
            total_rows += recv2[n, on_line(d)[0], span].astype(F32)
        return total_rows

    def stage(n, q):
        swap(n).wait_recv()
        relay(n).start()
        if n != 1:
            arrived(recv1.at[q, 1:], r1.at[q])
        arrived(wfull.at[n, 0:2], rwp.at[n])
        product(n, q)

    stage(0, 0)
    stage(1, 0)
    stage(2, 1)

    def share(q, n):
        k, there = beside(n)
        return copy(recv1.at[q, :, k], rows_all.at[q, quarter], out.at[5], rx, there)

    for q in range(2):
        for n in range(3):
            share(q, n).start()
        rows_all[q, quarter] = recv1[q, :, quarter]

    def unit(n, *place):
        return all3.at[(0 if n < 2 else slice(1, 3), *place, band(2, n % 2))]

    def held(n, z):
        return unit(n, quarter, z)

    last = lines - 1
    at_end = (line == 0) | (line == last)
    inner = jnp.logical_not(at_end)
    beside_end = (line == 1) | (line == last - 1)

    def block(n, z, d, sem, there):
        return copy(held(n, z), held(n, z), sem, r3z.at[n, d - 1], there)

    def spread_out(*which):
        for d in [last - 1] + list(range(1, last - 1)):
            for n in which:
                block(n, line, d, out.at[6], on_line(d)[1]).start()
        for n in which:
            pl.when(inner)(block(n, line, last, out.at[10], on_line(last)[1]).start)
            copy(held(n, line), held(n, line), out.at[14 if n == 3 else 7], r3y.at[n], across).start()

    def take_in(n, d):
        z, there = on_line(d)
        block(n, z, d, out.at[6], there).wait_recv()
        if d == last - 1:
            pl.when(beside_end)(block(n, z, last, out.at[11], on_line(1)[1]).start)
        if n == 3 and d == last - 1:
            pl.when(beside_end)(copy(held(n, z), held(n, z), out.at[13], r3y.at[n], slanted).start)
        if n == 3 and d == last:
            pl.when(inner)(copy(held(n, z), held(n, z), out.at[12], r3y.at[n], across).start)
        else:
            copy(held(n, z), held(n, z), out.at[14 if n == 3 else 7], r3y.at[n], across).start()

    def to_partner(n):
        mine = unit(n, quarter, slice(None))
        copy(mine, mine, out.at[8], r3c.at[n], partner).start()

    def from_across(n):
        arrived(unit(n, 0, slice(None)), r3y.at[n])
        other = 2 * (1 - side) + core
        theirs = unit(n, other, slice(None))
        copy(theirs, theirs, out.at[8], r3c.at[n], partner).start()

    gate = summed(0)
    sig = 1.0 / (1.0 + jnp.exp(-gate))
    to_hidden, slope = gate * sig, sig * (1.0 + gate * (1.0 - sig))
    to_gate = []
    for e in range(2):
        up, span = summed(1, e), band(2, e)
        all3[0, quarter, line, span] = (to_hidden[span] * up).astype(BF16)
        spread_out(e)
        to_gate.append(up * slope[span])
    for e in range(2):
        dhidden, span = summed(2, e), band(2, e)
        all3[1, quarter, line, span] = (dhidden * to_gate[e]).astype(BF16)
        all3[2, quarter, line, span] = (dhidden * to_hidden[span]).astype(BF16)
        spread_out(2 + e)

    def finish(n):
        take_in(n, last)
        to_partner(n)

    def output_rows():
        places = [flip(line, d, lines) for d in range(lines)]
        hidden = jnp.concatenate([all3[0, quarter, z] for z in places], axis=0)
        rows = dot(hidden, wfull[2].reshape(line_depth, width), ((1,), (1,))).astype(BF16)
        rows = rows.reshape(lines, members, cap, line_depth)
        for i, z in enumerate(places):
            for m in range(members):
                send4[z * members + m] = rows[i, m]
            for dj in range(0 if i else 1, members):
                member = flip(j, dj, members)
                there = device(z, side, core, member)
                copy(send4.at[z * members + member], recv4.at[j, line], out.at[9], r4, there).start()
        recv4[j, line] = send4[flat]

    far = last - 1

    @pl.when(at_end)
    def _():
        for n in (0, 1):
            for d in range(1, last):
                take_in(n, d)
        for n in (2, 3):
            for d in range(1, far):
                take_in(n, d)
        finish(0)
        finish(1)
        output_rows()
        for n in (2, 3):
            take_in(n, far)
            finish(n)

    @pl.when(inner)
    def _():
        for n in (0, 1):
            for d in range(1, last):
                take_in(n, d)
        finish(0)
        finish(1)
        for n in (2, 3):
            for d in range(1, last):
                take_in(n, d)
        output_rows()
        finish(2)
        finish(3)

    for n in range(4):
        from_across(n)
    arrived(rows_all.at[:, 0:3], rx)
    for n in range(2):
        half_sum[n] = product_of_rows(rows_all, all3, 1 + n, 0, band(2, 1), (core, 2 + core))
    for n in range(2):
        arrived(unit(n, slice(0, 2), slice(None)), r3c.at[n])
    grad_down[...] = product_of_rows(rows_all, all3, 0, 1, slice(0, members * cap), range(4)).astype(BF16)
    arrived(unit(2, slice(0, 2), slice(None)), r3c.at[2])
    for n in range(2):
        half_sum[n] += product_of_rows(rows_all, all3, 1 + n, 0, band(2, 0), range(4))
    arrived(send4.at[1:], r4)
    for z in range(lines):
        out_rows = recv4[0, z].astype(F32)
        for m in range(1, members):
            out_rows += recv4[m, z].astype(F32)
        placed = dot(spread, (out_rows * slot_weight).astype(BF16), ((1,), (0,)))
        mixed[:, z * line_depth : (z + 1) * line_depth] = placed.astype(BF16)
    arrived(unit(3, slice(0, 2), slice(None)), r3c.at[3])

    for n in range(3):
        departed(wfull.at[:, 0], n)
    departed(recv1.at[:, 1:], 3)
    departed(send2.at[:, 1:], 4)
    departed(rows_all.at[:, 0:3], 5)
    departed(all3.at[:, 0, 1:last], 6)
    pl.when(inner)(functools.partial(departed, all3.at[:, 0, 0], 10))
    pl.when(beside_end)(functools.partial(departed, all3.at[:, 0, 0], 11))
    departed(all3.at[0:2, 0], 7)
    departed(all3.at[0, 0, 1:], 14)
    pl.when(inner)(functools.partial(departed, all3.at[0, 0, 0], 12))
    pl.when(beside_end)(functools.partial(departed, all3.at[0, 0, 0], 13))
    departed(all3.at[:, 0:2], 8)
    departed(send4.at[1:], 9)


def write_out(mixed, grad_down, half_sum, all3, rows_all, mixed_out, gate_out, up_out, down_out, last_two, sems):
    core = lax.rem(lax.axis_index("dp"), 2)
    height = all3.shape[3]
    copies = [
        pltpu.make_async_copy(src, dst, sems.at[n])
        for n, (src, dst) in enumerate(
            ((mixed, mixed_out), (grad_down, down_out), (last_two.at[0], gate_out), (last_two.at[1], up_out))
        )
    ]
    copies[0].start()
    copies[1].start()
    for n in range(2):
        rest = product_of_rows(rows_all, all3, 1 + n, 0, slice(height // 2, height), (1 - core, 3 - core))
        last_two[n] = (half_sum[n] + rest).astype(BF16)
        copies[2 + n].start()
    for c in copies:
        c.wait()


def per_device(lines, members, tokens, cotangent, expert_ids, route_weights, join_groups, w_gate, w_up, w_down):
    tok_count, model = tokens.shape
    depth, width = w_gate.shape
    cap = tok_count // 8
    total = lines * members
    rows = members * cap
    vmem = pl.BlockSpec(memory_space=pltpu.VMEM)
    hbm = pl.BlockSpec(memory_space=pltpu.HBM)
    dma = pltpu.SemaphoreType.DMA
    grad = jax.ShapeDtypeStruct((depth, width), BF16)
    results = pl.pallas_call(
        functools.partial(kernel, lines, members, cap),
        out_shape=(
            pltpu.VMEM((tok_count, model), BF16),
            pltpu.VMEM((depth, width), BF16),
            pltpu.VMEM((2, depth, width), F32),
            pltpu.VMEM((3, 4, lines, rows, width), BF16),
            pltpu.VMEM((2, 4, total, cap, depth), BF16),
        ),
        in_specs=[hbm] * 8,
        out_specs=(vmem,) * 5,
        scratch_shapes=[
            pltpu.SMEM(join_groups.shape, jnp.int32),
            pltpu.VMEM(expert_ids.shape[::-1], jnp.int32),
            pltpu.VMEM(route_weights.shape[::-1], F32),
            pltpu.VMEM((tok_count, model), BF16),
            pltpu.VMEM((tok_count, model), BF16),
            pltpu.VMEM((3, 4, depth, width), BF16),
            pltpu.VMEM((2, lines, 4, cap, depth), BF16),
            pltpu.VMEM((2, total, 4, cap, depth), BF16),
            pltpu.VMEM((3, lines, rows, width), F32),
            pltpu.VMEM((3, lines, rows, width), BF16),
            pltpu.VMEM((3, lines, rows, width), BF16),
            pltpu.VMEM((total, cap, 4 * depth), BF16),
            pltpu.VMEM((members, lines, cap, 4 * depth), BF16),
            dma((6,)), dma((15,)),
            dma((3,)), dma((3,)),
            dma((2,)), dma(()),
            dma((5,)),
            dma((4, lines - 1)), dma((4,)), dma((4,)),
            dma(()),
        ],
        compiler_params=pltpu.CompilerParams(
            collective_id=0, has_side_effects=True, vmem_limit_bytes=44 * 1024 * 1024
        ),
        name="expert_step",
    )(
        *(
            pltpu.with_memory_space_constraint(x, pltpu.HBM)
            for x in (join_groups, tokens, cotangent, expert_ids.T, route_weights.T, w_gate, w_up, w_down)
        )
    )
    return pl.pallas_call(
        write_out,
        out_shape=(jax.ShapeDtypeStruct((tok_count, model), BF16), grad, grad, grad),
        in_specs=[vmem] * 5,
        out_specs=(hbm,) * 4,
        scratch_shapes=[pltpu.VMEM((2, depth, width), BF16), dma((4,))],
        compiler_params=pltpu.CompilerParams(vmem_limit_bytes=16 * 1024 * 1024),
        name="write_out",
    )(*(pltpu.with_memory_space_constraint(r, pltpu.VMEM) for r in results))


def solution(mesh):
    in_specs = (
        P(("dp", "expert"), None),
        P(("dp", "expert"), None),
        P(("dp", "expert"), None),
        P(("dp", "expert"), None),
        P(),
        P("dp", "expert"),
        P("dp", "expert"),
        P("dp", "expert"),
    )
    out_specs = (P(("dp", "expert"), None), P("dp", "expert"), P("dp", "expert"), P("dp", "expert"))
    body = functools.partial(per_device, mesh.shape["dp"] // 4, mesh.shape["expert"])
    return jax.shard_map(body, mesh=mesh, in_specs=in_specs, out_specs=out_specs, check_vma=False)
```

```python
import functools

import jax
import jax.numpy as jnp
from jax import lax
from jax.experimental import pallas as pl
from jax.experimental.pallas import tpu as pltpu
from jax.sharding import PartitionSpec as P

F32, BF16 = jnp.float32, jnp.bfloat16
MESH = pl.DeviceIdType.MESH
SPLIT, FIRST = (1, 2, 2), (0, 1, 3)


def dot(a, b, dims):
    return lax.dot_general(a, b, (dims, ((), ())), preferred_element_type=F32)


def flip(a, d, count):
    out, bit = 0, 1
    while bit < count:
        mine = lax.rem(lax.div(a, bit), 2)
        turn = (d // bit) % 2 if isinstance(d, int) else lax.rem(lax.div(d, bit), 2)
        out += bit * (mine + turn - 2 * mine * turn)
        bit *= 2
    return out


def each(low, high, body):
    if high - low <= 16:
        for i in range(low, high):
            body(i)
    else:
        lax.fori_loop(low, high, lambda i, carry: (body(i), carry)[1], 0)


def product_of_rows(rows_all, all3, n, q, span, quarters):
    lines, height, width = all3.shape[2:]
    count, depth = lines * (span.stop - span.start), rows_all.shape[-1]
    left = [rows_all[q, k].reshape(lines, height, depth)[:, span].reshape(count, depth) for k in quarters]
    right = [all3[n, k, :, span].reshape(count, width) for k in quarters]
    return dot(jnp.concatenate(left, axis=0), jnp.concatenate(right, axis=0), ((0,), (0,)))


def kernel(
    lines, members, cap,
    join, tok, cot, ids, wts, wg, wu, wd,
    mixed, grad_down, half_sum, all3, rows_all,
    joinv, idv, wtv, tokv, cotv, wfull, blk, recv1, part, send2, recv2, send4, recv4,
    local, out, rwy, rwp, r1, rx, r2, r3z, r3y, r3c, r4,
):
    p, j = lax.axis_index("dp"), lax.axis_index("expert")
    line, side, core = lax.div(p, 4), lax.rem(lax.div(p, 2), 2), lax.rem(p, 2)
    quarter = 2 * side + core
    total = lines * members
    flat = line * members + j
    tok_count = tok.shape[0]
    depth, width = wg.shape
    line_depth = 4 * depth

    def device(z, y, c, member):
        return (4 * z + 2 * y + c, member)

    partner = device(line, side, 1 - core, j)
    across = device(line, 1 - side, core, j)

    def copy(src, dst, send, recv, target):
        return pltpu.make_async_remote_copy(
            src_ref=src, dst_ref=dst, send_sem=send, recv_sem=recv, device_id=target, device_id_type=MESH
        )

    def peer(t):
        if isinstance(t, int):
            dz, dj = t // members, t % members
        else:
            dz, dj = lax.div(t, members), lax.rem(t, members)
        return flip(line, dz, lines), flip(j, dj, members)

    def on_line(d):
        z = flip(line, d, lines)
        return z, device(z, side, core, j)

    near = [(0, 1), (1, 0), (1, 1)]

    def beside(n):
        y = 1 - side if near[n][0] else side
        c = 1 - core if near[n][1] else core
        return 2 * y + c, device(line, y, c, j)

    barrier = pltpu.get_barrier_semaphore()

    def greet(t):
        z, member = peer(t)
        pl.semaphore_signal(barrier, inc=1, device_id=device(z, side, core, member), device_id_type=MESH)

    each(1, total, greet)
    slanted = device(flip(line, 1, lines), 1 - side, core, j)
    for there in [beside(n)[1] for n in range(3)] + [slanted]:
        pl.semaphore_signal(barrier, inc=1, device_id=there, device_id_type=MESH)

    loads = [
        pltpu.make_async_copy(src, dst, local.at[n])
        for n, (src, dst) in enumerate(((ids, idv), (wts, wtv), (join, joinv), (tok, tokv), (cot, cotv)))
    ]
    own = [pltpu.make_async_copy(w, wfull.at[n, quarter], local.at[5]) for n, w in enumerate((wg, wu, wd))]
    for load in loads[:3] + own + loads[3:]:
        load.start()
    for load in loads[:2]:
        load.wait()

    chosen = idv[...] == 0
    routed = jnp.max(jnp.where(chosen, 1.0, 0.0), axis=0, keepdims=True)
    weight = jnp.sum(jnp.where(chosen, wtv[...], 0.0), axis=0, keepdims=True)
    upper = lax.broadcasted_iota(jnp.int32, (tok_count, tok_count), 0) <= lax.broadcasted_iota(
        jnp.int32, (tok_count, tok_count), 1
    )
    wide = jnp.broadcast_to(routed, (cap, tok_count))
    places = dot(wide.astype(BF16), jnp.where(upper, 1.0, 0.0).astype(BF16), ((1,), (0,))) - 1.0
    slot = lax.broadcasted_iota(jnp.int32, (cap, tok_count), 0).astype(F32)
    pick = jnp.where((places == slot) & (wide > 0.5), 1.0, 0.0)
    slot_weight = jnp.sum(pick * weight, axis=1, keepdims=True)
    spread = pick.T.astype(BF16)
    pick = pick.astype(BF16)
    loads[2].wait()
    active = 1.0 - joinv[p].astype(F32)
    mine = wfull.at[:, quarter]
    pltpu.make_async_copy(mine, mine, local.at[5]).wait()

    def swap(n):
        return copy(wfull.at[n, quarter], wfull.at[n, quarter], out.at[0], rwy.at[n], across)

    def lend(n):
        return copy(wfull.at[n, quarter], wfull.at[n, quarter], out.at[1], rwp.at[n], partner)

    def relay(n):
        held = wfull.at[n, 2 * (1 - side) + core]
        return copy(held, held, out.at[2], rwp.at[n], partner)

    def give(q, t):
        z, member = peer(t)
        copy(blk.at[q, z], recv1.at[q, flat], out.at[3], r1.at[q], device(z, side, core, member)).start()

    def cut(q, taken):
        for z in range(lines):
            for k in range(4):
                at = z * line_depth + k * depth
                blk[q, z, k] = taken[:, at : at + depth]

    def arrived(ref, recv):
        copy(ref, ref, out.at[0], recv, partner).wait_recv()

    def departed(ref, n):
        copy(ref, ref, out.at[n], rx, partner).wait_send()

    pl.semaphore_wait(barrier, total - 1 + 4)

    swap(0).start()
    loads[3].wait()
    cut(0, dot(pick, tokv[...], ((1,), (0,))).astype(BF16))
    each(1, total, functools.partial(give, 0))
    swap(1).start()
    lend(0).start()
    loads[4].wait()
    cut(1, (dot(pick, cotv[...], ((1,), (0,))) * (slot_weight * active)).astype(BF16))
    swap(2).start()
    each(1, total, functools.partial(give, 1))
    lend(1).start()
    lend(2).start()
    for q in range(2):
        recv1[q, flat] = blk[q, line]

    def product(n, q):
        left = jnp.concatenate([recv1[q, :, k].reshape(total * cap, depth) for k in range(4)], axis=1)
        term = dot(left, wfull[n].reshape(line_depth, width), ((1,), (0,)))
        term = term.reshape(lines, members * cap, width)
        part[n] = term
        send2[n] = term.astype(BF16)
        for e in range(SPLIT[n]):
            span = band(n, e)
            for d in range(1, lines):
                z, there = on_line(d)
                recv = r2.at[FIRST[n] + e]
                copy(send2.at[n, z, span], recv2.at[n, line, span], out.at[4], recv, there).start()

    def band(n, e):
        height = members * cap // SPLIT[n]
        return slice(e * height, (e + 1) * height)

    def summed(n, e=0):
        span = band(n, e)
        arrived(send2.at[n, 1:, span], r2.at[FIRST[n] + e])
        total_rows = part[n, line, span]
        for d in range(1, lines):
            total_rows += recv2[n, on_line(d)[0], span].astype(F32)
        return total_rows

    def stage(n, q):
        swap(n).wait_recv()
        relay(n).start()
        if n != 1:
            arrived(recv1.at[q, 1:], r1.at[q])
        arrived(wfull.at[n, 0:2], rwp.at[n])
        product(n, q)

    stage(0, 0)
    stage(1, 0)
    stage(2, 1)

    def share(q, n):
        k, there = beside(n)
        return copy(recv1.at[q, :, k], rows_all.at[q, quarter], out.at[5], rx, there)

    for q in range(2):
        for n in range(3):
            share(q, n).start()
        rows_all[q, quarter] = recv1[q, :, quarter]

    def unit(n, *place):
        return all3.at[(0 if n < 2 else slice(1, 3), *place, band(2, n % 2))]

    def held(n, z):
        return unit(n, quarter, z)

    last = lines - 1
    at_end = (line == 0) | (line == last)
    inner = jnp.logical_not(at_end)
    beside_end = (line == 1) | (line == last - 1)

    def block(n, z, d, sem, there):
        return copy(held(n, z), held(n, z), sem, r3z.at[n, d - 1], there)

    def spread_out(*which):
        for d in [last - 1] + list(range(1, last - 1)):
            for n in which:
                block(n, line, d, out.at[6], on_line(d)[1]).start()
        for n in which:
            pl.when(inner)(block(n, line, last, out.at[10], on_line(last)[1]).start)
            copy(held(n, line), held(n, line), out.at[14 if n >= 2 else 7], r3y.at[n], across).start()

    def take_in(n, d):
        z, there = on_line(d)
        block(n, z, d, out.at[6], there).wait_recv()
        if d == last - 1:
            pl.when(beside_end)(block(n, z, last, out.at[11], on_line(1)[1]).start)
        if n >= 2 and d == last - 1:
            pl.when(beside_end)(copy(held(n, z), held(n, z), out.at[13], r3y.at[n], slanted).start)
        if n >= 2 and d == last:
            pl.when(inner)(copy(held(n, z), held(n, z), out.at[12], r3y.at[n], across).start)
        else:
            copy(held(n, z), held(n, z), out.at[14 if n >= 2 else 7], r3y.at[n], across).start()

    def to_partner(n):
        mine = unit(n, quarter, slice(None))
        copy(mine, mine, out.at[8], r3c.at[n], partner).start()

    def from_across(n):
        arrived(unit(n, 0, slice(None)), r3y.at[n])
        other = 2 * (1 - side) + core
        theirs = unit(n, other, slice(None))
        copy(theirs, theirs, out.at[8], r3c.at[n], partner).start()

    gate = summed(0)
    sig = 1.0 / (1.0 + jnp.exp(-gate))
    to_hidden, slope = gate * sig, sig * (1.0 + gate * (1.0 - sig))
    to_gate = []
    for e in range(2):
        up, span = summed(1, e), band(2, e)
        all3[0, quarter, line, span] = (to_hidden[span] * up).astype(BF16)
        spread_out(e)
        to_gate.append(up * slope[span])
    for e in range(2):
        dhidden, span = summed(2, e), band(2, e)
        all3[1, quarter, line, span] = (dhidden * to_gate[e]).astype(BF16)
        all3[2, quarter, line, span] = (dhidden * to_hidden[span]).astype(BF16)
        spread_out(2 + e)

    def finish(n):
        take_in(n, last)
        to_partner(n)

    def output_rows():
        places = [flip(line, d, lines) for d in range(lines)]
        hidden = jnp.concatenate([all3[0, quarter, z] for z in places], axis=0)
        rows = dot(hidden, wfull[2].reshape(line_depth, width), ((1,), (1,))).astype(BF16)
        rows = rows.reshape(lines, members, cap, line_depth)
        for i, z in enumerate(places):
            for m in range(members):
                send4[z * members + m] = rows[i, m]
            for dj in range(0 if i else 1, members):
                member = flip(j, dj, members)
                there = device(z, side, core, member)
                copy(send4.at[z * members + member], recv4.at[j, line], out.at[9], r4, there).start()
        recv4[j, line] = send4[flat]

    far = last - 1

    @pl.when(at_end)
    def _():
        for n in (0, 1):
            for d in range(1, last):
                take_in(n, d)
        for n in (2, 3):
            for d in range(1, far):
                take_in(n, d)
        finish(0)
        finish(1)
        output_rows()
        for n in (2, 3):
            take_in(n, far)
            finish(n)

    @pl.when(inner)
    def _():
        for n in (0, 1):
            for d in range(1, last):
                take_in(n, d)
        finish(0)
        finish(1)
        for n in (2, 3):
            for d in range(1, last):
                take_in(n, d)
        output_rows()
        finish(2)
        finish(3)

    for n in range(4):
        from_across(n)
    arrived(rows_all.at[:, 0:3], rx)
    for n in range(2):
        half_sum[n] = product_of_rows(rows_all, all3, 1 + n, 0, band(2, 1), (core, 2 + core))
    for n in range(2):
        arrived(unit(n, slice(0, 2), slice(None)), r3c.at[n])
    grad_down[...] = product_of_rows(rows_all, all3, 0, 1, slice(0, members * cap), range(4)).astype(BF16)
    arrived(unit(2, slice(0, 2), slice(None)), r3c.at[2])
    for n in range(2):
        half_sum[n] += product_of_rows(rows_all, all3, 1 + n, 0, band(2, 0), range(4))
    arrived(send4.at[1:], r4)
    for z in range(lines):
        out_rows = recv4[0, z].astype(F32)
        for m in range(1, members):
            out_rows += recv4[m, z].astype(F32)
        placed = dot(spread, (out_rows * slot_weight).astype(BF16), ((1,), (0,)))
        mixed[:, z * line_depth : (z + 1) * line_depth] = placed.astype(BF16)
    arrived(unit(3, slice(0, 2), slice(None)), r3c.at[3])

    for n in range(3):
        departed(wfull.at[:, 0], n)
    departed(recv1.at[:, 1:], 3)
    departed(send2.at[:, 1:], 4)
    departed(rows_all.at[:, 0:3], 5)
    departed(all3.at[:, 0, 1:last], 6)
    pl.when(inner)(functools.partial(departed, all3.at[:, 0, 0], 10))
    pl.when(beside_end)(functools.partial(departed, all3.at[:, 0, 0], 11))
    departed(all3.at[0, 0], 7)
    departed(all3.at[0:2, 0, 1:], 14)
    pl.when(inner)(functools.partial(departed, all3.at[0:2, 0, 0], 12))
    pl.when(beside_end)(functools.partial(departed, all3.at[0:2, 0, 0], 13))
    departed(all3.at[:, 0:2], 8)
    departed(send4.at[1:], 9)


def write_out(mixed, grad_down, half_sum, all3, rows_all, mixed_out, gate_out, up_out, down_out, last_two, sems):
    core = lax.rem(lax.axis_index("dp"), 2)
    height = all3.shape[3]
    copies = [
        pltpu.make_async_copy(src, dst, sems.at[n])
        for n, (src, dst) in enumerate(
            ((mixed, mixed_out), (grad_down, down_out), (last_two.at[0], gate_out), (last_two.at[1], up_out))
        )
    ]
    copies[0].start()
    copies[1].start()
    for n in range(2):
        rest = product_of_rows(rows_all, all3, 1 + n, 0, slice(height // 2, height), (1 - core, 3 - core))
        last_two[n] = (half_sum[n] + rest).astype(BF16)
        copies[2 + n].start()
    for c in copies:
        c.wait()


def per_device(lines, members, tokens, cotangent, expert_ids, route_weights, join_groups, w_gate, w_up, w_down):
    tok_count, model = tokens.shape
    depth, width = w_gate.shape
    cap = tok_count // 8
    total = lines * members
    rows = members * cap
    vmem = pl.BlockSpec(memory_space=pltpu.VMEM)
    hbm = pl.BlockSpec(memory_space=pltpu.HBM)
    dma = pltpu.SemaphoreType.DMA
    grad = jax.ShapeDtypeStruct((depth, width), BF16)
    results = pl.pallas_call(
        functools.partial(kernel, lines, members, cap),
        out_shape=(
            pltpu.VMEM((tok_count, model), BF16),
            pltpu.VMEM((depth, width), BF16),
            pltpu.VMEM((2, depth, width), F32),
            pltpu.VMEM((3, 4, lines, rows, width), BF16),
            pltpu.VMEM((2, 4, total, cap, depth), BF16),
        ),
        in_specs=[hbm] * 8,
        out_specs=(vmem,) * 5,
        scratch_shapes=[
            pltpu.SMEM(join_groups.shape, jnp.int32),
            pltpu.VMEM(expert_ids.shape[::-1], jnp.int32),
            pltpu.VMEM(route_weights.shape[::-1], F32),
            pltpu.VMEM((tok_count, model), BF16),
            pltpu.VMEM((tok_count, model), BF16),
            pltpu.VMEM((3, 4, depth, width), BF16),
            pltpu.VMEM((2, lines, 4, cap, depth), BF16),
            pltpu.VMEM((2, total, 4, cap, depth), BF16),
            pltpu.VMEM((3, lines, rows, width), F32),
            pltpu.VMEM((3, lines, rows, width), BF16),
            pltpu.VMEM((3, lines, rows, width), BF16),
            pltpu.VMEM((total, cap, 4 * depth), BF16),
            pltpu.VMEM((members, lines, cap, 4 * depth), BF16),
            dma((6,)), dma((15,)),
            dma((3,)), dma((3,)),
            dma((2,)), dma(()),
            dma((5,)),
            dma((4, lines - 1)), dma((4,)), dma((4,)),
            dma(()),
        ],
        compiler_params=pltpu.CompilerParams(
            collective_id=0, has_side_effects=True, vmem_limit_bytes=44 * 1024 * 1024
        ),
        name="expert_step",
    )(
        *(
            pltpu.with_memory_space_constraint(x, pltpu.HBM)
            for x in (join_groups, tokens, cotangent, expert_ids.T, route_weights.T, w_gate, w_up, w_down)
        )
    )
    return pl.pallas_call(
        write_out,
        out_shape=(jax.ShapeDtypeStruct((tok_count, model), BF16), grad, grad, grad),
        in_specs=[vmem] * 5,
        out_specs=(hbm,) * 4,
        scratch_shapes=[pltpu.VMEM((2, depth, width), BF16), dma((4,))],
        compiler_params=pltpu.CompilerParams(vmem_limit_bytes=16 * 1024 * 1024),
        name="write_out",
    )(*(pltpu.with_memory_space_constraint(r, pltpu.VMEM) for r in results))


def solution(mesh):
    in_specs = (
        P(("dp", "expert"), None),
        P(("dp", "expert"), None),
        P(("dp", "expert"), None),
        P(("dp", "expert"), None),
        P(),
        P("dp", "expert"),
        P("dp", "expert"),
        P("dp", "expert"),
    )
    out_specs = (P(("dp", "expert"), None), P("dp", "expert"), P("dp", "expert"), P("dp", "expert"))
    body = functools.partial(per_device, mesh.shape["dp"] // 4, mesh.shape["expert"])
    return jax.shard_map(body, mesh=mesh, in_specs=in_specs, out_specs=out_specs, check_vma=False)
```

```python
import functools

import jax
import jax.numpy as jnp
from jax import lax
from jax.experimental import pallas as pl
from jax.experimental.pallas import tpu as pltpu
from jax.sharding import PartitionSpec as P

F32, BF16 = jnp.float32, jnp.bfloat16
MESH = pl.DeviceIdType.MESH
SPLIT, FIRST = (1, 2, 2), (0, 1, 3)


def dot(a, b, dims):
    return lax.dot_general(a, b, (dims, ((), ())), preferred_element_type=F32)


def flip(a, d, count):
    out, bit = 0, 1
    while bit < count:
        mine = lax.rem(lax.div(a, bit), 2)
        turn = (d // bit) % 2 if isinstance(d, int) else lax.rem(lax.div(d, bit), 2)
        out += bit * (mine + turn - 2 * mine * turn)
        bit *= 2
    return out


def each(low, high, body):
    if high - low <= 16:
        for i in range(low, high):
            body(i)
    else:
        lax.fori_loop(low, high, lambda i, carry: (body(i), carry)[1], 0)


def product_of_rows(rows_all, all3, n, q, span, quarters):
    lines, height, width = all3.shape[2:]
    count, depth = lines * (span.stop - span.start), rows_all.shape[-1]
    left = [rows_all[q, k].reshape(lines, height, depth)[:, span].reshape(count, depth) for k in quarters]
    right = [all3[n, k, :, span].reshape(count, width) for k in quarters]
    return dot(jnp.concatenate(left, axis=0), jnp.concatenate(right, axis=0), ((0,), (0,)))


def kernel(
    lines, members, cap,
    join, tok, cot, ids, wts, wg, wu, wd,
    mixed, grad_down, half_sum, all3, rows_all,
    joinv, idv, wtv, tokv, cotv, wfull, blk, recv1, part, send2, recv2, send4, recv4,
    local, out, rwy, rwp, r1, rx, r2, r3z, r3y, r3c, r4,
):
    p, j = lax.axis_index("dp"), lax.axis_index("expert")
    line, side, core = lax.div(p, 4), lax.rem(lax.div(p, 2), 2), lax.rem(p, 2)
    quarter = 2 * side + core
    total = lines * members
    flat = line * members + j
    tok_count = tok.shape[0]
    depth, width = wg.shape
    line_depth = 4 * depth

    def device(z, y, c, member):
        return (4 * z + 2 * y + c, member)

    partner = device(line, side, 1 - core, j)
    across = device(line, 1 - side, core, j)

    def copy(src, dst, send, recv, target):
        return pltpu.make_async_remote_copy(
            src_ref=src, dst_ref=dst, send_sem=send, recv_sem=recv, device_id=target, device_id_type=MESH
        )

    def peer(t):
        if isinstance(t, int):
            dz, dj = t // members, t % members
        else:
            dz, dj = lax.div(t, members), lax.rem(t, members)
        return flip(line, dz, lines), flip(j, dj, members)

    def on_line(d):
        z = flip(line, d, lines)
        return z, device(z, side, core, j)

    near = [(0, 1), (1, 0), (1, 1)]

    def beside(n):
        y = 1 - side if near[n][0] else side
        c = 1 - core if near[n][1] else core
        return 2 * y + c, device(line, y, c, j)

    barrier = pltpu.get_barrier_semaphore()

    def greet(t):
        z, member = peer(t)
        pl.semaphore_signal(barrier, inc=1, device_id=device(z, side, core, member), device_id_type=MESH)

    each(1, total, lambda t: greet(total - t))
    slanted = device(flip(line, 1, lines), 1 - side, core, j)
    for there in [beside(n)[1] for n in range(3)] + [slanted]:
        pl.semaphore_signal(barrier, inc=1, device_id=there, device_id_type=MESH)

    loads = [
        pltpu.make_async_copy(src, dst, local.at[n])
        for n, (src, dst) in enumerate(((ids, idv), (wts, wtv), (join, joinv), (tok, tokv), (cot, cotv)))
    ]
    own = [pltpu.make_async_copy(w, wfull.at[n, quarter], local.at[5]) for n, w in enumerate((wg, wu, wd))]
    for load in loads[:3] + own + loads[3:]:
        load.start()
    for load in loads[:2]:
        load.wait()

    chosen = idv[...] == 0
    routed = jnp.max(jnp.where(chosen, 1.0, 0.0), axis=0, keepdims=True)
    weight = jnp.sum(jnp.where(chosen, wtv[...], 0.0), axis=0, keepdims=True)
    upper = lax.broadcasted_iota(jnp.int32, (tok_count, tok_count), 0) <= lax.broadcasted_iota(
        jnp.int32, (tok_count, tok_count), 1
    )
    wide = jnp.broadcast_to(routed, (cap, tok_count))
    places = dot(wide.astype(BF16), jnp.where(upper, 1.0, 0.0).astype(BF16), ((1,), (0,))) - 1.0
    slot = lax.broadcasted_iota(jnp.int32, (cap, tok_count), 0).astype(F32)
    pick = jnp.where((places == slot) & (wide > 0.5), 1.0, 0.0)
    slot_weight = jnp.sum(pick * weight, axis=1, keepdims=True)
    spread = pick.T.astype(BF16)
    pick = pick.astype(BF16)
    loads[2].wait()
    active = 1.0 - joinv[p].astype(F32)
    mine = wfull.at[:, quarter]
    pltpu.make_async_copy(mine, mine, local.at[5]).wait()

    def swap(n):
        return copy(wfull.at[n, quarter], wfull.at[n, quarter], out.at[0], rwy.at[n], across)

    def lend(n):
        return copy(wfull.at[n, quarter], wfull.at[n, quarter], out.at[0], rwp.at[n], partner)

    def relay(n):
        held = wfull.at[n, 2 * (1 - side) + core]
        return copy(held, held, out.at[0], rwp.at[n], partner)

    def give(q, t):
        z, member = peer(t)
        copy(blk.at[q, z], recv1.at[q, flat], out.at[3], r1.at[q], device(z, side, core, member)).start()

    def cut(q, taken):
        for z in range(lines):
            for k in range(4):
                at = z * line_depth + k * depth
                blk[q, z, k] = taken[:, at : at + depth]

    def arrived(ref, recv):
        copy(ref, ref, out.at[0], recv, partner).wait_recv()

    def departed(ref, n):
        copy(ref, ref, out.at[n], rx, partner).wait_send()

    pl.semaphore_wait(barrier, total - 1 + 4)

    swap(0).start()
    loads[3].wait()
    cut(0, dot(pick, tokv[...], ((1,), (0,))).astype(BF16))
    each(1, total, functools.partial(give, 0))
    swap(1).start()
    lend(0).start()
    loads[4].wait()
    cut(1, (dot(pick, cotv[...], ((1,), (0,))) * (slot_weight * active)).astype(BF16))
    swap(2).start()
    each(1, total, functools.partial(give, 1))
    lend(1).start()
    lend(2).start()
    for q in range(2):
        recv1[q, flat] = blk[q, line]

    def product(n, q):
        left = jnp.concatenate([recv1[q, :, k].reshape(total * cap, depth) for k in range(4)], axis=1)
        term = dot(left, wfull[n].reshape(line_depth, width), ((1,), (0,)))
        term = term.reshape(lines, members * cap, width)
        part[n] = term
        send2[n] = term.astype(BF16)
        for e in range(SPLIT[n]):
            span = band(n, e)
            for d in range(1, lines):
                z, there = on_line(d)
                recv = r2.at[FIRST[n] + e]
                copy(send2.at[n, z, span], recv2.at[n, line, span], out.at[4], recv, there).start()

    def band(n, e):
        height = members * cap // SPLIT[n]
        return slice(e * height, (e + 1) * height)

    def summed(n, e=0):
        span = band(n, e)
        arrived(send2.at[n, 1:, span], r2.at[FIRST[n] + e])
        total_rows = part[n, line, span]
        for d in range(1, lines):
            total_rows += recv2[n, on_line(d)[0], span].astype(F32)
        return total_rows

    def stage(n, q):
        swap(n).wait_recv()
        relay(n).start()
        if n != 1:
            arrived(recv1.at[q, 1:], r1.at[q])
        arrived(wfull.at[n, 0:2], rwp.at[n])
        product(n, q)

    stage(0, 0)
    stage(1, 0)
    stage(2, 1)

    def share(q, n):
        k, there = beside(n)
        return copy(recv1.at[q, :, k], rows_all.at[q, quarter], out.at[5], rx, there)

    for q in range(2):
        for n in range(3):
            share(q, n).start()
        rows_all[q, quarter] = recv1[q, :, quarter]

    def unit(n, *place):
        return all3.at[(0 if n < 2 else slice(1, 3), *place, band(2, n % 2))]

    def held(n, z):
        return unit(n, quarter, z)

    last = lines - 1
    at_end = (line == 0) | (line == last)
    inner = jnp.logical_not(at_end)
    beside_end = (line == 1) | (line == last - 1)

    def block(n, z, d, sem, there):
        return copy(held(n, z), held(n, z), sem, r3z.at[n, d - 1], there)

    def spread_out(*which):
        for d in [last - 1] + list(range(1, last - 1)):
            for n in which:
                block(n, line, d, out.at[6], on_line(d)[1]).start()
        for n in which:
            pl.when(inner)(block(n, line, last, out.at[10], on_line(last)[1]).start)
            copy(held(n, line), held(n, line), out.at[2 if n >= 2 else 7], r3y.at[n], across).start()

    def take_in(n, d):
        z, there = on_line(d)
        block(n, z, d, out.at[6], there).wait_recv()
        if d == last - 1:
            pl.when(beside_end)(block(n, z, last, out.at[11], on_line(1)[1]).start)
        if n >= 2 and d == last - 1:
            pl.when(beside_end)(copy(held(n, z), held(n, z), out.at[1], r3y.at[n], slanted).start)
        if n >= 2 and d == last:
            pl.when(inner)(copy(held(n, z), held(n, z), out.at[12], r3y.at[n], across).start)
        else:
            copy(held(n, z), held(n, z), out.at[2 if n >= 2 else 7], r3y.at[n], across).start()

    def to_partner(n):
        mine = unit(n, quarter, slice(None))
        copy(mine, mine, out.at[8], r3c.at[n], partner).start()

    def from_across(n):
        arrived(unit(n, 0, slice(None)), r3y.at[n])
        other = 2 * (1 - side) + core
        theirs = unit(n, other, slice(None))
        copy(theirs, theirs, out.at[8], r3c.at[n], partner).start()

    gate = summed(0)
    sig = 1.0 / (1.0 + jnp.exp(-gate))
    to_hidden, slope = gate * sig, sig * (1.0 + gate * (1.0 - sig))
    to_gate = []
    for e in range(2):
        up, span = summed(1, e), band(2, e)
        all3[0, quarter, line, span] = (to_hidden[span] * up).astype(BF16)
        spread_out(e)
        to_gate.append(up * slope[span])
    for e in range(2):
        dhidden, span = summed(2, e), band(2, e)
        all3[1, quarter, line, span] = (dhidden * to_gate[e]).astype(BF16)
        all3[2, quarter, line, span] = (dhidden * to_hidden[span]).astype(BF16)
        spread_out(2 + e)

    def finish(n):
        take_in(n, last)
        to_partner(n)

    def output_rows():
        places = [flip(line, d, lines) for d in range(lines)]
        hidden = jnp.concatenate([all3[0, quarter, z] for z in places], axis=0)
        rows = dot(hidden, wfull[2].reshape(line_depth, width), ((1,), (1,))).astype(BF16)
        rows = rows.reshape(lines, members, cap, line_depth)
        for i, z in enumerate(places):
            for m in range(members):
                send4[z * members + m] = rows[i, m]
            for dj in range(0 if i else 1, members):
                member = flip(j, dj, members)
                there = device(z, side, core, member)
                copy(send4.at[z * members + member], recv4.at[j, line], out.at[9], r4, there).start()
        recv4[j, line] = send4[flat]

    far = last - 1

    @pl.when(at_end)
    def _():
        for n in (0, 1):
            for d in range(1, last):
                take_in(n, d)
        for n in (2, 3):
            for d in range(1, far):
                take_in(n, d)
        finish(0)
        finish(1)
        output_rows()
        for n in (2, 3):
            take_in(n, far)
            finish(n)

    @pl.when(inner)
    def _():
        for n in (0, 1):
            for d in range(1, last):
                take_in(n, d)
        finish(0)
        finish(1)
        for n in (2, 3):
            for d in range(1, last):
                take_in(n, d)
        output_rows()
        finish(2)
        finish(3)

    for n in range(4):
        from_across(n)
    arrived(rows_all.at[:, 0:3], rx)
    for n in range(2):
        half_sum[n] = product_of_rows(rows_all, all3, 1 + n, 0, band(2, 1), (core, 2 + core))
    for n in range(2):
        arrived(unit(n, slice(0, 2), slice(None)), r3c.at[n])
    grad_down[...] = product_of_rows(rows_all, all3, 0, 1, slice(0, members * cap), range(4)).astype(BF16)
    arrived(unit(2, slice(0, 2), slice(None)), r3c.at[2])
    for n in range(2):
        half_sum[n] += product_of_rows(rows_all, all3, 1 + n, 0, band(2, 0), range(4))
    arrived(send4.at[1:], r4)
    for z in range(lines):
        out_rows = recv4[0, z].astype(F32)
        for m in range(1, members):
            out_rows += recv4[m, z].astype(F32)
        placed = dot(spread, (out_rows * slot_weight).astype(BF16), ((1,), (0,)))
        mixed[:, z * line_depth : (z + 1) * line_depth] = placed.astype(BF16)
    arrived(unit(3, slice(0, 2), slice(None)), r3c.at[3])

    departed(wfull.at[:, 0:3], 0)
    departed(recv1.at[:, 1:], 3)
    departed(send2.at[:, 1:], 4)
    departed(rows_all.at[:, 0:3], 5)
    departed(all3.at[:, 0, 1:last], 6)
    pl.when(inner)(functools.partial(departed, all3.at[:, 0, 0], 10))
    pl.when(beside_end)(functools.partial(departed, all3.at[:, 0, 0], 11))
    departed(all3.at[0, 0], 7)
    departed(all3.at[0:2, 0, 1:], 2)
    pl.when(inner)(functools.partial(departed, all3.at[0:2, 0, 0], 12))
    pl.when(beside_end)(functools.partial(departed, all3.at[0:2, 0, 0], 1))
    departed(all3.at[:, 0:2], 8)
    departed(send4.at[1:], 9)


def write_out(mixed, grad_down, half_sum, all3, rows_all, mixed_out, gate_out, up_out, down_out, last_two, sems):
    core = lax.rem(lax.axis_index("dp"), 2)
    height = all3.shape[3]
    copies = [
        pltpu.make_async_copy(src, dst, sems.at[n])
        for n, (src, dst) in enumerate(
            ((mixed, mixed_out), (grad_down, down_out), (last_two.at[0], gate_out), (last_two.at[1], up_out))
        )
    ]
    copies[0].start()
    copies[1].start()
    for n in range(2):
        rest = product_of_rows(rows_all, all3, 1 + n, 0, slice(height // 2, height), (1 - core, 3 - core))
        last_two[n] = (half_sum[n] + rest).astype(BF16)
        copies[2 + n].start()
    for c in copies:
        c.wait()


def per_device(lines, members, tokens, cotangent, expert_ids, route_weights, join_groups, w_gate, w_up, w_down):
    tok_count, model = tokens.shape
    depth, width = w_gate.shape
    cap = tok_count // 8
    total = lines * members
    rows = members * cap
    vmem = pl.BlockSpec(memory_space=pltpu.VMEM)
    hbm = pl.BlockSpec(memory_space=pltpu.HBM)
    dma = pltpu.SemaphoreType.DMA
    grad = jax.ShapeDtypeStruct((depth, width), BF16)
    results = pl.pallas_call(
        functools.partial(kernel, lines, members, cap),
        out_shape=(
            pltpu.VMEM((tok_count, model), BF16),
            pltpu.VMEM((depth, width), BF16),
            pltpu.VMEM((2, depth, width), F32),
            pltpu.VMEM((3, 4, lines, rows, width), BF16),
            pltpu.VMEM((2, 4, total, cap, depth), BF16),
        ),
        in_specs=[hbm] * 8,
        out_specs=(vmem,) * 5,
        scratch_shapes=[
            pltpu.SMEM(join_groups.shape, jnp.int32),
            pltpu.VMEM(expert_ids.shape[::-1], jnp.int32),
            pltpu.VMEM(route_weights.shape[::-1], F32),
            pltpu.VMEM((tok_count, model), BF16),
            pltpu.VMEM((tok_count, model), BF16),
            pltpu.VMEM((3, 4, depth, width), BF16),
            pltpu.VMEM((2, lines, 4, cap, depth), BF16),
            pltpu.VMEM((2, total, 4, cap, depth), BF16),
            pltpu.VMEM((3, lines, rows, width), F32),
            pltpu.VMEM((3, lines, rows, width), BF16),
            pltpu.VMEM((3, lines, rows, width), BF16),
            pltpu.VMEM((total, cap, 4 * depth), BF16),
            pltpu.VMEM((members, lines, cap, 4 * depth), BF16),
            dma((6,)), dma((13,)),
            dma((3,)), dma((3,)),
            dma((2,)), dma(()),
            dma((5,)),
            dma((4, lines - 1)), dma((4,)), dma((4,)),
            dma(()),
        ],
        compiler_params=pltpu.CompilerParams(
            collective_id=0, has_side_effects=True, vmem_limit_bytes=44 * 1024 * 1024
        ),
        name="expert_step",
    )(
        *(
            pltpu.with_memory_space_constraint(x, pltpu.HBM)
            for x in (join_groups, tokens, cotangent, expert_ids.T, route_weights.T, w_gate, w_up, w_down)
        )
    )
    return pl.pallas_call(
        write_out,
        out_shape=(jax.ShapeDtypeStruct((tok_count, model), BF16), grad, grad, grad),
        in_specs=[vmem] * 5,
        out_specs=(hbm,) * 4,
        scratch_shapes=[pltpu.VMEM((2, depth, width), BF16), dma((4,))],
        compiler_params=pltpu.CompilerParams(vmem_limit_bytes=16 * 1024 * 1024),
        name="write_out",
    )(*(pltpu.with_memory_space_constraint(r, pltpu.VMEM) for r in results))


def solution(mesh):
    in_specs = (
        P(("dp", "expert"), None),
        P(("dp", "expert"), None),
        P(("dp", "expert"), None),
        P(("dp", "expert"), None),
        P(),
        P("dp", "expert"),
        P("dp", "expert"),
        P("dp", "expert"),
    )
    out_specs = (P(("dp", "expert"), None), P("dp", "expert"), P("dp", "expert"), P("dp", "expert"))
    body = functools.partial(per_device, mesh.shape["dp"] // 4, mesh.shape["expert"])
    return jax.shard_map(body, mesh=mesh, in_specs=in_specs, out_specs=out_specs, check_vma=False)
```
